32 devices in a mesh: seg: 8 (over z, core), patch: 4 (over y, x).
Axes of the slice: x: 2, y: 2, z: 4, core: 2. Of those that a mesh axis runs over, the one named last changes fastest.
Arguments:
- incident: bfloat16 [8, 64, 4096], P('seg', None, 'patch'), may hold values from -6 to 6
- wall_axial: float32 [8, 4096], P('seg'), may hold values from 0 to 1
- wall_angle: float32 [8, 4096], P('seg'), may hold values from -3.140625 to 3.140625
- wall_area: float32 [8, 4096], P('seg'), may hold values from 0.5 to 2
- visibility: int32 [8, 2, 32, 32], P('seg', None, 'patch'), may hold values 0 or 1
- end_reflection: float32 [2, 32], replicated, may hold values from -0.9 to 0.9
Outputs:
- currents: bfloat16 [8, 64, 4096], P('seg', None, 'patch')
The draws below stay inside these ranges and needn't reach their ends.
Inputs may be any that keep to these rules, and one draw needn't show every extreme that they name: `visibility`: 1 where the source block is lit for the target block, 0 where it is in shadow.
All inputs are finite; a program needn't handle non-finite values.
Results may differ from the reference program's by a relative error of at most 0.0034.
Values may be sent and summed in bfloat16 or wider, within the bound.
No kernel may reach another device: no remote copies, remote signals or barrier semaphores. Data moves between devices by JAX's collectives and lax.ppermute only.
A program may use at most 64 MiB of HBM per device.

```python
import math
import jax
import jax.numpy as jnp
from jax import lax

PATCHES = 4096
ANGLES = 16
BLK = 128
ITERS = 2
NSEG = 8


def place_ends(values, key, low, top_value):
    spot = [jax.random.randint(jax.random.fold_in(key, axis), (), 0, length) for axis, length in enumerate(values.shape)]
    main_axis = values.shape.index(max(values.shape))
    neighbour = spot[:main_axis] + [(spot[main_axis] + 1) % values.shape[main_axis]] + spot[main_axis + 1:]
    return values.at[tuple(spot)].set(low).at[tuple(neighbour)].set(top_value)


def steps_of(rng, shape, cuts, low, largest):
    level, own = 1.0, jax.random.fold_in(rng, 6)
    for dim, parts in cuts:
        heights = jnp.exp(jax.random.uniform(jax.random.fold_in(own, dim), (parts,), jnp.float32, low / len(cuts), largest / len(cuts)))
        level = level * jnp.repeat(heights, shape[dim] // parts).reshape([-1 if axis == dim else 1 for axis in range(len(shape))])
    return level


def scatter_about(key, extent, scale, bound, pieces=(), kind=jnp.bfloat16):
    factor_of = steps_of(key, extent, pieces, -0.22, 0.18) if pieces else 1.0
    drawn = jax.random.normal(key, extent, jnp.float32) * scale * factor_of
    return jnp.minimum(jnp.maximum(drawn, -bound), bound).astype(kind)


def setup_inputs(seed: int = 0) -> dict:
    streams_of = jax.random.split(jax.random.key(seed), 7)
    return {
        "incident": scatter_about(streams_of[0], (NSEG, 4 * ANGLES, PATCHES), 1.0, 6.0, ((0, 8), (2, 4))),
        "wall_axial": jnp.clip(1.0 * jax.random.uniform(streams_of[1], (NSEG, PATCHES), jnp.float32) ** steps_of(streams_of[1], (NSEG, PATCHES), ((0, 8),), -0.2, 0.2), 0.0, 1.0),
        "wall_angle": jnp.clip(jax.random.uniform(streams_of[2], (NSEG, PATCHES), jnp.float32, -3.140625, 3.140625), -3.140625, 3.140625),
        "wall_area": jnp.clip(jnp.exp(math.log(2.0) - 1.3862944 * jax.random.uniform(streams_of[3], (NSEG, PATCHES), jnp.float32) ** steps_of(streams_of[3], (NSEG, PATCHES), ((0, 8),), -0.2, 0.2)), 0.5, 2.0),
        "visibility": place_ends((jax.random.randint(streams_of[4], (NSEG, 2, PATCHES // BLK, PATCHES // BLK), 0, 4) < 3).astype(jnp.int32), jax.random.fold_in(streams_of[4], 1), 0, 1),
        "end_reflection": jnp.clip(jax.random.uniform(streams_of[5], (2, 2 * ANGLES), jnp.float32, -0.9, 0.9), -0.9, 0.9),
    }


WAVENUMBER = 40.0
RADIUS = 0.5
SOFTENING = 0.25

def kernel_piece(target, source, offset, visible, patches):
    axial_gap = offset + target[0][:, None] - source[0][None, :]
    chord = 2.0 * RADIUS * RADIUS * (1.0 - jnp.cos(target[1][:, None] - source[1][None, :]))
    squared = axial_gap * axial_gap + chord
    magnitude = source[2][None, :] * visible.astype(jnp.float32) / jnp.sqrt(patches * (squared + SOFTENING))
    phases = WAVENUMBER * jnp.sqrt(squared)
    kernel_re = (magnitude * jnp.cos(phases)).astype(jnp.bfloat16)
    kernel_im = (-magnitude * jnp.sin(phases)).astype(jnp.bfloat16)
    return (kernel_re, kernel_im)

def couple(sources, kernel_re, kernel_im, angles):
    contract = (((1,), (1,)), ((), ()))
    prod_re = lax.dot_general(sources, kernel_re, contract, preferred_element_type=jnp.float32)
    prod_im = lax.dot_general(sources, kernel_im, contract, preferred_element_type=jnp.float32)
    return jnp.concatenate([prod_re[:angles] - prod_im[angles:], prod_re[angles:] + prod_im[:angles]], 0)

def reflect(coef, values, angles):
    coef_re = coef[:angles][:, None]
    coef_im = coef[angles:][:, None]
    real_part = values[:angles]
    imag_part = values[angles:]
    return jnp.concatenate([coef_re * real_part - coef_im * imag_part, coef_re * imag_part + coef_im * real_part], 0)

def reference(incident, wall_axial, wall_angle, wall_area, visibility, end_reflection):
    seg_count, channel_count, patches = incident.shape
    angles = channel_count // 4
    block_rows = min(1024, patches)
    block_count = patches // block_rows
    block_size = patches // visibility.shape[3]
    geometry = jnp.stack([wall_axial, wall_angle, wall_area], 1)
    empty_geometry = jnp.zeros((1, 3, patches), jnp.float32)
    prev_geo = jnp.concatenate([empty_geometry, geometry[:-1]], 0)
    next_geo = jnp.concatenate([geometry[1:], empty_geometry], 0)
    empty_currents = jnp.zeros((1, 2 * angles, patches), jnp.bfloat16)
    state = incident
    for sweep in range(ITERS):
        prev_cur = jnp.concatenate([empty_currents, state[:-1, :2 * angles]], 0)
        next_cur = jnp.concatenate([state[1:, 2 * angles:], empty_currents], 0)

        def one_segment(members):
            target_geo, before_geo, after_geo, before_cur, after_cur, visible = members

            def one_block(block_index):
                target = lax.dynamic_slice_in_dim(target_geo, block_index * block_rows, block_rows, 1)
                lit = lax.dynamic_slice_in_dim(visible, block_index * (block_rows // block_size), block_rows // block_size, 1)
                lit = jnp.repeat(jnp.repeat(lit, block_size, axis=1), block_size, axis=2)
                kernel_re, kernel_im = kernel_piece(target, before_geo, 1.0, lit[0], patches)
                forward = couple(before_cur, kernel_re, kernel_im, angles)
                kernel_re, kernel_im = kernel_piece(target, after_geo, -1.0, lit[1], patches)
                backward = couple(after_cur, kernel_re, kernel_im, angles)
                return jnp.concatenate([forward, backward], 0)
            result = lax.map(one_block, jnp.arange(block_count, dtype=jnp.int32))
            return jnp.transpose(result, (1, 0, 2)).reshape(channel_count, patches)
        coupled = lax.map(one_segment, (geometry, prev_geo, next_geo, prev_cur, next_cur, visibility))
        previous = state.astype(jnp.float32)
        first_end = reflect(end_reflection[0], previous[0, 2 * angles:], angles)
        last_end = reflect(end_reflection[1], previous[-1, :2 * angles], angles)
        mirrored = jnp.zeros((seg_count, channel_count, patches), jnp.float32)
        mirrored = mirrored.at[0, :2 * angles].set(first_end).at[seg_count - 1, 2 * angles:].set(last_end)
        state = (incident.astype(jnp.float32) + coupled + mirrored).astype(jnp.bfloat16)
    return state
```

```python
import functools
import math

import jax
import jax.numpy as jnp
from jax import lax
from jax.experimental import pallas as pl
from jax.experimental.pallas import tpu as pltpu
from jax.sharding import PartitionSpec as P

ITERS = 2

WAVENUMBER = 40.0
RADIUS = 0.5
SOFTENING = 0.25

KAPPA = WAVENUMBER / (2.0 * math.pi)
HALF_CHORD = 2.0 * RADIUS * RADIUS * KAPPA * KAPPA
SINE = (4.442867903112522, -7.307443423342558, 3.5947880930735288, -0.7843740618048793)
COSINE = (1.4142040804693898, -6.9776420568649025, 5.7152383957142225, -1.728348664791446)

FEATURES = 32
UNROLL = 4
BF = jnp.bfloat16
F32 = jnp.float32


def leading(x):
    wide = x * 65537.0
    return wide - (wide - x)


def split3(x):
    high = leading(x)
    rest = x - high
    mid = leading(rest)
    return high, mid, rest - mid


def near_side(geo, direction):
    return (geo[0:1] if direction == 0 else 1.0 - geo[0:1]) * KAPPA


def far_side(geo, direction):
    return (1.0 - geo[0:1] if direction == 0 else geo[0:1]) * KAPPA


def pad_rows(rows):
    width = rows[0].shape[1]
    rows = rows + [jnp.zeros((FEATURES - len(rows), width), F32)]
    return jnp.concatenate(rows, 0)


def target_features(geo, direction):
    u = near_side(geo, direction)
    one = jnp.ones_like(u)
    rows = list(split3(u * u + HALF_CHORD)) + [one, one, one]
    for value in (2.0 * u, -HALF_CHORD * geo[1:2], -HALF_CHORD * geo[2:3]):
        h, m, l = split3(value)
        rows += [h, h, m, m, h, l]
    return pad_rows(rows)


def source_features(geo, direction):
    v = far_side(geo, direction)
    one = jnp.ones_like(v)
    rows = [one, one, one] + list(split3(v * v))
    for value in (v, geo[1:2], geo[2:3]):
        h, m, l = split3(value)
        rows += [h, m, h, m, l, h]
    return pad_rows(rows)


def plan_kernel(per_chunk, vis_ref, list_ref, count_ref):
    targets, sources = vis_ref.shape[2], vis_ref.shape[3]
    chunks = sources // per_chunk
    size = per_chunk * targets
    for direction in range(2):
        for chunk in range(chunks):
            row = direction * chunks + chunk

            def step(n, lit, direction=direction, chunk=chunk, row=row):
                src = n // targets
                tgt = n % targets
                flag = vis_ref[0, direction, tgt, chunk * per_chunk + src]
                place = jnp.where(flag > 0, lit, size - 1 - (n - lit))
                list_ref[row, place] = n
                return lit + flag

            count_ref[row] = lax.fori_loop(0, size, step, jnp.int32(0))


def make_plan(visibility, per_chunk):
    targets, sources = visibility.shape[2], visibility.shape[3]
    chunks = sources // per_chunk
    return pl.pallas_call(
        functools.partial(plan_kernel, per_chunk),
        out_shape=(
            jax.ShapeDtypeStruct((2 * chunks, per_chunk * targets), jnp.int32),
            jax.ShapeDtypeStruct((2 * chunks,), jnp.int32),
        ),
        in_specs=[pl.BlockSpec(memory_space=pltpu.SMEM)],
        out_specs=[pl.BlockSpec(memory_space=pltpu.SMEM)] * 2,
        name="plan",
    )(visibility)


def table_block(q):
    q = jnp.maximum(q, 1e-12)
    turns = q * lax.rsqrt(q)
    f = turns - jnp.round(turns)
    mag = lax.rsqrt(q + SOFTENING * KAPPA * KAPPA)
    z = f * f
    s = (((SINE[3] * z + SINE[2]) * z + SINE[1]) * z + SINE[0]) * f
    c = ((COSINE[3] * z + COSINE[2]) * z + COSINE[1]) * z + COSINE[0]
    real = mag - (s * s) * mag
    imag = (mag * s) * c
    return real.astype(BF), imag.astype(BF)


def build_chunk(direction, row, block, targets, list_ref, count_ref, tf_ref, sf_ref, base, k_ref):
    count = count_ref[row]
    size = list_ref.shape[1]

    def body(step, carry):
        for u in range(UNROLL):
            code = list_ref[row, jnp.minimum(step * UNROLL + u, count - 1)]
            src, tgt = code // targets, code % targets
            cols = pl.ds(pl.multiple_of(tgt * block, block), block)
            feats = sf_ref[pl.ds(pl.multiple_of(base + src * block, block), block), :]
            q = jnp.dot(feats, tf_ref[:, cols], preferred_element_type=F32)
            top = pl.multiple_of(src * (2 * block), 2 * block)
            part = 32
            for h in range(0, block, part):
                real, imag = table_block(q[h : h + part])
                k_ref[pl.ds(pl.multiple_of(top + h, part), part), cols] = real
                k_ref[pl.ds(pl.multiple_of(top + block + h, part), part), cols] = imag
        return carry

    lax.fori_loop(0, (count + UNROLL - 1) // UNROLL, body, 0)

    def clear(n, carry):
        code = list_ref[row, n]
        src, tgt = code // targets, code % targets
        cols = pl.ds(pl.multiple_of(tgt * block, block), block)
        rows = pl.ds(pl.multiple_of(src * (2 * block), 2 * block), 2 * block)
        k_ref[rows, cols] = jnp.zeros((2 * block, block), BF)
        return carry

    lax.fori_loop(count, size, clear, 0)


def build_features(direction, block, tgeo_ref, sgeo_ref, tf_ref, sf_ref):
    tf_ref[...] = target_features(tgeo_ref[...], direction).astype(BF)
    feats = source_features(sgeo_ref[...], direction)
    sf_ref[...] = feats.T.astype(BF)


def build_kernel(direction, block, per_chunk, list_ref, count_ref, tgeo_ref, sgeo_ref, k_ref, tf_ref, sf_ref):
    chunk = pl.program_id(0)
    chunks = pl.num_programs(0)
    targets = tgeo_ref.shape[1] // block

    @pl.when(chunk == 0)
    def _():
        build_features(direction, block, tgeo_ref, sgeo_ref, tf_ref, sf_ref)

    build_chunk(
        direction, direction * chunks + chunk, block, targets, list_ref, count_ref, tf_ref, sf_ref,
        chunk * (per_chunk * block), k_ref,
    )


def call_build(direction, block, per_chunk, plan, tgeo, sgeo):
    patches, rows = sgeo.shape[1], tgeo.shape[1]
    chunks = patches // (block * per_chunk)
    chunk_rows = 2 * block * per_chunk
    whole = lambda shape: pl.BlockSpec(shape, lambda c: (0, 0))
    return pl.pallas_call(
        functools.partial(build_kernel, direction, block, per_chunk),
        grid=(chunks,),
        out_shape=jax.ShapeDtypeStruct((2 * patches, rows), BF),
        in_specs=[
            pl.BlockSpec(memory_space=pltpu.SMEM),
            pl.BlockSpec(memory_space=pltpu.SMEM),
            whole(tgeo.shape),
            whole(sgeo.shape),
        ],
        out_specs=pl.BlockSpec((chunk_rows, rows), lambda c: (c, 0)),
        scratch_shapes=[pltpu.VMEM((FEATURES, rows), BF), pltpu.VMEM((patches, FEATURES), BF)],
        compiler_params=pltpu.CompilerParams(dimension_semantics=("arbitrary",)),
        name=f"build{direction}",
    )(*plan, tgeo, sgeo)


def load_sources(where_ref, piece_refs, before_ref, after_ref, left_ref, scale, block):
    channels = piece_refs[0].shape[0] // 2
    half = channels // 2
    width = piece_refs[0].shape[1]
    for k, piece in enumerate(piece_refs):
        start = where_ref[k] * width
        for d, geo_ref in enumerate((before_ref, after_ref)):
            for n in range(width // block):
                cur = piece[d * channels : (d + 1) * channels, n * block : (n + 1) * block].astype(F32)
                lanes = pl.ds(pl.multiple_of(start + n * block, block), block)
                cur = cur * (geo_ref[3:4, lanes] * scale)
                high = leading(cur)
                low = (cur - high).astype(BF)
                high = high.astype(BF)
                a = jnp.concatenate([high, low], 0)
                b = jnp.concatenate([high[half:], -high[:half], low[half:], -low[:half]], 0)
                top = pl.multiple_of(2 * (start + n * block), 2 * block)
                left_ref[d, :, pl.ds(top, block)] = a
                left_ref[d, :, pl.ds(pl.multiple_of(top + block, block), block)] = b


def finish(acc_ref, inc_ref, prev_ref, coef_ref, out_ref):
    channels = inc_ref.shape[0] // 2
    half = channels // 2
    prev = prev_ref[...].astype(F32)
    for d in range(2):
        total = acc_ref[d, :channels] + acc_ref[d, channels:]
        other = prev[(1 - d) * channels : (2 - d) * channels]
        cre = coef_ref[d, :half]
        cim = coef_ref[d, half:]
        mirrored = jnp.concatenate(
            [cre * other[:half] - cim * other[half:], cre * other[half:] + cim * other[:half]], 0
        )
        rows = slice(d * channels, (d + 1) * channels)
        out_ref[rows] = (inc_ref[rows].astype(F32) + total + mirrored).astype(BF)


def accumulate(acc_ref, left_ref, d, chunk, k_ref):
    rows = k_ref.shape[0]
    cols = pl.ds(pl.multiple_of(chunk * rows, rows), rows)
    part = jnp.dot(left_ref[d, :, cols], k_ref[...], preferred_element_type=F32)

    @pl.when(chunk == 0)
    def _():
        acc_ref[d] = part

    @pl.when(chunk > 0)
    def _():
        acc_ref[d] += part


def build_sweep_kernel(
    block, per_chunk, pieces, scale,
    list_ref, count_ref, where_ref, tgeo_ref, before_ref, after_ref, inc_ref, coef_ref, k0_ref, *rest
):
    piece_refs = rest[:pieces]
    k_ref, out_ref, tf_ref, sf_ref, left_ref, acc_ref = rest[pieces:]
    chunk = pl.program_id(0)
    chunks = pl.num_programs(0)
    targets = tgeo_ref.shape[1] // block

    @pl.when(chunk == 0)
    def _():
        build_features(1, block, tgeo_ref, after_ref, tf_ref, sf_ref)
        load_sources(where_ref, piece_refs, before_ref, after_ref, left_ref, scale, block)

    build_chunk(
        1, chunks + chunk, block, targets, list_ref, count_ref, tf_ref, sf_ref,
        chunk * (per_chunk * block), k_ref,
    )
    accumulate(acc_ref, left_ref, 0, chunk, k0_ref)
    accumulate(acc_ref, left_ref, 1, chunk, k_ref)

    @pl.when(chunk == chunks - 1)
    def _():
        finish(acc_ref, inc_ref, inc_ref, coef_ref, out_ref)


def call_build_sweep(block, per_chunk, scale, plan, where, tgeo, before, after, inc, coef, k0, pieces):
    patches, rows = before.shape[1], tgeo.shape[1]
    chunks = patches // (block * per_chunk)
    chunk_rows = 2 * block * per_chunk
    whole = lambda x: pl.BlockSpec(x.shape, lambda c: (0,) * x.ndim)
    smem = pl.BlockSpec(memory_space=pltpu.SMEM)
    channels = inc.shape[0]
    return pl.pallas_call(
        functools.partial(build_sweep_kernel, block, per_chunk, len(pieces), scale),
        grid=(chunks,),
        out_shape=(
            jax.ShapeDtypeStruct((2 * patches, rows), BF),
            jax.ShapeDtypeStruct((channels, rows), BF),
        ),
        in_specs=[smem, smem, smem, whole(tgeo), whole(before), whole(after), whole(inc), whole(coef),
                  pl.BlockSpec((chunk_rows, rows), lambda c: (c, 0))] + [whole(p) for p in pieces],
        out_specs=(
            pl.BlockSpec((chunk_rows, rows), lambda c: (c, 0)),
            pl.BlockSpec((channels, rows), lambda c: (0, 0)),
        ),
        scratch_shapes=[
            pltpu.VMEM((FEATURES, rows), BF),
            pltpu.VMEM((patches, FEATURES), BF),
            pltpu.VMEM((2, channels, 2 * patches), BF),
            pltpu.VMEM((2, channels, rows), F32),
        ],
        compiler_params=pltpu.CompilerParams(dimension_semantics=("arbitrary",)),
        name="build_sweep",
    )(*plan, where, tgeo, before, after, inc, coef, k0, *pieces)


def sweep_kernel(
    block, pieces, scale, where_ref, before_ref, after_ref, inc_ref, prev_ref, coef_ref, k0_ref, k1_ref, *rest
):
    piece_refs = rest[:pieces]
    out_ref, left_ref, acc_ref = rest[pieces:]
    chunk = pl.program_id(0)

    @pl.when(chunk == 0)
    def _():
        load_sources(where_ref, piece_refs, before_ref, after_ref, left_ref, scale, block)

    accumulate(acc_ref, left_ref, 0, chunk, k0_ref)
    accumulate(acc_ref, left_ref, 1, chunk, k1_ref)

    @pl.when(chunk == pl.num_programs(0) - 1)
    def _():
        finish(acc_ref, inc_ref, prev_ref, coef_ref, out_ref)


def call_sweep(block, per_chunk, scale, where, before, after, inc, prev, coef, k0, k1, pieces):
    patches, rows = before.shape[1], inc.shape[1]
    chunks = patches // (block * per_chunk)
    chunk_rows = 2 * block * per_chunk
    whole = lambda x: pl.BlockSpec(x.shape, lambda c: (0,) * x.ndim)
    smem = pl.BlockSpec(memory_space=pltpu.SMEM)
    channels = inc.shape[0]
    table = pl.BlockSpec((chunk_rows, rows), lambda c: (c, 0))
    return pl.pallas_call(
        functools.partial(sweep_kernel, block, len(pieces), scale),
        grid=(chunks,),
        out_shape=jax.ShapeDtypeStruct((channels, rows), BF),
        in_specs=[smem, whole(before), whole(after), whole(inc), whole(prev), whole(coef), table, table]
        + [whole(p) for p in pieces],
        out_specs=pl.BlockSpec((channels, rows), lambda c: (0, 0)),
        scratch_shapes=[
            pltpu.VMEM((2, channels, 2 * patches), BF),
            pltpu.VMEM((2, channels, rows), F32),
        ],
        compiler_params=pltpu.CompilerParams(dimension_semantics=("arbitrary",)),
        name="sweep",
    )(where, before, after, inc, prev, coef, k0, k1, *pieces)


def shift(value, step):
    count = lax.axis_size("seg")
    return lax.ppermute(value, "seg", [(i, i + step) for i in range(count) if 0 <= i + step < count])


def gather_patches(value):
    count = lax.axis_size("patch")
    me = lax.axis_index("patch")
    pieces, where = [value], [me]
    if count <= 4:
        for k in range(1, count):
            pieces.append(lax.ppermute(value, "patch", [(i, i ^ k) for i in range(count)]))
            where.append(me ^ k)
        return pieces, jnp.stack(where).astype(jnp.int32)
    return [lax.all_gather(value, "patch", axis=1, tiled=True)], jnp.zeros((1,), jnp.int32)


def on_device(incident, wall_axial, wall_angle, wall_area, visibility, end_reflection):
    channels = incident.shape[1]
    rows = incident.shape[2]
    patches = wall_axial.shape[1]
    block = patches // visibility.shape[3]
    half = channels // 2
    per_chunk = min(8, patches // block)
    seg_index = lax.axis_index("seg")
    seg_count = lax.axis_size("seg")
    patch_index = lax.axis_index("patch")
    scale = KAPPA / math.sqrt(patches)
    inc = incident[0]
    angle = wall_angle[0]
    geo = jnp.stack([wall_axial[0], jnp.cos(angle), jnp.sin(angle), wall_area[0]])
    before, after = shift(geo, 1), shift(geo, -1)
    tgeo = lax.dynamic_slice_in_dim(geo, patch_index * rows, rows, 1)
    ends = jnp.stack([seg_index == 0, seg_index == seg_count - 1])
    coef = jnp.where(ends[:, None], end_reflection, 0.0)[:, :, None]
    plan = make_plan(visibility, per_chunk)

    def exchange(state):
        moved = jnp.concatenate([shift(state[:half], 1), shift(state[half:], -1)], 0)
        return gather_patches(moved)

    k0 = call_build(0, block, per_chunk, plan, tgeo, before)
    pieces, where = exchange(inc)
    k1, state = call_build_sweep(
        block, per_chunk, scale, plan, where, tgeo, before, after, inc, coef, k0, pieces
    )
    for sweep in range(1, ITERS):
        pieces, where = exchange(state)
        state = call_sweep(block, per_chunk, scale, where, before, after, inc, state, coef, k0, k1, pieces)
    return state[None]


def solution(mesh):
    return jax.shard_map(
        on_device,
        mesh=mesh,
        in_specs=(
            P("seg", None, "patch"),
            P("seg", None),
            P("seg", None),
            P("seg", None),
            P("seg", None, "patch", None),
            P(),
        ),
        out_specs=P("seg", None, "patch"),
        check_vma=False,
    )
```

```python
import functools
import math

import jax
import jax.numpy as jnp
from jax import lax
from jax.experimental import pallas as pl
from jax.experimental.pallas import tpu as pltpu
from jax.sharding import PartitionSpec as P

ITERS = 2

WAVENUMBER = 40.0
RADIUS = 0.5
SOFTENING = 0.25

KAPPA = WAVENUMBER / (2.0 * math.pi)
HALF_CHORD = 2.0 * RADIUS * RADIUS * KAPPA * KAPPA
SINE = tuple(
    value * (1.0 - 5e-7)
    for value in (4.442867903112522, -7.307443423342558, 3.5947880930735288, -0.7843740618048793)
)
SINE_HALF = (0.999999976589841, -0.16666647634617332, 0.00833289982302485, -0.00019800897745117133,
             2.5904884686762915e-06)
COSINE_HALF = (0.9999999997806504, -0.4999999935847076, 0.04166663625803946, -0.0013888361399933481,
               2.476016133696864e-05, -2.605149496508554e-07)

FEATURES = 32
PAIR = 8
BF = jnp.bfloat16
F32 = jnp.float32


def leading(x):
    wide = x * 65537.0
    return wide - (wide - x)


def split3(x):
    high = leading(x)
    rest = x - high
    mid = leading(rest)
    return high, mid, rest - mid


def near_side(geo, direction):
    return (geo[0:1] if direction == 0 else 1.0 - geo[0:1]) * KAPPA


def far_side(geo, direction):
    return (1.0 - geo[0:1] if direction == 0 else geo[0:1]) * KAPPA


def pad_rows(rows):
    width = rows[0].shape[1]
    rows = rows + [jnp.zeros((FEATURES - len(rows), width), F32)]
    return jnp.concatenate(rows, 0)


def target_features(geo, direction):
    u = near_side(geo, direction)
    one = jnp.ones_like(u)
    rows = list(split3(u * u + HALF_CHORD)) + [one, one, one]
    for value in (2.0 * u, -HALF_CHORD * geo[1:2], -HALF_CHORD * geo[2:3]):
        h, m, l = split3(value)
        rows += [h, h, m, m, h, l]
    return pad_rows(rows)


def source_features(geo, direction):
    v = far_side(geo, direction)
    one = jnp.ones_like(v)
    rows = [one, one, one] + list(split3(v * v))
    for value in (v, geo[1:2], geo[2:3]):
        h, m, l = split3(value)
        rows += [h, m, h, m, l, h]
    return pad_rows(rows)


def horner(coefs, x):
    total = coefs[-1]
    for coef in coefs[-2::-1]:
        total = total * x + coef
    return total


def exact_dot(a, b):
    return jnp.dot(a.astype(BF), b.astype(BF), preferred_element_type=F32)


def make_lists(lit, per_chunk):
    targets, sources = lit.shape
    chunks = sources // per_chunk
    size = per_chunk * targets
    i0 = lax.broadcasted_iota(jnp.int32, (sources, sources), 0)
    i1 = lax.broadcasted_iota(jnp.int32, (sources, sources), 1)
    same = i0 // per_chunk == i1 // per_chunk
    above = lax.broadcasted_iota(jnp.int32, (targets, targets), 0) > lax.broadcasted_iota(
        jnp.int32, (targets, targets), 1
    )
    sums = exact_dot(lit, jnp.where(same, 1.0, 0.0))
    rank = exact_dot(lit, jnp.where(same & (i0 < i1), 1.0, 0.0)) + exact_dot(
        jnp.where(above, 1.0, 0.0), sums
    )
    src = lax.broadcasted_iota(jnp.int32, lit.shape, 1) % per_chunk
    tgt = lax.broadcasted_iota(jnp.int32, lit.shape, 0)
    order = (tgt * per_chunk + src).astype(F32)
    place = jnp.where(lit > 0.5, rank, size - 1 - (order - rank))
    code = (src * targets + tgt).astype(F32)
    slot = lax.broadcasted_iota(jnp.int32, (size, sources), 0).astype(F32)
    found = jnp.zeros((size, sources), F32)
    for t in range(targets):
        found += jnp.where(slot == place[t : t + 1], code[t : t + 1], 0.0)
    c0 = lax.broadcasted_iota(jnp.int32, (sources, chunks), 0)
    c1 = lax.broadcasted_iota(jnp.int32, (sources, chunks), 1)
    pick = jnp.where(c0 // per_chunk == c1, 1.0, 0.0)
    codes = exact_dot(found, pick)
    counts = jnp.sum(exact_dot(lit, pick), axis=0, keepdims=True)
    return codes.astype(jnp.int32), counts.astype(jnp.int32)


def prep_kernel(per_chunk, axial_ref, angle_ref, area_ref, inc_ref, vis_ref, up_ref, down_ref, list_ref):
    rows = inc_ref.shape[1]
    channels = inc_ref.shape[0] // 2
    half = angle_ref[...] * 0.5
    square = half * half
    sine = horner(SINE_HALF, square) * half
    cosine = horner(COSINE_HALF, square)
    geo = [axial_ref[...], 1.0 - 2.0 * sine * sine, 2.0 * sine * cosine, area_ref[...]]
    for j in range(axial_ref.shape[1] // rows):
        part = jnp.concatenate([g[:, j * rows : (j + 1) * rows] for g in geo], 0)
        up_ref[channels + 4 * j : channels + 4 * j + 4] = part
        down_ref[channels + 4 * j : channels + 4 * j + 4] = part
    up_ref[:channels] = inc_ref[:channels].astype(F32)
    down_ref[:channels] = inc_ref[channels:].astype(F32)
    for d in range(2):
        codes, counts = make_lists(vis_ref[0, d].astype(F32), per_chunk)
        list_ref[d, : codes.shape[0]] = codes
        list_ref[d, codes.shape[0] :] = jnp.broadcast_to(counts, (8, counts.shape[1]))


def call_prep(per_chunk, axial, angle, area, inc, visibility):
    targets, sources = visibility.shape[2], visibility.shape[3]
    channels = inc.shape[0] // 2
    rows, patches = inc.shape[1], axial.shape[1]
    pack = jax.ShapeDtypeStruct((channels + 4 * (patches // rows), rows), F32)
    vmem = pl.BlockSpec(memory_space=pltpu.VMEM)
    return pl.pallas_call(
        functools.partial(prep_kernel, per_chunk),
        out_shape=(
            pack, pack,
            jax.ShapeDtypeStruct((2, per_chunk * targets + 8, sources // per_chunk), jnp.int32),
        ),
        in_specs=[vmem] * 5,
        out_specs=[vmem] * 3,
        name="prep",
    )(axial, angle, area, inc, visibility)


def table_block(q):
    q = jnp.maximum(q, 1e-12)
    turns = q * lax.rsqrt(q)
    f = turns - jnp.round(turns)
    mag = lax.rsqrt(q + SOFTENING * KAPPA * KAPPA)
    s = horner(SINE, f * f) * f
    rest = 2.0 - s * s
    both = mag * rest
    real = both - mag
    imag = (s * both) * lax.rsqrt(rest)
    return real.astype(BF), imag.astype(BF)


def build_chunk(direction, chunk, block, targets, list_ref, tf_ref, sf_ref, base, k_ref, even_ref, odd_ref):
    size = list_ref.shape[1] - 8
    count = list_ref[direction, size, chunk]

    def block_of(n):
        code = list_ref[direction, jnp.maximum(jnp.minimum(n, count - 1), 0), chunk]
        return lax.div(code, jnp.int32(targets)), lax.rem(code, jnp.int32(targets))

    def distances(group, q_ref):
        for u in range(PAIR):
            src, tgt = block_of(group * PAIR + u)
            cols = pl.ds(pl.multiple_of(tgt * block, block), block)
            feats = sf_ref[pl.ds(pl.multiple_of(base + src * block, block), block), :]
            q_ref[u * block : (u + 1) * block] = jnp.dot(feats, tf_ref[:, cols], preferred_element_type=F32)

    def entries(group, q_ref):
        for u in range(PAIR):
            src, tgt = block_of(group * PAIR + u)
            top = pl.multiple_of(src * (2 * block), 2 * block)
            part = 32
            for h in range(0, block, part):
                real, imag = table_block(q_ref[u * block + h : u * block + h + part])
                k_ref[tgt, pl.ds(pl.multiple_of(top + h, part), part), :] = real
                k_ref[tgt, pl.ds(pl.multiple_of(top + block + h, part), part), :] = imag

    def body(step, carry):
        distances(step, even_ref)
        entries(step, even_ref)
        return carry

    lax.fori_loop(0, lax.div(count + PAIR - 1, jnp.int32(PAIR)), body, 0)

    def clear(n, carry):
        code = list_ref[direction, n, chunk]
        src, tgt = lax.div(code, jnp.int32(targets)), lax.rem(code, jnp.int32(targets))
        rows = pl.ds(pl.multiple_of(src * (2 * block), 2 * block), 2 * block)
        k_ref[tgt, rows, :] = jnp.zeros((2 * block, block), BF)
        return carry

    lax.fori_loop(count, size, clear, 0)


def quarters(pack_ref, channels):
    return [pack_ref[r : r + 4] for r in range(channels, pack_ref.shape[0], 4)]


def pick(parts, index):
    chosen = parts[0]
    for j in range(1, len(parts)):
        chosen = jnp.where(index == j, parts[j], chosen)
    return chosen


def build_features(direction, channels, own_ref, pack_ref, tf_ref, sf_ref):
    rows = own_ref.shape[1]
    own = pick(quarters(own_ref, channels), lax.axis_index("patch"))
    tf_ref[...] = target_features(own, direction).astype(BF)
    for j, geo in enumerate(quarters(pack_ref, channels)):
        sf_ref[j * rows : (j + 1) * rows] = source_features(geo, direction).T.astype(BF)


def build_kernel(direction, block, per_chunk, channels, list_ref, own_ref, pack_ref, k_ref, tf_ref, sf_ref, *q):
    chunk = pl.program_id(0)

    @pl.when(chunk == 0)
    def _():
        build_features(direction, channels, own_ref, pack_ref, tf_ref, sf_ref)

    build_chunk(
        direction, chunk, block, k_ref.shape[0], list_ref, tf_ref, sf_ref, chunk * (per_chunk * block), k_ref, *q
    )


def whole(x):
    return pl.BlockSpec(x.shape, lambda c: (0,) * x.ndim)


def table_spec(targets, chunk_rows, block):
    return pl.BlockSpec((targets, chunk_rows, block), lambda c: (0, c, 0))


def call_build(direction, block, per_chunk, channels, lists, own, pack, patches):
    rows = own.shape[1]
    targets = rows // block
    chunk_rows = 2 * block * per_chunk
    return pl.pallas_call(
        functools.partial(build_kernel, direction, block, per_chunk, channels),
        grid=(patches // (block * per_chunk),),
        out_shape=jax.ShapeDtypeStruct((targets, 2 * patches, block), BF),
        in_specs=[pl.BlockSpec(memory_space=pltpu.SMEM), whole(own), whole(pack)],
        out_specs=table_spec(targets, chunk_rows, block),
        scratch_shapes=[
            pltpu.VMEM((FEATURES, rows), BF),
            pltpu.VMEM((patches, FEATURES), BF),
            pltpu.VMEM((PAIR * block, block), F32),
            pltpu.VMEM((PAIR * block, block), F32),
        ],
        compiler_params=pltpu.CompilerParams(dimension_semantics=("arbitrary",)),
        name=f"build{direction}",
    )(lists, own, pack)


def load_piece(k, piece_ref, packs, left_ref, scale, block):
    channels = piece_ref.shape[0] // 2
    half = channels // 2
    width = piece_ref.shape[1]
    gathered = width != packs[0].shape[1]
    group = lax.axis_index("patch") ^ k
    for d, pack_ref in enumerate(packs):
        areas = [pack_ref[r + 3 : r + 4] for r in range(channels, pack_ref.shape[0], 4)]
        area = jnp.concatenate(areas, 1) if gathered else pick(areas, group)
        area = area * scale
        for n in range(width // block):
            cur = piece_ref[d * channels : (d + 1) * channels, n * block : (n + 1) * block].astype(F32)
            cur = cur * area[:, n * block : (n + 1) * block]
            high = leading(cur)
            low = (cur - high).astype(BF)
            high = high.astype(BF)
            a = jnp.concatenate([high, low], 0)
            b = jnp.concatenate([high[half:], -high[:half], low[half:], -low[:half]], 0)
            start = n * block if gathered else group * width + n * block
            top = pl.multiple_of(2 * start, 2 * block)
            left_ref[d, :, pl.ds(top, block)] = a
            left_ref[d, :, pl.ds(pl.multiple_of(top + block, block), block)] = b


def finish(acc_ref, inc_ref, prev_ref, ends_ref, out_ref):
    channels = inc_ref.shape[0] // 2
    half = channels // 2
    prev = prev_ref[...].astype(F32)
    seg = lax.axis_index("seg")
    diagonal = lax.broadcasted_iota(jnp.int32, (channels, channels), 0) == lax.broadcasted_iota(
        jnp.int32, (channels, channels), 1
    )
    for d, end in enumerate((0, lax.axis_size("seg") - 1)):
        total = acc_ref[d, :channels] + acc_ref[d, channels:]
        other = prev[(1 - d) * channels : (2 - d) * channels]
        flag = jnp.where(seg == end, 1.0, 0.0)
        coef = jnp.sum(jnp.where(diagonal, ends_ref[d : d + 1] * flag, 0.0), axis=1, keepdims=True)
        cre = coef[:half]
        cim = coef[half:]
        mirrored = jnp.concatenate(
            [cre * other[:half] - cim * other[half:], cre * other[half:] + cim * other[:half]], 0
        )
        rows = slice(d * channels, (d + 1) * channels)
        out_ref[rows] = (inc_ref[rows].astype(F32) + total + mirrored).astype(BF)


def accumulate(acc_ref, left_ref, chunk, k_refs):
    targets, rows, block = k_refs[1].shape
    cols = pl.ds(pl.multiple_of(chunk * rows, rows), rows)
    group = 2 if targets % 2 == 0 else 1

    def body(n, carry):
        lanes = pl.ds(pl.multiple_of(n * (group * block), group * block), group * block)
        for d, k_ref in k_refs.items():
            right = jnp.concatenate([k_ref[n * group + g] for g in range(group)], 1)
            part = jnp.dot(left_ref[d, :, cols], right, preferred_element_type=F32)
            acc_ref[d, :, lanes] = jnp.where(chunk == 0, part, acc_ref[d, :, lanes] + part)
        return carry

    lax.fori_loop(0, targets // group, body, 0)


def build_sweep_kernel(
    block, per_chunk, pieces, scale, list_ref, own_ref, before_ref, after_ref, inc_ref, ends_ref, k0_ref, *rest
):
    piece_refs = rest[:pieces]
    k_ref, out_ref, tf_ref, sf_ref, left_ref, acc_ref, even_ref, odd_ref = rest[pieces:]
    chunk = pl.program_id(0)
    channels = inc_ref.shape[0] // 2

    @pl.when(chunk == 0)
    def _():
        build_features(1, channels, own_ref, after_ref, tf_ref, sf_ref)
        for k, piece_ref in enumerate(piece_refs):
            load_piece(k, piece_ref, (before_ref, after_ref), left_ref, scale, block)

    build_chunk(
        1, chunk, block, k_ref.shape[0], list_ref, tf_ref, sf_ref, chunk * (per_chunk * block), k_ref,
        even_ref, odd_ref,
    )
    accumulate(acc_ref, left_ref, chunk, {0: k0_ref, 1: k_ref})

    @pl.when(chunk == pl.num_programs(0) - 1)
    def _():
        finish(acc_ref, inc_ref, inc_ref, ends_ref, out_ref)


def call_build_sweep(block, per_chunk, scale, patches, lists, own, before, after, inc, ends, k0, pieces):
    rows = inc.shape[1]
    chunk_rows = 2 * block * per_chunk
    targets = rows // block
    channels = inc.shape[0]
    spec = table_spec(targets, chunk_rows, block)
    return pl.pallas_call(
        functools.partial(build_sweep_kernel, block, per_chunk, len(pieces), scale),
        grid=(patches // (block * per_chunk),),
        out_shape=(jax.ShapeDtypeStruct(k0.shape, BF), jax.ShapeDtypeStruct(inc.shape, BF)),
        in_specs=[pl.BlockSpec(memory_space=pltpu.SMEM), whole(own), whole(before), whole(after), whole(inc),
                  whole(ends), spec] + [whole(p) for p in pieces],
        out_specs=(spec, whole(inc)),
        scratch_shapes=[
            pltpu.VMEM((FEATURES, rows), BF),
            pltpu.VMEM((patches, FEATURES), BF),
            pltpu.VMEM((2, channels, 2 * patches), BF),
            pltpu.VMEM((2, channels, rows), F32),
            pltpu.VMEM((PAIR * block, block), F32),
            pltpu.VMEM((PAIR * block, block), F32),
        ],
        compiler_params=pltpu.CompilerParams(dimension_semantics=("arbitrary",)),
        name="build_sweep",
    )(lists, own, before, after, inc, ends, k0, *pieces)


def sweep_kernel(block, pieces, scale, before_ref, after_ref, inc_ref, prev_ref, ends_ref, k0_ref, k1_ref, *rest):
    piece_refs = rest[:pieces]
    out_ref, left_ref, acc_ref = rest[pieces:]
    chunk = pl.program_id(0)

    @pl.when(chunk == 0)
    def _():
        for k, piece_ref in enumerate(piece_refs):
            load_piece(k, piece_ref, (before_ref, after_ref), left_ref, scale, block)

    accumulate(acc_ref, left_ref, chunk, {0: k0_ref, 1: k1_ref})

    @pl.when(chunk == pl.num_programs(0) - 1)
    def _():
        finish(acc_ref, inc_ref, prev_ref, ends_ref, out_ref)


def call_sweep(block, per_chunk, scale, patches, before, after, inc, prev, ends, k0, k1, pieces):
    rows = inc.shape[1]
    chunk_rows = 2 * block * per_chunk
    channels = inc.shape[0]
    spec = table_spec(rows // block, chunk_rows, block)
    return pl.pallas_call(
        functools.partial(sweep_kernel, block, len(pieces), scale),
        grid=(patches // (block * per_chunk),),
        out_shape=jax.ShapeDtypeStruct(inc.shape, BF),
        in_specs=[whole(before), whole(after), whole(inc), whole(prev), whole(ends), spec, spec]
        + [whole(p) for p in pieces],
        out_specs=whole(inc),
        scratch_shapes=[
            pltpu.VMEM((2, channels, 2 * patches), BF),
            pltpu.VMEM((2, channels, rows), F32),
        ],
        compiler_params=pltpu.CompilerParams(dimension_semantics=("arbitrary",)),
        name="sweep",
    )(before, after, inc, prev, ends, k0, k1, *pieces)


def shift(value, step):
    count = lax.axis_size("seg")
    return lax.ppermute(value, "seg", [(i, i + step) for i in range(count) if 0 <= i + step < count])


def gather_patches(value):
    count = lax.axis_size("patch")
    if count not in (1, 2, 4):
        return [lax.all_gather(value, "patch", axis=1, tiled=True)]
    return [value] + [
        lax.ppermute(value, "patch", [(i, i ^ k) for i in range(count)]) for k in range(1, count)
    ]


def on_device(incident, wall_axial, wall_angle, wall_area, visibility, end_reflection):
    channels = incident.shape[1]
    patches = wall_axial.shape[1]
    block = patches // visibility.shape[3]
    half = channels // 2
    per_chunk = min(8, patches // block)
    scale = KAPPA / math.sqrt(patches)
    inc = incident[0]
    up, down, lists = call_prep(per_chunk, wall_axial, wall_angle, wall_area, inc, visibility)
    before, after = shift(up, 1), shift(down, -1)
    moved = jnp.concatenate([before[:half], after[:half]], 0).astype(BF)
    pieces = gather_patches(moved)
    k0 = call_build(0, block, per_chunk, half, lists, up, before, patches)
    k1, state = call_build_sweep(
        block, per_chunk, scale, patches, lists, up, before, after, inc, end_reflection, k0, pieces
    )
    for sweep in range(1, ITERS):
        moved = jnp.concatenate([shift(state[:half], 1), shift(state[half:], -1)], 0)
        pieces = gather_patches(moved)
        state = call_sweep(
            block, per_chunk, scale, patches, before, after, inc, state, end_reflection, k0, k1, pieces
        )
    return state[None]


def solution(mesh):
    return jax.shard_map(
        on_device,
        mesh=mesh,
        in_specs=(
            P("seg", None, "patch"),
            P("seg", None),
            P("seg", None),
            P("seg", None),
            P("seg", None, "patch", None),
            P(),
        ),
        out_specs=P("seg", None, "patch"),
        check_vma=False,
    )
```

```python
import functools
import math

import jax
import jax.numpy as jnp
from jax import lax
from jax.experimental import pallas as pl
from jax.experimental.pallas import tpu as pltpu
from jax.sharding import PartitionSpec as P

ITERS = 2

WAVENUMBER = 40.0
RADIUS = 0.5
SOFTENING = 0.25

KAPPA = WAVENUMBER / (2.0 * math.pi)
HALF_CHORD = 2.0 * RADIUS * RADIUS * KAPPA * KAPPA
SINE = tuple(
    value * (1.0 - 5e-7)
    for value in (4.442867903112522, -7.307443423342558, 3.5947880930735288, -0.7843740618048793)
)
SINE_HALF = (0.999999976589841, -0.16666647634617332, 0.00833289982302485, -0.00019800897745117133,
             2.5904884686762915e-06)
COSINE_HALF = (0.9999999997806504, -0.4999999935847076, 0.04166663625803946, -0.0013888361399933481,
               2.476016133696864e-05, -2.605149496508554e-07)

FEATURES = 32
ROOMY = 50 * 2**20
PAIR = 8
BF = jnp.bfloat16
F32 = jnp.float32


def leading(x):
    wide = x * 65537.0
    return wide - (wide - x)


def split3(x):
    high = leading(x)
    rest = x - high
    mid = leading(rest)
    return high, mid, rest - mid


def near_side(geo, direction):
    return (geo[0:1] if direction == 0 else 1.0 - geo[0:1]) * KAPPA


def far_side(geo, direction):
    return (1.0 - geo[0:1] if direction == 0 else geo[0:1]) * KAPPA


def pad_rows(rows):
    width = rows[0].shape[1]
    rows = rows + [jnp.zeros((FEATURES - len(rows), width), F32)]
    return jnp.concatenate(rows, 0)


def target_features(geo, direction):
    u = near_side(geo, direction)
    one = jnp.ones_like(u)
    rows = list(split3(u * u + HALF_CHORD)) + [one, one, one]
    for value in (2.0 * u, -HALF_CHORD * geo[1:2], -HALF_CHORD * geo[2:3]):
        h, m, l = split3(value)
        rows += [h, h, m, m, h, l]
    return pad_rows(rows)


def source_features(geo, direction):
    v = far_side(geo, direction)
    one = jnp.ones_like(v)
    rows = [one, one, one] + list(split3(v * v))
    for value in (v, geo[1:2], geo[2:3]):
        h, m, l = split3(value)
        rows += [h, m, h, m, l, h]
    return pad_rows(rows)


def horner(coefs, x):
    total = coefs[-1]
    for coef in coefs[-2::-1]:
        total = total * x + coef
    return total


def exact_dot(a, b):
    return jnp.dot(a.astype(BF), b.astype(BF), preferred_element_type=F32)


def make_lists(lit, per_chunk):
    targets, sources = lit.shape
    chunks = sources // per_chunk
    size = per_chunk * targets
    i0 = lax.broadcasted_iota(jnp.int32, (sources, sources), 0)
    i1 = lax.broadcasted_iota(jnp.int32, (sources, sources), 1)
    same = i0 // per_chunk == i1 // per_chunk
    above = lax.broadcasted_iota(jnp.int32, (targets, targets), 0) > lax.broadcasted_iota(
        jnp.int32, (targets, targets), 1
    )
    sums = exact_dot(lit, jnp.where(same, 1.0, 0.0))
    rank = exact_dot(lit, jnp.where(same & (i0 < i1), 1.0, 0.0)) + exact_dot(
        jnp.where(above, 1.0, 0.0), sums
    )
    src = lax.broadcasted_iota(jnp.int32, lit.shape, 1) % per_chunk
    tgt = lax.broadcasted_iota(jnp.int32, lit.shape, 0)
    order = (tgt * per_chunk + src).astype(F32)
    place = jnp.where(lit > 0.5, rank, size - 1 - (order - rank))
    code = (src * targets + tgt).astype(F32)
    slot = lax.broadcasted_iota(jnp.int32, (size, sources), 0).astype(F32)
    found = jnp.zeros((size, sources), F32)
    for t in range(targets):
        found += jnp.where(slot == place[t : t + 1], code[t : t + 1], 0.0)
    c0 = lax.broadcasted_iota(jnp.int32, (sources, chunks), 0)
    c1 = lax.broadcasted_iota(jnp.int32, (sources, chunks), 1)
    pick = jnp.where(c0 // per_chunk == c1, 1.0, 0.0)
    codes = exact_dot(found, pick)
    counts = jnp.sum(exact_dot(lit, pick), axis=0, keepdims=True)
    return codes.astype(jnp.int32), counts.astype(jnp.int32)


def prep_kernel(per_chunk, axial_ref, angle_ref, area_ref, inc_ref, vis_ref, up_ref, down_ref, list_ref):
    rows = inc_ref.shape[1]
    channels = inc_ref.shape[0] // 2
    half = angle_ref[...] * 0.5
    square = half * half
    sine = horner(SINE_HALF, square) * half
    cosine = horner(COSINE_HALF, square)
    geo = [axial_ref[...], 1.0 - 2.0 * sine * sine, 2.0 * sine * cosine, area_ref[...]]
    for j in range(axial_ref.shape[1] // rows):
        part = jnp.concatenate([g[:, j * rows : (j + 1) * rows] for g in geo], 0)
        up_ref[channels + 4 * j : channels + 4 * j + 4] = part
        down_ref[channels + 4 * j : channels + 4 * j + 4] = part
    up_ref[:channels] = inc_ref[:channels].astype(F32)
    down_ref[:channels] = inc_ref[channels:].astype(F32)
    for d in range(2):
        codes, counts = make_lists(vis_ref[0, d].astype(F32), per_chunk)
        list_ref[d, : codes.shape[0]] = codes
        list_ref[d, codes.shape[0] :] = jnp.broadcast_to(counts, (8, counts.shape[1]))


def call_prep(per_chunk, axial, angle, area, inc, visibility):
    targets, sources = visibility.shape[2], visibility.shape[3]
    channels = inc.shape[0] // 2
    rows, patches = inc.shape[1], axial.shape[1]
    pack = jax.ShapeDtypeStruct((channels + 4 * (patches // rows), rows), F32)
    vmem = pl.BlockSpec(memory_space=pltpu.VMEM)
    return pl.pallas_call(
        functools.partial(prep_kernel, per_chunk),
        out_shape=(
            pack, pack,
            jax.ShapeDtypeStruct((2, per_chunk * targets + 8, sources // per_chunk), jnp.int32),
        ),
        in_specs=[vmem] * 5,
        out_specs=[vmem] * 3,
        name="prep",
    )(axial, angle, area, inc, visibility)


def table_block(q):
    q = jnp.maximum(q, 1e-12)
    turns = q * lax.rsqrt(q)
    f = turns - jnp.round(turns)
    mag = lax.rsqrt(q + SOFTENING * KAPPA * KAPPA)
    s = horner(SINE, f * f) * f
    rest = 2.0 - s * s
    both = mag * rest
    real = both - mag
    imag = (s * both) * lax.rsqrt(rest)
    return real.astype(BF), imag.astype(BF)


def build_chunk(direction, chunk, block, targets, list_ref, tf_ref, sf_ref, base, k_ref, even_ref, odd_ref):
    size = list_ref.shape[1] - 8
    count = list_ref[direction, size, chunk]

    def block_of(n):
        code = list_ref[direction, jnp.maximum(jnp.minimum(n, count - 1), 0), chunk]
        return lax.div(code, jnp.int32(targets)), lax.rem(code, jnp.int32(targets))

    def distances(group, q_ref):
        for u in range(PAIR):
            src, tgt = block_of(group * PAIR + u)
            cols = pl.ds(pl.multiple_of(tgt * block, block), block)
            feats = sf_ref[pl.ds(pl.multiple_of(base + src * block, block), block), :]
            q_ref[u * block : (u + 1) * block] = jnp.dot(feats, tf_ref[:, cols], preferred_element_type=F32)

    def entries(group, q_ref):
        for u in range(PAIR):
            src, tgt = block_of(group * PAIR + u)
            top = pl.multiple_of(src * (2 * block), 2 * block)
            part = 32
            for h in range(0, block, part):
                real, imag = table_block(q_ref[u * block + h : u * block + h + part])
                k_ref[tgt, pl.ds(pl.multiple_of(top + h, part), part), :] = real
                k_ref[tgt, pl.ds(pl.multiple_of(top + block + h, part), part), :] = imag

    def body(step, carry):
        distances(step, even_ref)
        entries(step, even_ref)
        return carry

    lax.fori_loop(0, lax.div(count + PAIR - 1, jnp.int32(PAIR)), body, 0)

    def clear(n, carry):
        code = list_ref[direction, n, chunk]
        src, tgt = lax.div(code, jnp.int32(targets)), lax.rem(code, jnp.int32(targets))
        rows = pl.ds(pl.multiple_of(src * (2 * block), 2 * block), 2 * block)
        k_ref[tgt, rows, :] = jnp.zeros((2 * block, block), BF)
        return carry

    lax.fori_loop(count, size, clear, 0)


def quarters(pack_ref, channels):
    return [pack_ref[r : r + 4] for r in range(channels, pack_ref.shape[0], 4)]


def pick(parts, index):
    chosen = parts[0]
    for j in range(1, len(parts)):
        chosen = jnp.where(index == j, parts[j], chosen)
    return chosen


def build_features(direction, channels, own_ref, pack_ref, tf_ref, sf_ref):
    rows = own_ref.shape[1]
    own = pick(quarters(own_ref, channels), lax.axis_index("patch"))
    tf_ref[...] = target_features(own, direction).astype(BF)
    for j, geo in enumerate(quarters(pack_ref, channels)):
        sf_ref[j * rows : (j + 1) * rows] = source_features(geo, direction).T.astype(BF)


def build_kernel(direction, block, per_chunk, channels, list_ref, own_ref, pack_ref, k_ref, tf_ref, sf_ref, *q):
    chunk = pl.program_id(0)

    @pl.when(chunk == 0)
    def _():
        build_features(direction, channels, own_ref, pack_ref, tf_ref, sf_ref)

    build_chunk(
        direction, chunk, block, k_ref.shape[0], list_ref, tf_ref, sf_ref, chunk * (per_chunk * block), k_ref, *q
    )


def whole(x):
    return pl.BlockSpec(x.shape, lambda c: (0,) * x.ndim)


def table_spec(targets, chunk_rows, block):
    return pl.BlockSpec((targets, chunk_rows, block), lambda c: (0, c, 0))


def call_build(direction, block, per_chunk, channels, lists, own, pack, patches):
    rows = own.shape[1]
    targets = rows // block
    chunk_rows = 2 * block * per_chunk
    return pl.pallas_call(
        functools.partial(build_kernel, direction, block, per_chunk, channels),
        grid=(patches // (block * per_chunk),),
        out_shape=jax.ShapeDtypeStruct((targets, 2 * patches, block), BF),
        in_specs=[pl.BlockSpec(memory_space=pltpu.SMEM), whole(own), whole(pack)],
        out_specs=table_spec(targets, chunk_rows, block),
        scratch_shapes=[
            pltpu.VMEM((FEATURES, rows), BF),
            pltpu.VMEM((patches, FEATURES), BF),
            pltpu.VMEM((PAIR * block, block), F32),
            pltpu.VMEM((PAIR * block, block), F32),
        ],
        compiler_params=pltpu.CompilerParams(dimension_semantics=("arbitrary",), vmem_limit_bytes=ROOMY),
        name=f"build{direction}",
    )(lists, own, pack)


def load_piece(k, piece_ref, packs, left_ref, scale, block, local=False):
    channels = piece_ref.shape[0] // 2
    half = channels // 2
    width = piece_ref.shape[1]
    gathered = width != packs[0].shape[1]
    group = lax.axis_index("patch") ^ k
    for d, pack_ref in enumerate(packs):
        areas = [pack_ref[r + 3 : r + 4] for r in range(channels, pack_ref.shape[0], 4)]
        area = jnp.concatenate(areas, 1) if gathered else pick(areas, group)
        area = area * scale
        for n in range(width // block):
            cur = piece_ref[d * channels : (d + 1) * channels, n * block : (n + 1) * block].astype(F32)
            cur = cur * area[:, n * block : (n + 1) * block]
            high = leading(cur)
            low = (cur - high).astype(BF)
            high = high.astype(BF)
            a = jnp.concatenate([high, low], 0)
            b = jnp.concatenate([high[half:], -high[:half], low[half:], -low[:half]], 0)
            start = n * block if gathered or local else group * width + n * block
            top = pl.multiple_of(2 * start, 2 * block)
            left_ref[d, :, pl.ds(top, block)] = a
            left_ref[d, :, pl.ds(pl.multiple_of(top + block, block), block)] = b


def finish(acc_ref, inc_ref, prev, ends_ref, store):
    channels = inc_ref.shape[0] // 2
    half = channels // 2
    seg = lax.axis_index("seg")
    diagonal = lax.broadcasted_iota(jnp.int32, (channels, channels), 0) == lax.broadcasted_iota(
        jnp.int32, (channels, channels), 1
    )
    for d, end in enumerate((0, lax.axis_size("seg") - 1)):
        total = acc_ref[d, :channels] + acc_ref[d, channels:]
        other = prev[1 - d].astype(F32)
        flag = jnp.where(seg == end, 1.0, 0.0)
        coef = jnp.sum(jnp.where(diagonal, ends_ref[d : d + 1] * flag, 0.0), axis=1, keepdims=True)
        cre = coef[:half]
        cim = coef[half:]
        mirrored = jnp.concatenate(
            [cre * other[:half] - cim * other[half:], cre * other[half:] + cim * other[:half]], 0
        )
        rows = slice(d * channels, (d + 1) * channels)
        store(d, (inc_ref[rows].astype(F32) + total + mirrored).astype(BF))


def accumulate(acc_ref, left_ref, chunk, k_refs):
    targets, rows, block = k_refs[1].shape
    cols = pl.ds(pl.multiple_of(chunk * rows, rows), rows)
    group = 2 if targets % 2 == 0 else 1

    def body(n, carry):
        lanes = pl.ds(pl.multiple_of(n * (group * block), group * block), group * block)
        for d, k_ref in k_refs.items():
            right = jnp.concatenate([k_ref[n * group + g] for g in range(group)], 1)
            part = jnp.dot(left_ref[d, :, cols], right, preferred_element_type=F32)
            acc_ref[d, :, lanes] = jnp.where(chunk == 0, part, acc_ref[d, :, lanes] + part)
        return carry

    lax.fori_loop(0, targets // group, body, 0)


def build_sweep_kernel(
    block, per_chunk, pieces, scale, list_ref, own_ref, before_ref, after_ref, inc_ref, ends_ref, k0_ref, *rest
):
    piece_refs = rest[:pieces]
    k_ref, fore_ref, back_ref, tf_ref, sf_ref, left_ref, acc_ref, even_ref, odd_ref = rest[pieces:]
    chunk = pl.program_id(0)
    channels = inc_ref.shape[0] // 2

    @pl.when(chunk == 0)
    def _():
        build_features(1, channels, own_ref, after_ref, tf_ref, sf_ref)
        for k, piece_ref in enumerate(piece_refs):
            load_piece(k, piece_ref, (before_ref, after_ref), left_ref, scale, block)

    build_chunk(
        1, chunk, block, k_ref.shape[0], list_ref, tf_ref, sf_ref, chunk * (per_chunk * block), k_ref,
        even_ref, odd_ref,
    )
    accumulate(acc_ref, left_ref, chunk, {0: k0_ref, 1: k_ref})

    @pl.when(chunk == pl.num_programs(0) - 1)
    def _():
        def store(d, value):
            (fore_ref, back_ref)[d][...] = value

        finish(acc_ref, inc_ref, (inc_ref[:channels], inc_ref[channels:]), ends_ref, store)


def call_build_sweep(block, per_chunk, scale, patches, lists, own, before, after, inc, ends, k0, pieces):
    rows = inc.shape[1]
    chunk_rows = 2 * block * per_chunk
    targets = rows // block
    channels = inc.shape[0]
    part = jax.ShapeDtypeStruct((channels // 2, rows), BF)
    spec = table_spec(targets, chunk_rows, block)
    return pl.pallas_call(
        functools.partial(build_sweep_kernel, block, per_chunk, len(pieces), scale),
        grid=(patches // (block * per_chunk),),
        out_shape=(jax.ShapeDtypeStruct(k0.shape, BF), part, part),
        in_specs=[pl.BlockSpec(memory_space=pltpu.SMEM), whole(own), whole(before), whole(after), whole(inc),
                  whole(ends), spec] + [whole(p) for p in pieces],
        out_specs=(spec, whole(part), whole(part)),
        scratch_shapes=[
            pltpu.VMEM((FEATURES, rows), BF),
            pltpu.VMEM((patches, FEATURES), BF),
            pltpu.VMEM((2, channels, 2 * patches), BF),
            pltpu.VMEM((2, channels, rows), F32),
            pltpu.VMEM((PAIR * block, block), F32),
            pltpu.VMEM((PAIR * block, block), F32),
        ],
        compiler_params=pltpu.CompilerParams(dimension_semantics=("arbitrary",), vmem_limit_bytes=ROOMY),
        name="build_sweep",
    )(lists, own, before, after, inc, ends, k0, *pieces)


def sweep_kernel(groups, block, scale, first, last, *refs):
    before_ref, after_ref, inc_ref, fore_ref, back_ref, ends_ref, k0_ref, k1_ref = refs[:8]
    count = len(groups)
    piece_refs = refs[8 : 8 + count]
    refs = refs[8 + count :]
    if not first:
        base_ref, refs = refs[0], refs[1:]
    out_ref, refs = refs[0], refs[1:]
    acc_ref = refs[0] if last else out_ref
    left_ref, buf_ref, sem_ref = refs[-3:]
    targets = k0_ref.shape[0]
    rows = buf_ref.shape[3]
    copies = {}
    for g, k in enumerate(groups):
        start = pl.multiple_of((lax.axis_index("patch") ^ k) * rows, block) if rows < k0_ref.shape[1] else 0
        for d, k_ref in enumerate((k0_ref, k1_ref)):
            copies[g, d] = pltpu.make_async_copy(
                k_ref.at[:, pl.ds(start, rows), :], buf_ref.at[g, d], sem_ref.at[g, d]
            )
            copies[g, d].start()
    for g, (k, piece_ref) in enumerate(zip(groups, piece_refs)):
        load_piece(k, piece_ref, (before_ref, after_ref), left_ref.at[g], scale, block, local=True)
    if not first:
        acc_ref[...] = base_ref[...]
    unit = 2 if targets % 2 == 0 else 1
    for g in range(count):
        for d in range(2):
            copies[g, d].wait()

            def body(n, carry, g=g, d=d):
                right = jnp.concatenate([buf_ref[g, d, n * unit + u] for u in range(unit)], 1)
                lanes = pl.ds(pl.multiple_of(n * (unit * block), unit * block), unit * block)
                part = jnp.dot(left_ref[g, d], right, preferred_element_type=F32)
                acc_ref[d, :, lanes] = part if first and g == 0 else acc_ref[d, :, lanes] + part
                return carry

            lax.fori_loop(0, targets // unit, body, 0)
    if last:
        half = out_ref.shape[0] // 2

        def store(d, value):
            out_ref[d * half : (d + 1) * half] = value

        finish(acc_ref, inc_ref, (fore_ref[...], back_ref[...]), ends_ref, store)


def call_sweep(groups, block, scale, before, after, inc, fore, back, ends, k0, k1, pieces, base, last):
    channels, rows = inc.shape
    targets = k0.shape[0]
    depth = 2 * pieces[0].shape[1]
    vmem = pl.BlockSpec(memory_space=pltpu.VMEM)
    table = pl.BlockSpec(memory_space=pl.ANY)
    extra = [] if base is None else [base]
    sums = jax.ShapeDtypeStruct((2, channels, rows), F32)
    return pl.pallas_call(
        functools.partial(sweep_kernel, groups, block, scale, base is None, last),
        out_shape=jax.ShapeDtypeStruct(inc.shape, BF) if last else sums,
        in_specs=[vmem] * 6 + [table] * 2 + [vmem] * (len(pieces) + len(extra)),
        out_specs=vmem,
        scratch_shapes=([pltpu.VMEM(sums.shape, F32)] if last else [])
        + [
            pltpu.VMEM((len(groups), 2, channels, depth), BF),
            pltpu.VMEM((len(groups), 2, targets, depth, block), BF),
            pltpu.SemaphoreType.DMA((len(groups), 2)),
        ],
        cost_estimate=pl.CostEstimate(
            flops=4 * len(groups) * channels * rows * depth,
            bytes_accessed=4 * len(groups) * rows * depth,
            transcendentals=0,
        ),
        compiler_params=pltpu.CompilerParams(vmem_limit_bytes=ROOMY),
        name="sweep" if last else "own_sweep",
    )(before, after, inc, fore, back, ends, k0, k1, *pieces, *extra)


def join_kernel(top_ref, bottom_ref, out_ref):
    half = out_ref.shape[0] // 2
    out_ref[:half] = top_ref[:half].astype(BF)
    out_ref[half:] = bottom_ref[:half].astype(BF)


def join(top, bottom, channels):
    vmem = pl.BlockSpec(memory_space=pltpu.VMEM)
    return pl.pallas_call(
        join_kernel,
        out_shape=jax.ShapeDtypeStruct((channels, top.shape[1]), BF),
        in_specs=[vmem] * 2,
        out_specs=vmem,
        compiler_params=pltpu.CompilerParams(vmem_limit_bytes=4 * 2**20),
        name="join",
    )(top, bottom)


def shift(value, step):
    count = lax.axis_size("seg")
    return lax.ppermute(value, "seg", [(i, i + step) for i in range(count) if 0 <= i + step < count])


def gather_patches(value):
    count = lax.axis_size("patch")
    if count not in (1, 2, 4):
        return [lax.all_gather(value, "patch", axis=1, tiled=True)]
    return [value] + [
        lax.ppermute(value, "patch", [(i, i ^ k) for i in range(count)]) for k in range(1, count)
    ]


def on_device(incident, wall_axial, wall_angle, wall_area, visibility, end_reflection):
    channels = incident.shape[1]
    patches = wall_axial.shape[1]
    block = patches // visibility.shape[3]
    half = channels // 2
    per_chunk = min(8, patches // block)
    scale = KAPPA / math.sqrt(patches)
    inc = incident[0]
    up, down, lists = call_prep(per_chunk, wall_axial, wall_angle, wall_area, inc, visibility)
    before, after = shift(up, 1), shift(down, -1)
    pieces = gather_patches(join(before, after, channels))
    k0 = call_build(0, block, per_chunk, half, lists, up, before, patches)
    k1, fore, back = call_build_sweep(
        block, per_chunk, scale, patches, lists, up, before, after, inc, end_reflection, k0, pieces
    )
    for sweep in range(1, ITERS):
        pieces = gather_patches(join(shift(fore, 1), shift(back, -1), channels))
        groups = tuple(range(len(pieces)))
        common = (block, scale, before, after, inc, fore, back, end_reflection, k0, k1)
        base = None
        if len(groups) > 1:
            base = call_sweep(groups[:1], *common, pieces[:1], None, False)
            groups, pieces = groups[1:], pieces[1:]
        state = call_sweep(groups, *common, pieces, base, True)
        if sweep + 1 < ITERS:
            fore, back = state[:half], state[half:]
    return state[None]


def solution(mesh):
    return jax.shard_map(
        on_device,
        mesh=mesh,
        in_specs=(
            P("seg", None, "patch"),
            P("seg", None),
            P("seg", None),
            P("seg", None),
            P("seg", None, "patch", None),
            P(),
        ),
        out_specs=P("seg", None, "patch"),
        check_vma=False,
    )
```

```python
import functools
import math

import jax
import jax.numpy as jnp
from jax import lax
from jax.experimental import pallas as pl
from jax.experimental.pallas import tpu as pltpu
from jax.sharding import PartitionSpec as P

ITERS = 2

WAVENUMBER = 40.0
RADIUS = 0.5
SOFTENING = 0.25

KAPPA = WAVENUMBER / (2.0 * math.pi)
HALF_CHORD = 2.0 * RADIUS * RADIUS * KAPPA * KAPPA
SINE = tuple(
    value * (1.0 - 5e-7)
    for value in (4.442867903112522, -7.307443423342558, 3.5947880930735288, -0.7843740618048793)
)
SINE_HALF = (0.999999976589841, -0.16666647634617332, 0.00833289982302485, -0.00019800897745117133,
             2.5904884686762915e-06)
COSINE_HALF = (0.9999999997806504, -0.4999999935847076, 0.04166663625803946, -0.0013888361399933481,
               2.476016133696864e-05, -2.605149496508554e-07)

FEATURES = 32
ROOMY = 50 * 2**20
PAIR = 8
BF = jnp.bfloat16
F32 = jnp.float32


def leading(x):
    wide = x * 65537.0
    return wide - (wide - x)


def split3(x):
    high = leading(x)
    rest = x - high
    mid = leading(rest)
    return high, mid, rest - mid


def near_side(geo, direction):
    return (geo[0:1] if direction == 0 else 1.0 - geo[0:1]) * KAPPA


def far_side(geo, direction):
    return (1.0 - geo[0:1] if direction == 0 else geo[0:1]) * KAPPA


def pad_rows(rows):
    width = rows[0].shape[1]
    rows = rows + [jnp.zeros((FEATURES - len(rows), width), F32)]
    return jnp.concatenate(rows, 0)


def target_features(geo, direction):
    u = near_side(geo, direction)
    one = jnp.ones_like(u)
    rows = list(split3(u * u + HALF_CHORD)) + [one, one, one]
    for value in (2.0 * u, -HALF_CHORD * geo[1:2], -HALF_CHORD * geo[2:3]):
        h, m, l = split3(value)
        rows += [h, h, m, m, h, l]
    return pad_rows(rows)


def source_features(geo, direction):
    v = far_side(geo, direction)
    one = jnp.ones_like(v)
    rows = [one, one, one] + list(split3(v * v))
    for value in (v, geo[1:2], geo[2:3]):
        h, m, l = split3(value)
        rows += [h, m, h, m, l, h]
    return pad_rows(rows)


def horner(coefs, x):
    total = coefs[-1]
    for coef in coefs[-2::-1]:
        total = total * x + coef
    return total


def exact_dot(a, b):
    return jnp.dot(a.astype(BF), b.astype(BF), preferred_element_type=F32)


def make_lists(lit, per_chunk):
    targets, sources = lit.shape
    chunks = sources // per_chunk
    size = per_chunk * targets
    i0 = lax.broadcasted_iota(jnp.int32, (sources, sources), 0)
    i1 = lax.broadcasted_iota(jnp.int32, (sources, sources), 1)
    same = i0 // per_chunk == i1 // per_chunk
    above = lax.broadcasted_iota(jnp.int32, (targets, targets), 0) > lax.broadcasted_iota(
        jnp.int32, (targets, targets), 1
    )
    sums = exact_dot(lit, jnp.where(same, 1.0, 0.0))
    rank = exact_dot(lit, jnp.where(same & (i0 < i1), 1.0, 0.0)) + exact_dot(
        jnp.where(above, 1.0, 0.0), sums
    )
    src = lax.broadcasted_iota(jnp.int32, lit.shape, 1) % per_chunk
    tgt = lax.broadcasted_iota(jnp.int32, lit.shape, 0)
    order = (tgt * per_chunk + src).astype(F32)
    place = jnp.where(lit > 0.5, rank, size - 1 - (order - rank))
    code = (src * targets + tgt).astype(F32)
    slot = lax.broadcasted_iota(jnp.int32, (size, sources), 0).astype(F32)
    found = jnp.zeros((size, sources), F32)
    for t in range(targets):
        found += jnp.where(slot == place[t : t + 1], code[t : t + 1], 0.0)
    c0 = lax.broadcasted_iota(jnp.int32, (sources, chunks), 0)
    c1 = lax.broadcasted_iota(jnp.int32, (sources, chunks), 1)
    pick = jnp.where(c0 // per_chunk == c1, 1.0, 0.0)
    codes = exact_dot(found, pick)
    counts = jnp.sum(exact_dot(lit, pick), axis=0, keepdims=True)
    return codes.astype(jnp.int32), counts.astype(jnp.int32)


def prep_kernel(per_chunk, axial_ref, angle_ref, area_ref, inc_ref, vis_ref, up_ref, down_ref, list_ref):
    rows = inc_ref.shape[1]
    channels = inc_ref.shape[0] // 2
    half = angle_ref[...] * 0.5
    square = half * half
    sine = horner(SINE_HALF, square) * half
    cosine = horner(COSINE_HALF, square)
    geo = [axial_ref[...], 1.0 - 2.0 * sine * sine, 2.0 * sine * cosine, area_ref[...]]
    for j in range(axial_ref.shape[1] // rows):
        part = jnp.concatenate([g[:, j * rows : (j + 1) * rows] for g in geo], 0)
        up_ref[channels + 4 * j : channels + 4 * j + 4] = part
        down_ref[channels + 4 * j : channels + 4 * j + 4] = part
    up_ref[:channels] = inc_ref[:channels].astype(F32)
    down_ref[:channels] = inc_ref[channels:].astype(F32)
    for d in range(2):
        codes, counts = make_lists(vis_ref[0, d].astype(F32), per_chunk)
        list_ref[d, : codes.shape[0]] = codes
        list_ref[d, codes.shape[0] :] = jnp.broadcast_to(counts, (8, counts.shape[1]))


def call_prep(per_chunk, axial, angle, area, inc, visibility):
    targets, sources = visibility.shape[2], visibility.shape[3]
    channels = inc.shape[0] // 2
    rows, patches = inc.shape[1], axial.shape[1]
    pack = jax.ShapeDtypeStruct((channels + 4 * (patches // rows), rows), F32)
    vmem = pl.BlockSpec(memory_space=pltpu.VMEM)
    axial, angle, area, inc, visibility = [
        pltpu.with_memory_space_constraint(x, pltpu.HBM) for x in (axial, angle, area, inc, visibility)
    ]
    return pl.pallas_call(
        functools.partial(prep_kernel, per_chunk),
        out_shape=(
            pack, pack,
            jax.ShapeDtypeStruct((2, per_chunk * targets + 8, sources // per_chunk), jnp.int32),
        ),
        in_specs=[vmem] * 5,
        out_specs=[vmem] * 3,
        compiler_params=pltpu.CompilerParams(vmem_limit_bytes=ROOMY),
        name="prep",
    )(axial, angle, area, inc, visibility)


def table_block(q):
    q = jnp.maximum(q, 1e-12)
    turns = q * lax.rsqrt(q)
    f = turns - jnp.round(turns)
    mag = lax.rsqrt(q + SOFTENING * KAPPA * KAPPA)
    s = horner(SINE, f * f) * f
    rest = 2.0 - s * s
    both = mag * rest
    real = both - mag
    imag = (s * both) * lax.rsqrt(rest)
    return real.astype(BF), imag.astype(BF)


def build_chunk(direction, chunk, block, targets, list_ref, tf_ref, sf_ref, base, k_ref, q_ref):
    size = list_ref.shape[1] - 8
    count = list_ref[direction, size, chunk]

    def block_of(n):
        code = list_ref[direction, jnp.maximum(jnp.minimum(n, count - 1), 0), chunk]
        return lax.div(code, jnp.int32(targets)), lax.rem(code, jnp.int32(targets))

    def distances(group, q_ref):
        for u in range(PAIR):
            src, tgt = block_of(group * PAIR + u)
            cols = pl.ds(pl.multiple_of(tgt * block, block), block)
            feats = sf_ref[pl.ds(pl.multiple_of(base + src * block, block), block), :]
            q_ref[u * block : (u + 1) * block] = jnp.dot(feats, tf_ref[:, cols], preferred_element_type=F32)

    def entries(group, q_ref):
        for u in range(PAIR):
            src, tgt = block_of(group * PAIR + u)
            top = pl.multiple_of(src * (2 * block), 2 * block)
            part = 32
            for h in range(0, block, part):
                real, imag = table_block(q_ref[u * block + h : u * block + h + part])
                k_ref[tgt, pl.ds(pl.multiple_of(top + h, part), part), :] = real
                k_ref[tgt, pl.ds(pl.multiple_of(top + block + h, part), part), :] = imag

    def body(step, carry):
        distances(step, q_ref)
        entries(step, q_ref)
        return carry

    lax.fori_loop(0, lax.div(count + PAIR - 1, jnp.int32(PAIR)), body, 0)

    def clear(n, carry):
        code = list_ref[direction, n, chunk]
        src, tgt = lax.div(code, jnp.int32(targets)), lax.rem(code, jnp.int32(targets))
        rows = pl.ds(pl.multiple_of(src * (2 * block), 2 * block), 2 * block)
        k_ref[tgt, rows, :] = jnp.zeros((2 * block, block), BF)
        return carry

    lax.fori_loop(count, size, clear, 0)


def quarters(pack_ref, channels):
    return [pack_ref[r : r + 4] for r in range(channels, pack_ref.shape[0], 4)]


def pick(parts, index):
    chosen = parts[0]
    for j in range(1, len(parts)):
        chosen = jnp.where(index == j, parts[j], chosen)
    return chosen


def build_features(direction, channels, own_ref, pack_ref, tf_ref, sf_ref):
    rows = own_ref.shape[1]
    own = pick(quarters(own_ref, channels), lax.axis_index("patch"))
    tf_ref[...] = target_features(own, direction).astype(BF)
    for j, geo in enumerate(quarters(pack_ref, channels)):
        sf_ref[j * rows : (j + 1) * rows] = source_features(geo, direction).T.astype(BF)


def build_kernel(direction, block, per_chunk, channels, list_ref, own_ref, pack_ref, k_ref, tf_ref, sf_ref, *q):
    chunk = pl.program_id(0)

    @pl.when(chunk == 0)
    def _():
        build_features(direction, channels, own_ref, pack_ref, tf_ref, sf_ref)

    build_chunk(
        direction, chunk, block, k_ref.shape[0], list_ref, tf_ref, sf_ref, chunk * (per_chunk * block), k_ref, *q
    )


def whole(x):
    return pl.BlockSpec(x.shape, lambda c: (0,) * x.ndim)


def table_spec(targets, chunk_rows, block):
    return pl.BlockSpec((targets, chunk_rows, block), lambda c: (0, c, 0))


def call_build(direction, block, per_chunk, channels, lists, own, pack, patches):
    rows = own.shape[1]
    targets = rows // block
    chunk_rows = 2 * block * per_chunk
    return pl.pallas_call(
        functools.partial(build_kernel, direction, block, per_chunk, channels),
        grid=(patches // (block * per_chunk),),
        out_shape=jax.ShapeDtypeStruct((targets, 2 * patches, block), BF),
        in_specs=[pl.BlockSpec(memory_space=pltpu.SMEM), whole(own), whole(pack)],
        out_specs=table_spec(targets, chunk_rows, block),
        scratch_shapes=[
            pltpu.VMEM((FEATURES, rows), BF),
            pltpu.VMEM((patches, FEATURES), BF),
            pltpu.VMEM((PAIR * block, block), F32),
        ],
        compiler_params=pltpu.CompilerParams(dimension_semantics=("arbitrary",), vmem_limit_bytes=ROOMY),
        name=f"build{direction}",
    )(lists, own, pack)


def load_piece(k, piece_ref, packs, left_ref, scale, block, local=False):
    channels = piece_ref.shape[0] // 2
    half = channels // 2
    width = piece_ref.shape[1]
    gathered = width != packs[0].shape[1]
    group = lax.axis_index("patch") ^ k
    for d, pack_ref in enumerate(packs):
        areas = [pack_ref[r + 3 : r + 4] for r in range(channels, pack_ref.shape[0], 4)]
        area = jnp.concatenate(areas, 1) if gathered else pick(areas, group)
        area = area * scale
        for n in range(width // block):
            cur = piece_ref[d * channels : (d + 1) * channels, n * block : (n + 1) * block].astype(F32)
            cur = cur * area[:, n * block : (n + 1) * block]
            high = leading(cur)
            low = (cur - high).astype(BF)
            high = high.astype(BF)
            a = jnp.concatenate([high, low], 0)
            b = jnp.concatenate([high[half:], -high[:half], low[half:], -low[:half]], 0)
            start = n * block if gathered or local else group * width + n * block
            top = pl.multiple_of(2 * start, 2 * block)
            left_ref[d, :, pl.ds(top, block)] = a
            left_ref[d, :, pl.ds(pl.multiple_of(top + block, block), block)] = b


def finish(acc_ref, inc_ref, prev, ends_ref, store):
    channels = inc_ref.shape[0] // 2
    half = channels // 2
    seg = lax.axis_index("seg")
    diagonal = lax.broadcasted_iota(jnp.int32, (channels, channels), 0) == lax.broadcasted_iota(
        jnp.int32, (channels, channels), 1
    )
    for d, end in enumerate((0, lax.axis_size("seg") - 1)):
        total = acc_ref[d, :channels] + acc_ref[d, channels:]
        other = prev[1 - d].astype(F32)
        flag = jnp.where(seg == end, 1.0, 0.0)
        coef = jnp.sum(jnp.where(diagonal, ends_ref[d : d + 1] * flag, 0.0), axis=1, keepdims=True)
        cre = coef[:half]
        cim = coef[half:]
        mirrored = jnp.concatenate(
            [cre * other[:half] - cim * other[half:], cre * other[half:] + cim * other[:half]], 0
        )
        rows = slice(d * channels, (d + 1) * channels)
        store(d, (inc_ref[rows].astype(F32) + total + mirrored).astype(BF))


def accumulate(acc_ref, left_ref, chunk, k_refs):
    targets, rows, block = k_refs[1].shape
    cols = pl.ds(pl.multiple_of(chunk * rows, rows), rows)
    group = 2 if targets % 2 == 0 else 1

    def body(n, carry):
        lanes = pl.ds(pl.multiple_of(n * (group * block), group * block), group * block)
        for d, k_ref in k_refs.items():
            right = jnp.concatenate([k_ref[n * group + g] for g in range(group)], 1)
            part = jnp.dot(left_ref[d, :, cols], right, preferred_element_type=F32)
            acc_ref[d, :, lanes] = jnp.where(chunk == 0, part, acc_ref[d, :, lanes] + part)
        return carry

    lax.fori_loop(0, targets // group, body, 0)


def build_sweep_kernel(
    block, per_chunk, pieces, scale, list_ref, own_ref, before_ref, after_ref, inc_ref, ends_ref, k0_ref, *rest
):
    piece_refs = rest[:pieces]
    k1_ref, fore_ref, back_ref, tf_ref, sf_ref, left_ref, acc_ref, q_ref = rest[pieces : pieces + 8]
    in_ref, k_ref, in_sem, out_sem = rest[pieces + 8 :]
    chunk = pl.program_id(0)
    chunks = pl.num_programs(0)
    channels = inc_ref.shape[0] // 2
    rows = in_ref.shape[2]
    slot = lax.rem(chunk, 2)

    def fetch(c, place):
        part = k0_ref.at[:, pl.ds(pl.multiple_of(c * rows, rows), rows), :]
        return pltpu.make_async_copy(part, in_ref.at[place], in_sem.at[place])

    def send(c, place):
        part = k1_ref.at[:, pl.ds(pl.multiple_of(c * rows, rows), rows), :]
        return pltpu.make_async_copy(k_ref.at[place], part, out_sem.at[place])

    @pl.when(chunk == 0)
    def _():
        fetch(chunk, slot).start()

    @pl.when(chunk + 1 < chunks)
    def _():
        fetch(chunk + 1, 1 - slot).start()

    @pl.when(chunk == 0)
    def _():
        build_features(1, channels, own_ref, after_ref, tf_ref, sf_ref)
        for k, piece_ref in enumerate(piece_refs):
            load_piece(k, piece_ref, (before_ref, after_ref), left_ref, scale, block)

    @pl.when(chunk >= 2)
    def _():
        send(chunk - 2, slot).wait()

    build_chunk(
        1, chunk, block, in_ref.shape[1], list_ref, tf_ref, sf_ref, chunk * (per_chunk * block),
        k_ref.at[slot], q_ref,
    )
    send(chunk, slot).start()
    fetch(chunk, slot).wait()
    accumulate(acc_ref, left_ref, chunk, {0: in_ref.at[slot], 1: k_ref.at[slot]})

    @pl.when(chunk == chunks - 1)
    def _():
        def store(d, value):
            (fore_ref, back_ref)[d][...] = value

        finish(acc_ref, inc_ref, (inc_ref[:channels], inc_ref[channels:]), ends_ref, store)
        send(chunk, slot).wait()

    @pl.when((chunk == chunks - 1) & (chunk >= 1))
    def _():
        send(chunk - 1, 1 - slot).wait()


def call_build_sweep(block, per_chunk, scale, patches, lists, own, before, after, inc, ends, k0, pieces):
    rows = inc.shape[1]
    chunk_rows = 2 * block * per_chunk
    targets = rows // block
    channels = inc.shape[0]
    part = jax.ShapeDtypeStruct((channels // 2, rows), BF)
    table = pl.BlockSpec(memory_space=pl.ANY)
    return pl.pallas_call(
        functools.partial(build_sweep_kernel, block, per_chunk, len(pieces), scale),
        grid=(patches // (block * per_chunk),),
        out_shape=(jax.ShapeDtypeStruct(k0.shape, BF), part, part),
        in_specs=[pl.BlockSpec(memory_space=pltpu.SMEM), whole(own), whole(before), whole(after), whole(inc),
                  whole(ends), table] + [whole(p) for p in pieces],
        out_specs=(table, whole(part), whole(part)),
        scratch_shapes=[
            pltpu.VMEM((FEATURES, rows), BF),
            pltpu.VMEM((patches, FEATURES), BF),
            pltpu.VMEM((2, channels, 2 * patches), BF),
            pltpu.VMEM((2, channels, rows), F32),
            pltpu.VMEM((PAIR * block, block), F32),
            pltpu.VMEM((2, targets, chunk_rows, block), BF),
            pltpu.VMEM((2, targets, chunk_rows, block), BF),
            pltpu.SemaphoreType.DMA((2,)),
            pltpu.SemaphoreType.DMA((2,)),
        ],
        compiler_params=pltpu.CompilerParams(dimension_semantics=("arbitrary",), vmem_limit_bytes=ROOMY),
        name="build_sweep",
    )(lists, own, before, after, inc, ends, k0, *pieces)


def sweep_kernel(groups, block, scale, first, last, *refs):
    before_ref, after_ref, inc_ref, fore_ref, back_ref, ends_ref, k0_ref, k1_ref = refs[:8]
    count = len(groups)
    piece_refs = refs[8 : 8 + count]
    refs = refs[8 + count :]
    if not first:
        base_ref, refs = refs[0], refs[1:]
    out_ref, refs = refs[0], refs[1:]
    acc_ref = refs[0] if last else out_ref
    left_ref, buf_ref, sem_ref = refs[-3:]
    targets = k0_ref.shape[0]
    rows = buf_ref.shape[3]
    copies = {}
    for g, k in enumerate(groups):
        start = pl.multiple_of((lax.axis_index("patch") ^ k) * rows, block) if rows < k0_ref.shape[1] else 0
        for d, k_ref in enumerate((k0_ref, k1_ref)):
            copies[g, d] = pltpu.make_async_copy(
                k_ref.at[:, pl.ds(start, rows), :], buf_ref.at[g, d], sem_ref.at[g, d]
            )
            copies[g, d].start()
    for g, (k, piece_ref) in enumerate(zip(groups, piece_refs)):
        load_piece(k, piece_ref, (before_ref, after_ref), left_ref.at[g], scale, block, local=True)
    if not first:
        acc_ref[...] = base_ref[...]
    unit = 2 if targets % 2 == 0 else 1
    for g in range(count):
        for d in range(2):
            copies[g, d].wait()

            def body(n, carry, g=g, d=d):
                right = jnp.concatenate([buf_ref[g, d, n * unit + u] for u in range(unit)], 1)
                lanes = pl.ds(pl.multiple_of(n * (unit * block), unit * block), unit * block)
                part = jnp.dot(left_ref[g, d], right, preferred_element_type=F32)
                acc_ref[d, :, lanes] = part if first and g == 0 else acc_ref[d, :, lanes] + part
                return carry

            lax.fori_loop(0, targets // unit, body, 0)
    if last:
        half = out_ref.shape[0] // 2

        def store(d, value):
            out_ref[d * half : (d + 1) * half] = value

        finish(acc_ref, inc_ref, (fore_ref[...], back_ref[...]), ends_ref, store)


def call_sweep(groups, block, scale, before, after, inc, fore, back, ends, k0, k1, pieces, base, last):
    channels, rows = inc.shape
    targets = k0.shape[0]
    depth = 2 * pieces[0].shape[1]
    vmem = pl.BlockSpec(memory_space=pltpu.VMEM)
    table = pl.BlockSpec(memory_space=pl.ANY)
    extra = [] if base is None else [base]
    sums = jax.ShapeDtypeStruct((2, channels, rows), F32)
    return pl.pallas_call(
        functools.partial(sweep_kernel, groups, block, scale, base is None, last),
        out_shape=jax.ShapeDtypeStruct(inc.shape, BF) if last else sums,
        in_specs=[vmem] * 6 + [table] * 2 + [vmem] * (len(pieces) + len(extra)),
        out_specs=vmem,
        scratch_shapes=([pltpu.VMEM(sums.shape, F32)] if last else [])
        + [
            pltpu.VMEM((len(groups), 2, channels, depth), BF),
            pltpu.VMEM((len(groups), 2, targets, depth, block), BF),
            pltpu.SemaphoreType.DMA((len(groups), 2)),
        ],
        cost_estimate=pl.CostEstimate(
            flops=4 * len(groups) * channels * rows * depth,
            bytes_accessed=4 * len(groups) * rows * depth,
            transcendentals=0,
        ),
        compiler_params=pltpu.CompilerParams(vmem_limit_bytes=ROOMY),
        name="sweep" if last else "own_sweep",
    )(before, after, inc, fore, back, ends, k0, k1, *pieces, *extra)


def join_kernel(top_ref, bottom_ref, out_ref):
    half = out_ref.shape[0] // 2
    out_ref[:half] = top_ref[:half].astype(BF)
    out_ref[half:] = bottom_ref[:half].astype(BF)


def join(top, bottom, channels):
    vmem = pl.BlockSpec(memory_space=pltpu.VMEM)
    return pl.pallas_call(
        join_kernel,
        out_shape=jax.ShapeDtypeStruct((channels, top.shape[1]), BF),
        in_specs=[vmem] * 2,
        out_specs=vmem,
        compiler_params=pltpu.CompilerParams(vmem_limit_bytes=4 * 2**20),
        name="join",
    )(top, bottom)


def shift(value, step):
    count = lax.axis_size("seg")
    return lax.ppermute(value, "seg", [(i, i + step) for i in range(count) if 0 <= i + step < count])


def gather_patches(value):
    count = lax.axis_size("patch")
    if count not in (1, 2, 4):
        return [lax.all_gather(value, "patch", axis=1, tiled=True)]
    return [value] + [
        lax.ppermute(value, "patch", [(i, i ^ k) for i in range(count)]) for k in range(1, count)
    ]


def on_device(incident, wall_axial, wall_angle, wall_area, visibility, end_reflection):
    channels = incident.shape[1]
    patches = wall_axial.shape[1]
    block = patches // visibility.shape[3]
    half = channels // 2
    per_chunk = min(8, patches // block)
    scale = KAPPA / math.sqrt(patches)
    inc = incident[0]
    up, down, lists = call_prep(per_chunk, wall_axial, wall_angle, wall_area, inc, visibility)
    before, after = shift(up, 1), shift(down, -1)
    pieces = gather_patches(join(before, after, channels))
    k0 = call_build(0, block, per_chunk, half, lists, up, before, patches)
    k1, fore, back = call_build_sweep(
        block, per_chunk, scale, patches, lists, up, before, after, inc, end_reflection, k0, pieces
    )
    for sweep in range(1, ITERS):
        pieces = gather_patches(join(shift(fore, 1), shift(back, -1), channels))
        groups = tuple(range(len(pieces)))
        common = (block, scale, before, after, inc, fore, back, end_reflection, k0, k1)
        base = None
        if len(groups) > 1:
            base = call_sweep(groups[:1], *common, pieces[:1], None, False)
            groups, pieces = groups[1:], pieces[1:]
        state = call_sweep(groups, *common, pieces, base, True)
        if sweep + 1 < ITERS:
            fore, back = state[:half], state[half:]
    return state[None]


def solution(mesh):
    return jax.shard_map(
        on_device,
        mesh=mesh,
        in_specs=(
            P("seg", None, "patch"),
            P("seg", None),
            P("seg", None),
            P("seg", None),
            P("seg", None, "patch", None),
            P(),
        ),
        out_specs=P("seg", None, "patch"),
        check_vma=False,
    )
```

```python
import functools
import math

import jax
import jax.numpy as jnp
from jax import lax
from jax.experimental import pallas as pl
from jax.experimental.pallas import tpu as pltpu
from jax.sharding import PartitionSpec as P

ITERS = 2

WAVENUMBER = 40.0
RADIUS = 0.5
SOFTENING = 0.25

KAPPA = WAVENUMBER / (2.0 * math.pi)
HALF_CHORD = 2.0 * RADIUS * RADIUS * KAPPA * KAPPA
SINE = tuple(
    value * (1.0 - 5e-7)
    for value in (4.442867903112522, -7.307443423342558, 3.5947880930735288, -0.7843740618048793)
)
SINE_HALF = (0.999999976589841, -0.16666647634617332, 0.00833289982302485, -0.00019800897745117133,
             2.5904884686762915e-06)
COSINE_HALF = (0.9999999997806504, -0.4999999935847076, 0.04166663625803946, -0.0013888361399933481,
               2.476016133696864e-05, -2.605149496508554e-07)

FEATURES = 32
ROOMY = 50 * 2**20
PAIR = 8
BF = jnp.bfloat16
F32 = jnp.float32


def leading(x):
    wide = x * 65537.0
    return wide - (wide - x)


def split3(x):
    high = leading(x)
    rest = x - high
    mid = leading(rest)
    return high, mid, rest - mid


def near_side(geo, direction):
    return (geo[0:1] if direction == 0 else 1.0 - geo[0:1]) * KAPPA


def far_side(geo, direction):
    return (1.0 - geo[0:1] if direction == 0 else geo[0:1]) * KAPPA


def pad_rows(rows):
    width = rows[0].shape[1]
    rows = rows + [jnp.zeros((FEATURES - len(rows), width), F32)]
    return jnp.concatenate(rows, 0)


def target_features(geo, direction):
    u = near_side(geo, direction)
    one = jnp.ones_like(u)
    rows = list(split3(u * u + HALF_CHORD)) + [one, one, one]
    for value in (2.0 * u, -HALF_CHORD * geo[1:2], -HALF_CHORD * geo[2:3]):
        h, m, l = split3(value)
        rows += [h, h, m, m, h, l]
    return pad_rows(rows)


def source_features(geo, direction):
    v = far_side(geo, direction)
    one = jnp.ones_like(v)
    rows = [one, one, one] + list(split3(v * v))
    for value in (v, geo[1:2], geo[2:3]):
        h, m, l = split3(value)
        rows += [h, m, h, m, l, h]
    return pad_rows(rows)


def horner(coefs, x):
    total = coefs[-1]
    for coef in coefs[-2::-1]:
        total = total * x + coef
    return total


def exact_dot(a, b):
    return jnp.dot(a.astype(BF), b.astype(BF), preferred_element_type=F32)


def make_lists(lit, per_chunk):
    targets, sources = lit.shape
    chunks = sources // per_chunk
    size = per_chunk * targets
    i0 = lax.broadcasted_iota(jnp.int32, (sources, sources), 0)
    i1 = lax.broadcasted_iota(jnp.int32, (sources, sources), 1)
    same = i0 // per_chunk == i1 // per_chunk
    above = lax.broadcasted_iota(jnp.int32, (targets, targets), 0) > lax.broadcasted_iota(
        jnp.int32, (targets, targets), 1
    )
    sums = exact_dot(lit, jnp.where(same, 1.0, 0.0))
    rank = exact_dot(lit, jnp.where(same & (i0 < i1), 1.0, 0.0)) + exact_dot(
        jnp.where(above, 1.0, 0.0), sums
    )
    src = lax.broadcasted_iota(jnp.int32, lit.shape, 1) % per_chunk
    tgt = lax.broadcasted_iota(jnp.int32, lit.shape, 0)
    order = (tgt * per_chunk + src).astype(F32)
    place = jnp.where(lit > 0.5, rank, size - 1 - (order - rank))
    code = (src * targets + tgt).astype(F32)
    slot = lax.broadcasted_iota(jnp.int32, (size, sources), 0).astype(F32)
    found = jnp.zeros((size, sources), F32)
    for t in range(targets):
        found += jnp.where(slot == place[t : t + 1], code[t : t + 1], 0.0)
    c0 = lax.broadcasted_iota(jnp.int32, (sources, chunks), 0)
    c1 = lax.broadcasted_iota(jnp.int32, (sources, chunks), 1)
    pick = jnp.where(c0 // per_chunk == c1, 1.0, 0.0)
    codes = exact_dot(found, pick)
    counts = jnp.sum(exact_dot(lit, pick), axis=0, keepdims=True)
    return codes.astype(jnp.int32), counts.astype(jnp.int32)


def by_parity(even, odd):
    is_odd = lax.rem(lax.axis_index("seg"), 2) == 1
    wide = [x.astype(F32) for x in (even, odd)]
    pair = jnp.where(is_odd, wide[1], wide[0]), jnp.where(is_odd, wide[0], wide[1])
    return tuple(x.astype(even.dtype) for x in pair)


def prep_kernel(per_chunk, axial_ref, angle_ref, area_ref, inc_ref, vis_ref, swap_ref, cross_ref, list_ref):
    rows = inc_ref.shape[1]
    channels = inc_ref.shape[0] // 2
    half = angle_ref[...] * 0.5
    square = half * half
    sine = horner(SINE_HALF, square) * half
    cosine = horner(COSINE_HALF, square)
    geo = [axial_ref[...], 1.0 - 2.0 * sine * sine, 2.0 * sine * cosine, area_ref[...]]
    for j in range(axial_ref.shape[1] // rows):
        part = jnp.concatenate([g[:, j * rows : (j + 1) * rows] for g in geo], 0)
        swap_ref[channels + 4 * j : channels + 4 * j + 4] = part
        cross_ref[channels + 4 * j : channels + 4 * j + 4] = part
    fore, back = inc_ref[:channels].astype(F32), inc_ref[channels:].astype(F32)
    swap_ref[:channels], cross_ref[:channels] = by_parity(fore, back)
    for d in range(2):
        codes, counts = make_lists(vis_ref[0, d].astype(F32), per_chunk)
        list_ref[d, : codes.shape[0]] = codes
        list_ref[d, codes.shape[0] :] = jnp.broadcast_to(counts, (8, counts.shape[1]))


def call_prep(per_chunk, axial, angle, area, inc, visibility):
    targets, sources = visibility.shape[2], visibility.shape[3]
    channels = inc.shape[0] // 2
    rows, patches = inc.shape[1], axial.shape[1]
    pack = jax.ShapeDtypeStruct((channels + 4 * (patches // rows), rows), F32)
    vmem = pl.BlockSpec(memory_space=pltpu.VMEM)
    axial, angle, area, inc, visibility = [
        pltpu.with_memory_space_constraint(x, pltpu.HBM) for x in (axial, angle, area, inc, visibility)
    ]
    return pl.pallas_call(
        functools.partial(prep_kernel, per_chunk),
        out_shape=(
            pack, pack,
            jax.ShapeDtypeStruct((2, per_chunk * targets + 8, sources // per_chunk), jnp.int32),
        ),
        in_specs=[vmem] * 5,
        out_specs=[vmem] * 3,
        compiler_params=pltpu.CompilerParams(vmem_limit_bytes=ROOMY),
        name="prep",
    )(axial, angle, area, inc, visibility)


def table_block(q):
    q = jnp.maximum(q, 1e-12)
    turns = q * lax.rsqrt(q)
    f = turns - jnp.round(turns)
    mag = lax.rsqrt(q + SOFTENING * KAPPA * KAPPA)
    s = horner(SINE, f * f) * f
    rest = 2.0 - s * s
    both = mag * rest
    real = both - mag
    imag = (s * both) * lax.rsqrt(rest)
    return real.astype(BF), imag.astype(BF)


def build_chunk(direction, chunk, block, targets, list_ref, tf_ref, sf_ref, base, k_ref, q_ref):
    size = list_ref.shape[1] - 8
    count = list_ref[direction, size, chunk]

    def block_of(n):
        code = list_ref[direction, jnp.maximum(jnp.minimum(n, count - 1), 0), chunk]
        return lax.div(code, jnp.int32(targets)), lax.rem(code, jnp.int32(targets))

    def distances(group, q_ref):
        for u in range(PAIR):
            src, tgt = block_of(group * PAIR + u)
            cols = pl.ds(pl.multiple_of(tgt * block, block), block)
            feats = sf_ref[pl.ds(pl.multiple_of(base + src * block, block), block), :]
            q_ref[u * block : (u + 1) * block] = jnp.dot(feats, tf_ref[:, cols], preferred_element_type=F32)

    def entries(group, q_ref):
        for u in range(PAIR):
            src, tgt = block_of(group * PAIR + u)
            top = pl.multiple_of(src * (2 * block), 2 * block)
            part = 32
            for h in range(0, block, part):
                real, imag = table_block(q_ref[u * block + h : u * block + h + part])
                k_ref[tgt, pl.ds(pl.multiple_of(top + h, part), part), :] = real
                k_ref[tgt, pl.ds(pl.multiple_of(top + block + h, part), part), :] = imag

    def body(step, carry):
        distances(step, q_ref)
        entries(step, q_ref)
        return carry

    lax.fori_loop(0, lax.div(count + PAIR - 1, jnp.int32(PAIR)), body, 0)

    def clear(n, carry):
        code = list_ref[direction, n, chunk]
        src, tgt = lax.div(code, jnp.int32(targets)), lax.rem(code, jnp.int32(targets))
        rows = pl.ds(pl.multiple_of(src * (2 * block), 2 * block), 2 * block)
        k_ref[tgt, rows, :] = jnp.zeros((2 * block, block), BF)
        return carry

    lax.fori_loop(count, size, clear, 0)


def quarters(pack_ref, channels):
    return [pack_ref[r : r + 4] for r in range(channels, pack_ref.shape[0], 4)]


def pick(parts, index):
    chosen = parts[0]
    for j in range(1, len(parts)):
        chosen = jnp.where(index == j, parts[j], chosen)
    return chosen


def build_features(direction, channels, own_ref, pack_ref, tf_ref, sf_ref):
    rows = own_ref.shape[1]
    own = pick(quarters(own_ref, channels), lax.axis_index("patch"))
    tf_ref[...] = target_features(own, direction).astype(BF)
    for j, geo in enumerate(quarters(pack_ref, 0)):
        sf_ref[j * rows : (j + 1) * rows] = source_features(geo, direction).T.astype(BF)


def build_kernel(direction, block, per_chunk, channels, list_ref, own_ref, pack_ref, k_ref, tf_ref, sf_ref, *q):
    chunk = pl.program_id(0)

    @pl.when(chunk == 0)
    def _():
        build_features(direction, channels, own_ref, pack_ref, tf_ref, sf_ref)

    build_chunk(
        direction, chunk, block, k_ref.shape[0], list_ref, tf_ref, sf_ref, chunk * (per_chunk * block), k_ref, *q
    )


def whole(x):
    return pl.BlockSpec(x.shape, lambda c: (0,) * x.ndim)


def table_spec(targets, chunk_rows, block):
    return pl.BlockSpec((targets, chunk_rows, block), lambda c: (0, c, 0))


def call_build(direction, block, per_chunk, channels, lists, own, pack, patches):
    rows = own.shape[1]
    targets = rows // block
    chunk_rows = 2 * block * per_chunk
    return pl.pallas_call(
        functools.partial(build_kernel, direction, block, per_chunk, channels),
        grid=(patches // (block * per_chunk),),
        out_shape=jax.ShapeDtypeStruct((targets, 2 * patches, block), BF),
        in_specs=[pl.BlockSpec(memory_space=pltpu.SMEM), whole(own), whole(pack)],
        out_specs=table_spec(targets, chunk_rows, block),
        scratch_shapes=[
            pltpu.VMEM((FEATURES, rows), BF),
            pltpu.VMEM((patches, FEATURES), BF),
            pltpu.VMEM((PAIR * block, block), F32),
        ],
        compiler_params=pltpu.CompilerParams(dimension_semantics=("arbitrary",), vmem_limit_bytes=ROOMY),
        name=f"build{direction}",
    )(lists, own, pack)


def load_piece(k, piece_ref, packs, left_ref, scale, block, local=False):
    channels = piece_ref.shape[0] // 2
    half = channels // 2
    width = piece_ref.shape[1]
    gathered = width != packs[0].shape[1]
    group = lax.axis_index("patch") ^ k
    for d, pack_ref in enumerate(packs):
        areas = [pack_ref[r + 3 : r + 4] for r in range(0, pack_ref.shape[0], 4)]
        area = jnp.concatenate(areas, 1) if gathered else pick(areas, group)
        area = area * scale
        for n in range(width // block):
            cur = piece_ref[d * channels : (d + 1) * channels, n * block : (n + 1) * block].astype(F32)
            cur = cur * area[:, n * block : (n + 1) * block]
            high = leading(cur)
            low = (cur - high).astype(BF)
            high = high.astype(BF)
            a = jnp.concatenate([high, low], 0)
            b = jnp.concatenate([high[half:], -high[:half], low[half:], -low[:half]], 0)
            start = n * block if gathered or local else group * width + n * block
            top = pl.multiple_of(2 * start, 2 * block)
            left_ref[d, :, pl.ds(top, block)] = a
            left_ref[d, :, pl.ds(pl.multiple_of(top + block, block), block)] = b


def finish(acc_ref, inc_ref, prev, ends_ref, store):
    channels = inc_ref.shape[0] // 2
    half = channels // 2
    seg = lax.axis_index("seg")
    diagonal = lax.broadcasted_iota(jnp.int32, (channels, channels), 0) == lax.broadcasted_iota(
        jnp.int32, (channels, channels), 1
    )
    for d, end in enumerate((0, lax.axis_size("seg") - 1)):
        total = acc_ref[d, :channels] + acc_ref[d, channels:]
        other = prev[1 - d].astype(F32)
        flag = jnp.where(seg == end, 1.0, 0.0)
        coef = jnp.sum(jnp.where(diagonal, ends_ref[d : d + 1] * flag, 0.0), axis=1, keepdims=True)
        cre = coef[:half]
        cim = coef[half:]
        mirrored = jnp.concatenate(
            [cre * other[:half] - cim * other[half:], cre * other[half:] + cim * other[:half]], 0
        )
        rows = slice(d * channels, (d + 1) * channels)
        store(d, (inc_ref[rows].astype(F32) + total + mirrored).astype(BF))


def accumulate(acc_ref, left_ref, chunk, k_refs):
    targets, rows, block = k_refs[1].shape
    cols = pl.ds(pl.multiple_of(chunk * rows, rows), rows)
    group = 2 if targets % 2 == 0 else 1

    def body(n, carry):
        lanes = pl.ds(pl.multiple_of(n * (group * block), group * block), group * block)
        for d, k_ref in k_refs.items():
            right = jnp.concatenate([k_ref[n * group + g] for g in range(group)], 1)
            part = jnp.dot(left_ref[d, :, cols], right, preferred_element_type=F32)
            acc_ref[d, :, lanes] = jnp.where(chunk == 0, part, acc_ref[d, :, lanes] + part)
        return carry

    lax.fori_loop(0, targets // group, body, 0)


def build_sweep_kernel(
    block, per_chunk, pieces, scale, list_ref, own_ref, before_ref, after_ref, inc_ref, ends_ref, k0_ref, *rest
):
    piece_refs = rest[:pieces]
    k1_ref, fore_ref, back_ref, tf_ref, sf_ref, left_ref, acc_ref, q_ref = rest[pieces : pieces + 8]
    in_ref, k_ref, in_sem, out_sem = rest[pieces + 8 :]
    chunk = pl.program_id(0)
    chunks = pl.num_programs(0)
    channels = inc_ref.shape[0] // 2
    rows = in_ref.shape[2]
    slot = lax.rem(chunk, 2)

    def fetch(c, place):
        part = k0_ref.at[:, pl.ds(pl.multiple_of(c * rows, rows), rows), :]
        return pltpu.make_async_copy(part, in_ref.at[place], in_sem.at[place])

    def send(c, place):
        part = k1_ref.at[:, pl.ds(pl.multiple_of(c * rows, rows), rows), :]
        return pltpu.make_async_copy(k_ref.at[place], part, out_sem.at[place])

    @pl.when(chunk == 0)
    def _():
        fetch(chunk, slot).start()

    @pl.when(chunk + 1 < chunks)
    def _():
        fetch(chunk + 1, 1 - slot).start()

    @pl.when(chunk == 0)
    def _():
        build_features(1, channels, own_ref, after_ref, tf_ref, sf_ref)
        for k, piece_ref in enumerate(piece_refs):
            load_piece(k, piece_ref, (before_ref, after_ref), left_ref, scale, block)

    @pl.when(chunk >= 2)
    def _():
        send(chunk - 2, slot).wait()

    build_chunk(
        1, chunk, block, in_ref.shape[1], list_ref, tf_ref, sf_ref, chunk * (per_chunk * block),
        k_ref.at[slot], q_ref,
    )
    send(chunk, slot).start()
    fetch(chunk, slot).wait()
    accumulate(acc_ref, left_ref, chunk, {0: in_ref.at[slot], 1: k_ref.at[slot]})

    @pl.when(chunk == chunks - 1)
    def _():
        state = {}
        finish(acc_ref, inc_ref, (inc_ref[:channels], inc_ref[channels:]), ends_ref, state.__setitem__)
        fore_ref[...], back_ref[...] = by_parity(state[0], state[1])
        send(chunk, slot).wait()

    @pl.when((chunk == chunks - 1) & (chunk >= 1))
    def _():
        send(chunk - 1, 1 - slot).wait()


def call_build_sweep(block, per_chunk, scale, patches, lists, own, before, after, inc, ends, k0, pieces):
    rows = inc.shape[1]
    chunk_rows = 2 * block * per_chunk
    targets = rows // block
    channels = inc.shape[0]
    part = jax.ShapeDtypeStruct((channels // 2, rows), BF)
    table = pl.BlockSpec(memory_space=pl.ANY)
    return pl.pallas_call(
        functools.partial(build_sweep_kernel, block, per_chunk, len(pieces), scale),
        grid=(patches // (block * per_chunk),),
        out_shape=(jax.ShapeDtypeStruct(k0.shape, BF), part, part),
        in_specs=[pl.BlockSpec(memory_space=pltpu.SMEM), whole(own), whole(before), whole(after), whole(inc),
                  whole(ends), table] + [whole(p) for p in pieces],
        out_specs=(table, whole(part), whole(part)),
        scratch_shapes=[
            pltpu.VMEM((FEATURES, rows), BF),
            pltpu.VMEM((patches, FEATURES), BF),
            pltpu.VMEM((2, channels, 2 * patches), BF),
            pltpu.VMEM((2, channels, rows), F32),
            pltpu.VMEM((PAIR * block, block), F32),
            pltpu.VMEM((2, targets, chunk_rows, block), BF),
            pltpu.VMEM((2, targets, chunk_rows, block), BF),
            pltpu.SemaphoreType.DMA((2,)),
            pltpu.SemaphoreType.DMA((2,)),
        ],
        compiler_params=pltpu.CompilerParams(dimension_semantics=("arbitrary",), vmem_limit_bytes=ROOMY),
        name="build_sweep",
    )(lists, own, before, after, inc, ends, k0, *pieces)


def sweep_kernel(groups, block, scale, first, last, *refs):
    before_ref, after_ref, inc_ref, fore_ref, back_ref, ends_ref, k0_ref, k1_ref = refs[:8]
    count = len(groups)
    piece_refs = refs[8 : 8 + count]
    refs = refs[8 + count :]
    if not first:
        base_ref, refs = refs[0], refs[1:]
    out_ref, refs = refs[0], refs[1:]
    acc_ref = refs[0] if last else out_ref
    left_ref, buf_ref, sem_ref = refs[-3:]
    targets = k0_ref.shape[0]
    rows = buf_ref.shape[3]
    copies = {}
    for g, k in enumerate(groups):
        start = pl.multiple_of((lax.axis_index("patch") ^ k) * rows, block) if rows < k0_ref.shape[1] else 0
        for d, k_ref in enumerate((k0_ref, k1_ref)):
            copies[g, d] = pltpu.make_async_copy(
                k_ref.at[:, pl.ds(start, rows), :], buf_ref.at[g, d], sem_ref.at[g, d]
            )
            copies[g, d].start()
    for g, (k, piece_ref) in enumerate(zip(groups, piece_refs)):
        load_piece(k, piece_ref, (before_ref, after_ref), left_ref.at[g], scale, block, local=True)
    if not first:
        acc_ref[...] = base_ref[...]
    unit = 2 if targets % 2 == 0 else 1
    for g in range(count):
        for d in range(2):
            copies[g, d].wait()

            def body(n, carry, g=g, d=d):
                right = jnp.concatenate([buf_ref[g, d, n * unit + u] for u in range(unit)], 1)
                lanes = pl.ds(pl.multiple_of(n * (unit * block), unit * block), unit * block)
                part = jnp.dot(left_ref[g, d], right, preferred_element_type=F32)
                acc_ref[d, :, lanes] = part if first and g == 0 else acc_ref[d, :, lanes] + part
                return carry

            lax.fori_loop(0, targets // unit, body, 0)
    if last:
        half = out_ref.shape[0] // 2

        def store(d, value):
            out_ref[d * half : (d + 1) * half] = value

        finish(acc_ref, inc_ref, by_parity(fore_ref[...], back_ref[...]), ends_ref, store)


def call_sweep(groups, block, scale, before, after, inc, fore, back, ends, k0, k1, pieces, base, last):
    channels, rows = inc.shape
    targets = k0.shape[0]
    depth = 2 * pieces[0].shape[1]
    vmem = pl.BlockSpec(memory_space=pltpu.VMEM)
    table = pl.BlockSpec(memory_space=pl.ANY)
    extra = [] if base is None else [base]
    sums = jax.ShapeDtypeStruct((2, channels, rows), F32)
    return pl.pallas_call(
        functools.partial(sweep_kernel, groups, block, scale, base is None, last),
        out_shape=jax.ShapeDtypeStruct(inc.shape, BF) if last else sums,
        in_specs=[vmem] * 6 + [table] * 2 + [vmem] * (len(pieces) + len(extra)),
        out_specs=vmem,
        scratch_shapes=([pltpu.VMEM(sums.shape, F32)] if last else [])
        + [
            pltpu.VMEM((len(groups), 2, channels, depth), BF),
            pltpu.VMEM((len(groups), 2, targets, depth, block), BF),
            pltpu.SemaphoreType.DMA((len(groups), 2)),
        ],
        cost_estimate=pl.CostEstimate(
            flops=4 * len(groups) * channels * rows * depth,
            bytes_accessed=4 * len(groups) * rows * depth,
            transcendentals=0,
        ),
        compiler_params=pltpu.CompilerParams(vmem_limit_bytes=ROOMY),
        name="sweep" if last else "own_sweep",
    )(before, after, inc, fore, back, ends, k0, k1, *pieces, *extra)


def join_kernel(swap_ref, cross_ref, out_ref, *geo_refs):
    half = out_ref.shape[0] // 2
    after, before = by_parity(swap_ref[...], cross_ref[...])
    out_ref[:half] = before[:half].astype(BF)
    out_ref[half:] = after[:half].astype(BF)
    for ref, value in zip(geo_refs, (before, after)):
        ref[...] = value[half:]


def join(swapped, crossed, channels):
    vmem = pl.BlockSpec(memory_space=pltpu.VMEM)
    rows, width = swapped.shape
    geo = rows - channels // 2
    extra = [jax.ShapeDtypeStruct((geo, width), F32)] * 2 if geo else []
    return pl.pallas_call(
        join_kernel,
        out_shape=[jax.ShapeDtypeStruct((channels, width), BF)] + extra,
        in_specs=[vmem] * 2,
        out_specs=[vmem] * (1 + len(extra)),
        compiler_params=pltpu.CompilerParams(vmem_limit_bytes=4 * 2**20),
        name="join",
    )(swapped, crossed)


def neighbours(first, second):
    count = lax.axis_size("seg")
    moves = []
    for start in range(2):
        pairs = [(i, i + 1) for i in range(start, count - 1, 2)]
        moves.append(pairs + [(j, i) for i, j in pairs])
    return lax.ppermute(first, "seg", moves[0]), lax.ppermute(second, "seg", moves[1])


def gather_patches(value):
    count = lax.axis_size("patch")
    if count not in (1, 2, 4):
        return [lax.all_gather(value, "patch", axis=1, tiled=True)]
    return [value] + [
        lax.ppermute(value, "patch", [(i, i ^ k) for i in range(count)]) for k in range(1, count)
    ]


def on_device(incident, wall_axial, wall_angle, wall_area, visibility, end_reflection):
    channels = incident.shape[1]
    patches = wall_axial.shape[1]
    block = patches // visibility.shape[3]
    half = channels // 2
    per_chunk = min(8, patches // block)
    scale = KAPPA / math.sqrt(patches)
    inc = incident[0]
    own, other, lists = call_prep(per_chunk, wall_axial, wall_angle, wall_area, inc, visibility)
    moved, before, after = join(*neighbours(own, other), channels)
    pieces = gather_patches(moved)
    k0 = call_build(0, block, per_chunk, half, lists, own, before, patches)
    k1, first, second = call_build_sweep(
        block, per_chunk, scale, patches, lists, own, before, after, inc, end_reflection, k0, pieces
    )
    for sweep in range(1, ITERS):
        pieces = gather_patches(join(*neighbours(first, second), channels)[0])
        groups = tuple(range(len(pieces)))
        common = (block, scale, before, after, inc, first, second, end_reflection, k0, k1)
        base = None
        if len(groups) > 1:
            base = call_sweep(groups[:1], *common, pieces[:1], None, False)
            groups, pieces = groups[1:], pieces[1:]
        state = call_sweep(groups, *common, pieces, base, True)
        if sweep + 1 < ITERS:
            first, second = by_parity(state[:half], state[half:])
    return state[None]


def solution(mesh):
    return jax.shard_map(
        on_device,
        mesh=mesh,
        in_specs=(
            P("seg", None, "patch"),
            P("seg", None),
            P("seg", None),
            P("seg", None),
            P("seg", None, "patch", None),
            P(),
        ),
        out_specs=P("seg", None, "patch"),
        check_vma=False,
    )
```

```python
import functools
import math

import jax
import jax.numpy as jnp
from jax import lax
from jax.experimental import pallas as pl
from jax.experimental.pallas import tpu as pltpu
from jax.sharding import PartitionSpec as P

ITERS = 2

WAVENUMBER = 40.0
RADIUS = 0.5
SOFTENING = 0.25

KAPPA = WAVENUMBER / (2.0 * math.pi)
HALF_CHORD = 2.0 * RADIUS * RADIUS * KAPPA * KAPPA
SINE = tuple(
    value * (1.0 - 5e-7)
    for value in (4.442867903112522, -7.307443423342558, 3.5947880930735288, -0.7843740618048793)
)
SINE_HALF = (0.999999976589841, -0.16666647634617332, 0.00833289982302485, -0.00019800897745117133,
             2.5904884686762915e-06)
COSINE_HALF = (0.9999999997806504, -0.4999999935847076, 0.04166663625803946, -0.0013888361399933481,
               2.476016133696864e-05, -2.605149496508554e-07)

FEATURES = 32
ROOMY = 50 * 2**20
PAIR = 8
BF = jnp.bfloat16
F32 = jnp.float32


def leading(x):
    wide = x * 65537.0
    return wide - (wide - x)


def split3(x):
    high = leading(x)
    rest = x - high
    mid = leading(rest)
    return high, mid, rest - mid


def near_side(geo, direction):
    return (geo[0:1] if direction == 0 else 1.0 - geo[0:1]) * KAPPA


def far_side(geo, direction):
    return (1.0 - geo[0:1] if direction == 0 else geo[0:1]) * KAPPA


def pad_rows(rows):
    width = rows[0].shape[1]
    rows = rows + [jnp.zeros((FEATURES - len(rows), width), F32)]
    return jnp.concatenate(rows, 0)


def target_features(geo, direction):
    u = near_side(geo, direction)
    one = jnp.ones_like(u)
    rows = list(split3(u * u + HALF_CHORD)) + [one, one, one]
    for value in (2.0 * u, -HALF_CHORD * geo[1:2], -HALF_CHORD * geo[2:3]):
        h, m, l = split3(value)
        rows += [h, h, m, m, h, l]
    return pad_rows(rows)


def source_features(geo, direction):
    v = far_side(geo, direction)
    one = jnp.ones_like(v)
    rows = [one, one, one] + list(split3(v * v))
    for value in (v, geo[1:2], geo[2:3]):
        h, m, l = split3(value)
        rows += [h, m, h, m, l, h]
    return pad_rows(rows)


def horner(coefs, x):
    total = coefs[-1]
    for coef in coefs[-2::-1]:
        total = total * x + coef
    return total


def exact_dot(a, b):
    return jnp.dot(a.astype(BF), b.astype(BF), preferred_element_type=F32)


def make_lists(lit, per_chunk):
    targets, sources = lit.shape
    chunks = sources // per_chunk
    size = per_chunk * targets
    i0 = lax.broadcasted_iota(jnp.int32, (sources, sources), 0)
    i1 = lax.broadcasted_iota(jnp.int32, (sources, sources), 1)
    same = i0 // per_chunk == i1 // per_chunk
    above = lax.broadcasted_iota(jnp.int32, (targets, targets), 0) > lax.broadcasted_iota(
        jnp.int32, (targets, targets), 1
    )
    sums = exact_dot(lit, jnp.where(same, 1.0, 0.0))
    rank = exact_dot(lit, jnp.where(same & (i0 < i1), 1.0, 0.0)) + exact_dot(
        jnp.where(above, 1.0, 0.0), sums
    )
    src = lax.broadcasted_iota(jnp.int32, lit.shape, 1) % per_chunk
    tgt = lax.broadcasted_iota(jnp.int32, lit.shape, 0)
    order = (tgt * per_chunk + src).astype(F32)
    place = jnp.where(lit > 0.5, rank, size - 1 - (order - rank))
    code = (src * targets + tgt).astype(F32)
    slot = lax.broadcasted_iota(jnp.int32, (size, sources), 0).astype(F32)
    found = jnp.zeros((size, sources), F32)
    for t in range(targets):
        found += jnp.where(slot == place[t : t + 1], code[t : t + 1], 0.0)
    c0 = lax.broadcasted_iota(jnp.int32, (sources, chunks), 0)
    c1 = lax.broadcasted_iota(jnp.int32, (sources, chunks), 1)
    pick = jnp.where(c0 // per_chunk == c1, 1.0, 0.0)
    codes = exact_dot(found, pick)
    counts = jnp.sum(exact_dot(lit, pick), axis=0, keepdims=True)
    return codes.astype(jnp.int32), counts.astype(jnp.int32)


def by_parity(even, odd):
    is_odd = lax.rem(lax.axis_index("seg"), 2) == 1
    wide = [x.astype(F32) for x in (even, odd)]
    pair = jnp.where(is_odd, wide[1], wide[0]), jnp.where(is_odd, wide[0], wide[1])
    return tuple(x.astype(even.dtype) for x in pair)


def prep_kernel(per_chunk, axial_ref, angle_ref, area_ref, inc_ref, vis_ref, swap_ref, cross_ref, list_ref):
    rows = inc_ref.shape[1]
    channels = inc_ref.shape[0] // 2
    half = angle_ref[...] * 0.5
    square = half * half
    sine = horner(SINE_HALF, square) * half
    cosine = horner(COSINE_HALF, square)
    geo = [axial_ref[...], 1.0 - 2.0 * sine * sine, 2.0 * sine * cosine, area_ref[...]]
    for j in range(axial_ref.shape[1] // rows):
        part = jnp.concatenate([g[:, j * rows : (j + 1) * rows] for g in geo], 0)
        swap_ref[channels + 4 * j : channels + 4 * j + 4] = part
        cross_ref[channels + 4 * j : channels + 4 * j + 4] = part
    fore, back = inc_ref[:channels].astype(F32), inc_ref[channels:].astype(F32)
    swap_ref[:channels], cross_ref[:channels] = by_parity(fore, back)
    for d in range(2):
        codes, counts = make_lists(vis_ref[0, d].astype(F32), per_chunk)
        list_ref[d, : codes.shape[0]] = codes
        list_ref[d, codes.shape[0] :] = jnp.broadcast_to(counts, (8, counts.shape[1]))


def call_prep(per_chunk, axial, angle, area, inc, visibility):
    targets, sources = visibility.shape[2], visibility.shape[3]
    channels = inc.shape[0] // 2
    rows, patches = inc.shape[1], axial.shape[1]
    pack = jax.ShapeDtypeStruct((channels + 4 * (patches // rows), rows), F32)
    vmem = pl.BlockSpec(memory_space=pltpu.VMEM)
    axial, angle, area, inc, visibility = [
        pltpu.with_memory_space_constraint(x, pltpu.HBM) for x in (axial, angle, area, inc, visibility)
    ]
    return pl.pallas_call(
        functools.partial(prep_kernel, per_chunk),
        out_shape=(
            pack, pack,
            jax.ShapeDtypeStruct((2, per_chunk * targets + 8, sources // per_chunk), jnp.int32),
        ),
        in_specs=[vmem] * 5,
        out_specs=[vmem] * 3,
        compiler_params=pltpu.CompilerParams(vmem_limit_bytes=ROOMY),
        name="prep",
    )(axial, angle, area, inc, visibility)


def table_block(q):
    q = jnp.maximum(q, 1e-12)
    turns = q * lax.rsqrt(q)
    f = turns - jnp.round(turns)
    mag = lax.rsqrt(q + SOFTENING * KAPPA * KAPPA)
    s = horner(SINE, f * f) * f
    rest = 2.0 - s * s
    both = mag * rest
    real = both - mag
    imag = (s * both) * lax.rsqrt(rest)
    return real.astype(BF), imag.astype(BF)


def build_chunk(direction, chunk, block, targets, list_ref, tf_ref, sf_ref, base, k_ref, q_ref):
    size = list_ref.shape[1] - 8
    count = list_ref[direction, size, chunk]

    def block_of(n):
        code = list_ref[direction, jnp.maximum(jnp.minimum(n, count - 1), 0), chunk]
        return lax.div(code, jnp.int32(targets)), lax.rem(code, jnp.int32(targets))

    def distances(group, q_ref):
        for u in range(PAIR):
            src, tgt = block_of(group * PAIR + u)
            cols = pl.ds(pl.multiple_of(tgt * block, block), block)
            feats = sf_ref[pl.ds(pl.multiple_of(base + src * block, block), block), :]
            q_ref[u * block : (u + 1) * block] = jnp.dot(feats, tf_ref[:, cols], preferred_element_type=F32)

    def entries(group, q_ref):
        for u in range(PAIR):
            src, tgt = block_of(group * PAIR + u)
            top = pl.multiple_of(src * (2 * block), 2 * block)
            part = 32
            for h in range(0, block, part):
                real, imag = table_block(q_ref[u * block + h : u * block + h + part])
                k_ref[tgt, pl.ds(pl.multiple_of(top + h, part), part), :] = real
                k_ref[tgt, pl.ds(pl.multiple_of(top + block + h, part), part), :] = imag

    def body(step, carry):
        distances(step, q_ref)
        entries(step, q_ref)
        return carry

    lax.fori_loop(0, lax.div(count + PAIR - 1, jnp.int32(PAIR)), body, 0)

    def clear(n, carry):
        code = list_ref[direction, n, chunk]
        src, tgt = lax.div(code, jnp.int32(targets)), lax.rem(code, jnp.int32(targets))
        rows = pl.ds(pl.multiple_of(src * (2 * block), 2 * block), 2 * block)
        k_ref[tgt, rows, :] = jnp.zeros((2 * block, block), BF)
        return carry

    lax.fori_loop(count, size, clear, 0)


def quarters(pack_ref, channels):
    return [pack_ref[r : r + 4] for r in range(channels, pack_ref.shape[0], 4)]


def pick(parts, index):
    chosen = parts[0]
    for j in range(1, len(parts)):
        chosen = jnp.where(index == j, parts[j], chosen)
    return chosen


def build_features(direction, channels, own_ref, pack_ref, tf_ref, sf_ref):
    rows = own_ref.shape[1]
    own = pick(quarters(own_ref, channels), lax.axis_index("patch"))
    tf_ref[...] = target_features(own, direction).astype(BF)
    for j, geo in enumerate(quarters(pack_ref, 0)):
        sf_ref[j * rows : (j + 1) * rows] = source_features(geo, direction).T.astype(BF)


def build_kernel(direction, block, per_chunk, channels, list_ref, own_ref, pack_ref, k_ref, tf_ref, sf_ref, *q):
    chunk = pl.program_id(0)

    @pl.when(chunk == 0)
    def _():
        build_features(direction, channels, own_ref, pack_ref, tf_ref, sf_ref)

    build_chunk(
        direction, chunk, block, k_ref.shape[0], list_ref, tf_ref, sf_ref, chunk * (per_chunk * block), k_ref, *q
    )


def whole(x):
    return pl.BlockSpec(x.shape, lambda c: (0,) * x.ndim)


def table_spec(targets, chunk_rows, block):
    return pl.BlockSpec((targets, chunk_rows, block), lambda c: (0, c, 0))


def call_build(direction, block, per_chunk, channels, lists, own, pack, patches):
    rows = own.shape[1]
    targets = rows // block
    chunk_rows = 2 * block * per_chunk
    return pl.pallas_call(
        functools.partial(build_kernel, direction, block, per_chunk, channels),
        grid=(patches // (block * per_chunk),),
        out_shape=jax.ShapeDtypeStruct((targets, 2 * patches, block), BF),
        in_specs=[pl.BlockSpec(memory_space=pltpu.SMEM), whole(own), whole(pack)],
        out_specs=table_spec(targets, chunk_rows, block),
        scratch_shapes=[
            pltpu.VMEM((FEATURES, rows), BF),
            pltpu.VMEM((patches, FEATURES), BF),
            pltpu.VMEM((PAIR * block, block), F32),
        ],
        compiler_params=pltpu.CompilerParams(dimension_semantics=("arbitrary",), vmem_limit_bytes=ROOMY),
        name=f"build{direction}",
    )(lists, own, pack)


def load_piece(k, piece_ref, packs, left_ref, scale, block, local=False):
    channels = piece_ref.shape[0] // 2
    half = channels // 2
    width = piece_ref.shape[1]
    gathered = width != packs[0].shape[1]
    group = lax.axis_index("patch") ^ k
    for d, pack_ref in enumerate(packs):
        areas = [pack_ref[r + 3 : r + 4] for r in range(0, pack_ref.shape[0], 4)]
        area = jnp.concatenate(areas, 1) if gathered else pick(areas, group)
        area = area * scale
        for n in range(width // block):
            cur = piece_ref[d * channels : (d + 1) * channels, n * block : (n + 1) * block].astype(F32)
            cur = cur * area[:, n * block : (n + 1) * block]
            high = leading(cur)
            low = (cur - high).astype(BF)
            high = high.astype(BF)
            a = jnp.concatenate([high, low], 0)
            b = jnp.concatenate([high[half:], -high[:half], low[half:], -low[:half]], 0)
            start = n * block if gathered or local else group * width + n * block
            top = pl.multiple_of(2 * start, 2 * block)
            left_ref[d, :, pl.ds(top, block)] = a
            left_ref[d, :, pl.ds(pl.multiple_of(top + block, block), block)] = b


def finish(acc_ref, inc_ref, prev, ends_ref, store):
    channels = inc_ref.shape[0] // 2
    half = channels // 2
    seg = lax.axis_index("seg")
    diagonal = lax.broadcasted_iota(jnp.int32, (channels, channels), 0) == lax.broadcasted_iota(
        jnp.int32, (channels, channels), 1
    )
    for d, end in enumerate((0, lax.axis_size("seg") - 1)):
        total = acc_ref[d, :channels] + acc_ref[d, channels:]
        other = prev[1 - d].astype(F32)
        flag = jnp.where(seg == end, 1.0, 0.0)
        coef = jnp.sum(jnp.where(diagonal, ends_ref[d : d + 1] * flag, 0.0), axis=1, keepdims=True)
        cre = coef[:half]
        cim = coef[half:]
        mirrored = jnp.concatenate(
            [cre * other[:half] - cim * other[half:], cre * other[half:] + cim * other[:half]], 0
        )
        rows = slice(d * channels, (d + 1) * channels)
        store(d, (inc_ref[rows].astype(F32) + total + mirrored).astype(BF))


def accumulate(acc_ref, left_ref, chunk, k_refs):
    targets, rows, block = k_refs[1].shape
    cols = pl.ds(pl.multiple_of(chunk * rows, rows), rows)
    group = 2 if targets % 2 == 0 else 1

    def body(n, carry):
        lanes = pl.ds(pl.multiple_of(n * (group * block), group * block), group * block)
        for d, k_ref in k_refs.items():
            right = jnp.concatenate([k_ref[n * group + g] for g in range(group)], 1)
            part = jnp.dot(left_ref[d, :, cols], right, preferred_element_type=F32)
            acc_ref[d, :, lanes] = jnp.where(chunk == 0, part, acc_ref[d, :, lanes] + part)
        return carry

    lax.fori_loop(0, targets // group, body, 0)


def build_sweep_kernel(
    block, per_chunk, pieces, scale, list_ref, own_ref, before_ref, after_ref, inc_ref, ends_ref, k0_ref, *rest
):
    piece_refs = rest[:pieces]
    k1_ref, fore_ref, back_ref, tf_ref, sf_ref, left_ref, acc_ref, q_ref = rest[pieces : pieces + 8]
    in_ref, in_sem = rest[pieces + 8 :]
    chunk = pl.program_id(0)
    chunks = pl.num_programs(0)
    channels = inc_ref.shape[0] // 2
    rows = in_ref.shape[2]
    slot = lax.rem(chunk, 2)

    def fetch(c, place):
        part = k0_ref.at[:, pl.ds(pl.multiple_of(c * rows, rows), rows), :]
        return pltpu.make_async_copy(part, in_ref.at[place], in_sem.at[place])

    k_ref = k1_ref.at[:, pl.ds(pl.multiple_of(chunk * rows, rows), rows), :]

    @pl.when(chunk == 0)
    def _():
        fetch(chunk, slot).start()

    @pl.when(chunk + 1 < chunks)
    def _():
        fetch(chunk + 1, 1 - slot).start()

    @pl.when(chunk == 0)
    def _():
        build_features(1, channels, own_ref, after_ref, tf_ref, sf_ref)
        for k, piece_ref in enumerate(piece_refs):
            load_piece(k, piece_ref, (before_ref, after_ref), left_ref, scale, block)

    build_chunk(
        1, chunk, block, in_ref.shape[1], list_ref, tf_ref, sf_ref, chunk * (per_chunk * block),
        k_ref, q_ref,
    )
    fetch(chunk, slot).wait()
    accumulate(acc_ref, left_ref, chunk, {0: in_ref.at[slot], 1: k_ref})

    @pl.when(chunk == chunks - 1)
    def _():
        state = {}
        finish(acc_ref, inc_ref, (inc_ref[:channels], inc_ref[channels:]), ends_ref, state.__setitem__)
        fore_ref[...], back_ref[...] = by_parity(state[0], state[1])


def call_build_sweep(block, per_chunk, scale, patches, lists, own, before, after, inc, ends, k0, pieces):
    rows = inc.shape[1]
    chunk_rows = 2 * block * per_chunk
    targets = rows // block
    channels = inc.shape[0]
    part = jax.ShapeDtypeStruct((channels // 2, rows), BF)
    k0 = pltpu.with_memory_space_constraint(k0, pltpu.HBM)
    table = pl.BlockSpec(memory_space=pl.ANY)
    return pl.pallas_call(
        functools.partial(build_sweep_kernel, block, per_chunk, len(pieces), scale),
        grid=(patches // (block * per_chunk),),
        out_shape=(pltpu.VMEM(k0.shape, BF), part, part),
        in_specs=[pl.BlockSpec(memory_space=pltpu.SMEM), whole(own), whole(before), whole(after), whole(inc),
                  whole(ends), table] + [whole(p) for p in pieces],
        out_specs=(pl.BlockSpec(memory_space=pltpu.VMEM), whole(part), whole(part)),
        scratch_shapes=[
            pltpu.VMEM((FEATURES, rows), BF),
            pltpu.VMEM((patches, FEATURES), BF),
            pltpu.VMEM((2, channels, 2 * patches), BF),
            pltpu.VMEM((2, channels, rows), F32),
            pltpu.VMEM((PAIR * block, block), F32),
            pltpu.VMEM((2, targets, chunk_rows, block), BF),
            pltpu.SemaphoreType.DMA((2,)),
        ],
        compiler_params=pltpu.CompilerParams(dimension_semantics=("arbitrary",), vmem_limit_bytes=24 * 2**20),
        name="build_sweep",
    )(lists, own, before, after, inc, ends, k0, *pieces)


def sweep_kernel(groups, block, scale, first, last, *refs):
    before_ref, after_ref, inc_ref, fore_ref, back_ref, ends_ref, k0_ref, k1_ref = refs[:8]
    count = len(groups)
    piece_refs = refs[8 : 8 + count]
    refs = refs[8 + count :]
    if not first:
        base_ref, refs = refs[0], refs[1:]
    out_ref, refs = refs[0], refs[1:]
    acc_ref = refs[0] if last else out_ref
    left_ref, buf_ref, sem_ref = refs[-3:]
    targets = k0_ref.shape[0]
    rows = buf_ref.shape[2]
    copies, starts = {}, []
    for g, k in enumerate(groups):
        start = pl.multiple_of((lax.axis_index("patch") ^ k) * rows, block) if rows < k0_ref.shape[1] else 0
        starts.append(start)
        for d, k_ref in enumerate((k0_ref,)):
            copies[g, d] = pltpu.make_async_copy(
                k_ref.at[:, pl.ds(start, rows), :], buf_ref.at[g], sem_ref.at[g]
            )
            copies[g, d].start()
    for g, (k, piece_ref) in enumerate(zip(groups, piece_refs)):
        load_piece(k, piece_ref, (before_ref, after_ref), left_ref.at[g], scale, block, local=True)
    if not first:
        acc_ref[...] = base_ref[...]
    unit = 2 if targets % 2 == 0 else 1
    for d in (1, 0):
        for g in range(count):
            if d == 0:
                copies[g, d].wait()

            def body(n, carry, g=g, d=d):
                if d == 0:
                    parts = [buf_ref[g, n * unit + u] for u in range(unit)]
                else:
                    parts = [k1_ref[n * unit + u, pl.ds(starts[g], rows), :] for u in range(unit)]
                right = jnp.concatenate(parts, 1)
                lanes = pl.ds(pl.multiple_of(n * (unit * block), unit * block), unit * block)
                part = jnp.dot(left_ref[g, d], right, preferred_element_type=F32)
                acc_ref[d, :, lanes] = part if first and g == 0 else acc_ref[d, :, lanes] + part
                return carry

            lax.fori_loop(0, targets // unit, body, 0)
    if last:
        half = out_ref.shape[0] // 2

        def store(d, value):
            out_ref[d * half : (d + 1) * half] = value

        finish(acc_ref, inc_ref, by_parity(fore_ref[...], back_ref[...]), ends_ref, store)


def call_sweep(groups, block, scale, before, after, inc, fore, back, ends, k0, k1, pieces, base, last):
    channels, rows = inc.shape
    targets = k0.shape[0]
    depth = 2 * pieces[0].shape[1]
    k0 = pltpu.with_memory_space_constraint(k0, pltpu.HBM)
    k1 = pltpu.with_memory_space_constraint(k1, pltpu.VMEM)
    vmem = pl.BlockSpec(memory_space=pltpu.VMEM)
    table = pl.BlockSpec(memory_space=pl.ANY)
    extra = [] if base is None else [base]
    sums = jax.ShapeDtypeStruct((2, channels, rows), F32)
    return pl.pallas_call(
        functools.partial(sweep_kernel, groups, block, scale, base is None, last),
        out_shape=jax.ShapeDtypeStruct(inc.shape, BF) if last else sums,
        in_specs=[vmem] * 6 + [table, vmem] + [vmem] * (len(pieces) + len(extra)),
        out_specs=vmem,
        scratch_shapes=([pltpu.VMEM(sums.shape, F32)] if last else [])
        + [
            pltpu.VMEM((len(groups), 2, channels, depth), BF),
            pltpu.VMEM((len(groups), targets, depth, block), BF),
            pltpu.SemaphoreType.DMA((len(groups),)),
        ],
        cost_estimate=pl.CostEstimate(
            flops=4 * len(groups) * channels * rows * depth,
            bytes_accessed=4 * len(groups) * rows * depth,
            transcendentals=0,
        ),
        compiler_params=pltpu.CompilerParams(vmem_limit_bytes=24 * 2**20),
        name="sweep" if last else "own_sweep",
    )(before, after, inc, fore, back, ends, k0, k1, *pieces, *extra)


def join_kernel(swap_ref, cross_ref, out_ref, *geo_refs):
    half = out_ref.shape[0] // 2
    after, before = by_parity(swap_ref[...], cross_ref[...])
    out_ref[:half] = before[:half].astype(BF)
    out_ref[half:] = after[:half].astype(BF)
    for ref, value in zip(geo_refs, (before, after)):
        ref[...] = value[half:]


def join(swapped, crossed, channels):
    vmem = pl.BlockSpec(memory_space=pltpu.VMEM)
    rows, width = swapped.shape
    geo = rows - channels // 2
    extra = [jax.ShapeDtypeStruct((geo, width), F32)] * 2 if geo else []
    return pl.pallas_call(
        join_kernel,
        out_shape=[jax.ShapeDtypeStruct((channels, width), BF)] + extra,
        in_specs=[vmem] * 2,
        out_specs=[vmem] * (1 + len(extra)),
        compiler_params=pltpu.CompilerParams(vmem_limit_bytes=4 * 2**20),
        name="join",
    )(swapped, crossed)


def neighbours(first, second):
    count = lax.axis_size("seg")
    moves = []
    for start in range(2):
        pairs = [(i, i + 1) for i in range(start, count - 1, 2)]
        moves.append(pairs + [(j, i) for i, j in pairs])
    return lax.ppermute(first, "seg", moves[0]), lax.ppermute(second, "seg", moves[1])


def gather_patches(value):
    count = lax.axis_size("patch")
    if count not in (1, 2, 4):
        return [lax.all_gather(value, "patch", axis=1, tiled=True)]
    return [value] + [
        lax.ppermute(value, "patch", [(i, i ^ k) for i in range(count)]) for k in range(1, count)
    ]


def on_device(incident, wall_axial, wall_angle, wall_area, visibility, end_reflection):
    channels = incident.shape[1]
    patches = wall_axial.shape[1]
    block = patches // visibility.shape[3]
    half = channels // 2
    per_chunk = min(8, patches // block)
    scale = KAPPA / math.sqrt(patches)
    inc = incident[0]
    own, other, lists = call_prep(per_chunk, wall_axial, wall_angle, wall_area, inc, visibility)
    moved, before, after = join(*neighbours(own, other), channels)
    pieces = gather_patches(moved)
    k0 = call_build(0, block, per_chunk, half, lists, own, before, patches)
    k1, first, second = call_build_sweep(
        block, per_chunk, scale, patches, lists, own, before, after, inc, end_reflection, k0, pieces
    )
    for sweep in range(1, ITERS):
        pieces = gather_patches(join(*neighbours(first, second), channels)[0])
        groups = tuple(range(len(pieces)))
        common = (block, scale, before, after, inc, first, second, end_reflection, k0, k1)
        base = None
        if len(groups) > 1:
            base = call_sweep(groups[:1], *common, pieces[:1], None, False)
            groups, pieces = groups[1:], pieces[1:]
        state = call_sweep(groups, *common, pieces, base, True)
        if sweep + 1 < ITERS:
            first, second = by_parity(state[:half], state[half:])
    return state[None]


def solution(mesh):
    return jax.shard_map(
        on_device,
        mesh=mesh,
        in_specs=(
            P("seg", None, "patch"),
            P("seg", None),
            P("seg", None),
            P("seg", None),
            P("seg", None, "patch", None),
            P(),
        ),
        out_specs=P("seg", None, "patch"),
        check_vma=False,
    )
```

```python
import functools
import math

import jax
import jax.numpy as jnp
from jax import lax
from jax.experimental import pallas as pl
from jax.experimental.pallas import tpu as pltpu
from jax.sharding import PartitionSpec as P

ITERS = 2

WAVENUMBER = 40.0
RADIUS = 0.5
SOFTENING = 0.25

KAPPA = WAVENUMBER / (2.0 * math.pi)
HALF_CHORD = 2.0 * RADIUS * RADIUS * KAPPA * KAPPA
SINE = tuple(
    value * (1.0 - 5e-7)
    for value in (4.442867903112522, -7.307443423342558, 3.5947880930735288, -0.7843740618048793)
)
SINE_HALF = (0.999999976589841, -0.16666647634617332, 0.00833289982302485, -0.00019800897745117133,
             2.5904884686762915e-06)
COSINE_HALF = (0.9999999997806504, -0.4999999935847076, 0.04166663625803946, -0.0013888361399933481,
               2.476016133696864e-05, -2.605149496508554e-07)

FEATURES = 32
ROOMY = 12 * 2**20
PAIR = 8
BF = jnp.bfloat16
F32 = jnp.float32


def leading(x):
    wide = x * 65537.0
    return wide - (wide - x)


def split3(x):
    high = leading(x)
    rest = x - high
    mid = leading(rest)
    return high, mid, rest - mid


def near_side(geo, direction):
    return (geo[0:1] if direction == 0 else 1.0 - geo[0:1]) * KAPPA


def far_side(geo, direction):
    return (1.0 - geo[0:1] if direction == 0 else geo[0:1]) * KAPPA


def pad_rows(rows):
    width = rows[0].shape[1]
    rows = rows + [jnp.zeros((FEATURES - len(rows), width), F32)]
    return jnp.concatenate(rows, 0)


def target_features(geo, direction):
    u = near_side(geo, direction)
    one = jnp.ones_like(u)
    rows = list(split3(u * u + HALF_CHORD)) + [one, one, one]
    for value in (2.0 * u, -HALF_CHORD * geo[1:2], -HALF_CHORD * geo[2:3]):
        h, m, l = split3(value)
        rows += [h, h, m, m, h, l]
    return pad_rows(rows)


def source_features(geo, direction):
    v = far_side(geo, direction)
    one = jnp.ones_like(v)
    rows = [one, one, one] + list(split3(v * v))
    for value in (v, geo[1:2], geo[2:3]):
        h, m, l = split3(value)
        rows += [h, m, h, m, l, h]
    return pad_rows(rows)


def horner(coefs, x):
    total = coefs[-1]
    for coef in coefs[-2::-1]:
        total = total * x + coef
    return total


def exact_dot(a, b):
    return jnp.dot(a.astype(BF), b.astype(BF), preferred_element_type=F32)


def make_lists(lit, per_chunk):
    targets, sources = lit.shape
    chunks = sources // per_chunk
    size = per_chunk * targets
    i0 = lax.broadcasted_iota(jnp.int32, (sources, sources), 0)
    i1 = lax.broadcasted_iota(jnp.int32, (sources, sources), 1)
    same = i0 // per_chunk == i1 // per_chunk
    above = lax.broadcasted_iota(jnp.int32, (targets, targets), 0) > lax.broadcasted_iota(
        jnp.int32, (targets, targets), 1
    )
    sums = exact_dot(lit, jnp.where(same, 1.0, 0.0))
    rank = exact_dot(lit, jnp.where(same & (i0 < i1), 1.0, 0.0)) + exact_dot(
        jnp.where(above, 1.0, 0.0), sums
    )
    src = lax.broadcasted_iota(jnp.int32, lit.shape, 1) % per_chunk
    tgt = lax.broadcasted_iota(jnp.int32, lit.shape, 0)
    order = (tgt * per_chunk + src).astype(F32)
    place = jnp.where(lit > 0.5, rank, size - 1 - (order - rank))
    code = (src * targets + tgt).astype(F32)
    slot = lax.broadcasted_iota(jnp.int32, (size, sources), 0).astype(F32)
    found = jnp.zeros((size, sources), F32)
    for t in range(targets):
        found += jnp.where(slot == place[t : t + 1], code[t : t + 1], 0.0)
    c0 = lax.broadcasted_iota(jnp.int32, (sources, chunks), 0)
    c1 = lax.broadcasted_iota(jnp.int32, (sources, chunks), 1)
    pick = jnp.where(c0 // per_chunk == c1, 1.0, 0.0)
    codes = exact_dot(found, pick)
    counts = jnp.sum(exact_dot(lit, pick), axis=0, keepdims=True)
    return codes.astype(jnp.int32), counts.astype(jnp.int32)


def by_parity(even, odd):
    is_odd = lax.rem(lax.axis_index("seg"), 2) == 1
    wide = [x.astype(F32) for x in (even, odd)]
    pair = jnp.where(is_odd, wide[1], wide[0]), jnp.where(is_odd, wide[0], wide[1])
    return tuple(x.astype(even.dtype) for x in pair)


def prep_kernel(per_chunk, axial_ref, angle_ref, area_ref, inc_ref, vis_ref, swap_ref, cross_ref, list_ref):
    rows = inc_ref.shape[1]
    channels = inc_ref.shape[0] // 2
    half = angle_ref[...] * 0.5
    square = half * half
    sine = horner(SINE_HALF, square) * half
    cosine = horner(COSINE_HALF, square)
    geo = [axial_ref[...], 1.0 - 2.0 * sine * sine, 2.0 * sine * cosine, area_ref[...]]
    for j in range(axial_ref.shape[1] // rows):
        part = jnp.concatenate([g[:, j * rows : (j + 1) * rows] for g in geo], 0)
        swap_ref[channels + 4 * j : channels + 4 * j + 4] = part
        cross_ref[channels + 4 * j : channels + 4 * j + 4] = part
    fore, back = inc_ref[:channels].astype(F32), inc_ref[channels:].astype(F32)
    swap_ref[:channels], cross_ref[:channels] = by_parity(fore, back)
    for d in range(2):
        codes, counts = make_lists(vis_ref[0, d].astype(F32), per_chunk)
        list_ref[d, : codes.shape[0]] = codes
        list_ref[d, codes.shape[0] :] = jnp.broadcast_to(counts, (8, counts.shape[1]))


def call_prep(per_chunk, axial, angle, area, inc, visibility):
    targets, sources = visibility.shape[2], visibility.shape[3]
    channels = inc.shape[0] // 2
    rows, patches = inc.shape[1], axial.shape[1]
    pack = jax.ShapeDtypeStruct((channels + 4 * (patches // rows), rows), F32)
    vmem = pl.BlockSpec(memory_space=pltpu.VMEM)
    axial, angle, area, inc, visibility = [
        pltpu.with_memory_space_constraint(x, pltpu.HBM) for x in (axial, angle, area, inc, visibility)
    ]
    return pl.pallas_call(
        functools.partial(prep_kernel, per_chunk),
        out_shape=(
            pack, pack,
            jax.ShapeDtypeStruct((2, per_chunk * targets + 8, sources // per_chunk), jnp.int32),
        ),
        in_specs=[vmem] * 5,
        out_specs=[vmem] * 3,
        compiler_params=pltpu.CompilerParams(vmem_limit_bytes=ROOMY),
        name="prep",
    )(axial, angle, area, inc, visibility)


def table_block(q):
    q = jnp.maximum(q, 1e-12)
    turns = q * lax.rsqrt(q)
    f = turns - jnp.round(turns)
    mag = lax.rsqrt(q + SOFTENING * KAPPA * KAPPA)
    s = horner(SINE, f * f) * f
    rest = 2.0 - s * s
    both = mag * rest
    real = both - mag
    imag = (s * both) * lax.rsqrt(rest)
    return real.astype(BF), imag.astype(BF)


def build_chunk(direction, chunk, block, targets, list_ref, tf_ref, sf_ref, base, k_ref, q_ref):
    size = list_ref.shape[1] - 8
    count = list_ref[direction, size, chunk]

    def block_of(n):
        code = list_ref[direction, jnp.maximum(jnp.minimum(n, count - 1), 0), chunk]
        return lax.div(code, jnp.int32(targets)), lax.rem(code, jnp.int32(targets))

    def distances(group, q_ref):
        for u in range(PAIR):
            src, tgt = block_of(group * PAIR + u)
            cols = pl.ds(pl.multiple_of(tgt * block, block), block)
            feats = sf_ref[pl.ds(pl.multiple_of(base + src * block, block), block), :]
            q_ref[u * block : (u + 1) * block] = jnp.dot(feats, tf_ref[:, cols], preferred_element_type=F32)

    def entries(group, q_ref):
        for u in range(PAIR):
            src, tgt = block_of(group * PAIR + u)
            top = pl.multiple_of(src * (2 * block), 2 * block)
            part = 32
            for h in range(0, block, part):
                real, imag = table_block(q_ref[u * block + h : u * block + h + part])
                k_ref[tgt, pl.ds(pl.multiple_of(top + h, part), part), :] = real
                k_ref[tgt, pl.ds(pl.multiple_of(top + block + h, part), part), :] = imag

    def body(step, carry):
        distances(step, q_ref)
        entries(step, q_ref)
        return carry

    lax.fori_loop(0, lax.div(count + PAIR - 1, jnp.int32(PAIR)), body, 0)

    def clear(n, carry):
        code = list_ref[direction, n, chunk]
        src, tgt = lax.div(code, jnp.int32(targets)), lax.rem(code, jnp.int32(targets))
        rows = pl.ds(pl.multiple_of(src * (2 * block), 2 * block), 2 * block)
        k_ref[tgt, rows, :] = jnp.zeros((2 * block, block), BF)
        return carry

    lax.fori_loop(count, size, clear, 0)


def quarters(pack_ref, channels):
    return [pack_ref[r : r + 4] for r in range(channels, pack_ref.shape[0], 4)]


def pick(parts, index):
    chosen = parts[0]
    for j in range(1, len(parts)):
        chosen = jnp.where(index == j, parts[j], chosen)
    return chosen


def build_features(direction, channels, own_ref, pack_ref, tf_ref, sf_ref):
    rows = own_ref.shape[1]
    own = pick(quarters(own_ref, channels), lax.axis_index("patch"))
    tf_ref[...] = target_features(own, direction).astype(BF)
    for j, geo in enumerate(quarters(pack_ref, 0)):
        sf_ref[j * rows : (j + 1) * rows] = source_features(geo, direction).T.astype(BF)


def build_kernel(direction, block, per_chunk, channels, list_ref, own_ref, pack_ref, k_ref, tf_ref, sf_ref, *q):
    chunk = pl.program_id(0)

    @pl.when(chunk == 0)
    def _():
        build_features(direction, channels, own_ref, pack_ref, tf_ref, sf_ref)

    build_chunk(
        direction, chunk, block, k_ref.shape[0], list_ref, tf_ref, sf_ref, chunk * (per_chunk * block),
        rows_of(k_ref, chunk, 2 * per_chunk * block), *q
    )


def rows_of(k_ref, chunk, rows):
    return k_ref.at[:, pl.ds(pl.multiple_of(chunk * rows, rows), rows), :]


def whole(x):
    return pl.BlockSpec(x.shape, lambda c: (0,) * x.ndim)


def table_spec(targets, chunk_rows, block):
    return pl.BlockSpec((targets, chunk_rows, block), lambda c: (0, c, 0))


def call_build(direction, block, per_chunk, channels, lists, own, pack, patches):
    rows = own.shape[1]
    targets = rows // block
    chunk_rows = 2 * block * per_chunk
    return pl.pallas_call(
        functools.partial(build_kernel, direction, block, per_chunk, channels),
        grid=(patches // (block * per_chunk),),
        out_shape=pltpu.VMEM((targets, 2 * patches, block), BF),
        in_specs=[pl.BlockSpec(memory_space=pltpu.SMEM), whole(own), whole(pack)],
        out_specs=pl.BlockSpec(memory_space=pltpu.VMEM),
        scratch_shapes=[
            pltpu.VMEM((FEATURES, rows), BF),
            pltpu.VMEM((patches, FEATURES), BF),
            pltpu.VMEM((PAIR * block, block), F32),
        ],
        compiler_params=pltpu.CompilerParams(dimension_semantics=("arbitrary",), vmem_limit_bytes=ROOMY),
        name=f"build{direction}",
    )(lists, own, pack)


def load_piece(k, piece_ref, packs, left_ref, scale, block, local=False):
    channels = piece_ref.shape[0] // 2
    half = channels // 2
    width = piece_ref.shape[1]
    gathered = width != packs[0].shape[1]
    group = lax.axis_index("patch") ^ k
    for d, pack_ref in enumerate(packs):
        areas = [pack_ref[r + 3 : r + 4] for r in range(0, pack_ref.shape[0], 4)]
        area = jnp.concatenate(areas, 1) if gathered else pick(areas, group)
        area = area * scale
        for n in range(width // block):
            cur = piece_ref[d * channels : (d + 1) * channels, n * block : (n + 1) * block].astype(F32)
            cur = cur * area[:, n * block : (n + 1) * block]
            high = leading(cur)
            low = (cur - high).astype(BF)
            high = high.astype(BF)
            a = jnp.concatenate([high, low], 0)
            b = jnp.concatenate([high[half:], -high[:half], low[half:], -low[:half]], 0)
            start = n * block if gathered or local else group * width + n * block
            top = pl.multiple_of(2 * start, 2 * block)
            left_ref[d, :, pl.ds(top, block)] = a
            left_ref[d, :, pl.ds(pl.multiple_of(top + block, block), block)] = b


def finish(acc_ref, inc_ref, prev, ends_ref, store):
    channels = inc_ref.shape[0] // 2
    half = channels // 2
    seg = lax.axis_index("seg")
    diagonal = lax.broadcasted_iota(jnp.int32, (channels, channels), 0) == lax.broadcasted_iota(
        jnp.int32, (channels, channels), 1
    )
    for d, end in enumerate((0, lax.axis_size("seg") - 1)):
        total = acc_ref[d, :channels] + acc_ref[d, channels:]
        other = prev[1 - d].astype(F32)
        flag = jnp.where(seg == end, 1.0, 0.0)
        coef = jnp.sum(jnp.where(diagonal, ends_ref[d : d + 1] * flag, 0.0), axis=1, keepdims=True)
        cre = coef[:half]
        cim = coef[half:]
        mirrored = jnp.concatenate(
            [cre * other[:half] - cim * other[half:], cre * other[half:] + cim * other[:half]], 0
        )
        rows = slice(d * channels, (d + 1) * channels)
        store(d, (inc_ref[rows].astype(F32) + total + mirrored).astype(BF))


def accumulate(acc_ref, left_ref, chunk, k_refs):
    targets, rows, block = k_refs[1].shape
    cols = pl.ds(pl.multiple_of(chunk * rows, rows), rows)
    group = 2 if targets % 2 == 0 else 1

    def body(n, carry):
        lanes = pl.ds(pl.multiple_of(n * (group * block), group * block), group * block)
        for d, k_ref in k_refs.items():
            right = jnp.concatenate([k_ref[n * group + g] for g in range(group)], 1)
            part = jnp.dot(left_ref[d, :, cols], right, preferred_element_type=F32)
            acc_ref[d, :, lanes] = jnp.where(chunk == 0, part, acc_ref[d, :, lanes] + part)
        return carry

    lax.fori_loop(0, targets // group, body, 0)


def build_sweep_kernel(
    block, per_chunk, pieces, scale, list_ref, own_ref, before_ref, after_ref, inc_ref, ends_ref, k0_ref, *rest
):
    piece_refs = rest[:pieces]
    k1_ref, kept_ref, fore_ref, back_ref, tf_ref, sf_ref, left_ref, acc_ref, q_ref, sem_ref = rest[pieces:]
    chunk = pl.program_id(0)
    chunks = pl.num_programs(0)
    channels = inc_ref.shape[0] // 2
    rows = 2 * per_chunk * block
    k_ref = rows_of(k1_ref, chunk, rows)
    keep = pltpu.make_async_copy(k0_ref, kept_ref, sem_ref)

    @pl.when(chunk == 0)
    def _():
        keep.start()

    @pl.when(chunk == 0)
    def _():
        build_features(1, channels, own_ref, after_ref, tf_ref, sf_ref)
        for k, piece_ref in enumerate(piece_refs):
            load_piece(k, piece_ref, (before_ref, after_ref), left_ref, scale, block)

    build_chunk(
        1, chunk, block, k1_ref.shape[0], list_ref, tf_ref, sf_ref, chunk * (per_chunk * block),
        k_ref, q_ref,
    )
    accumulate(acc_ref, left_ref, chunk, {0: rows_of(k0_ref, chunk, rows), 1: k_ref})

    @pl.when(chunk == chunks - 1)
    def _():
        state = {}
        finish(acc_ref, inc_ref, (inc_ref[:channels], inc_ref[channels:]), ends_ref, state.__setitem__)
        fore_ref[...], back_ref[...] = by_parity(state[0], state[1])
        keep.wait()


def call_build_sweep(block, per_chunk, scale, patches, lists, own, before, after, inc, ends, k0, pieces):
    rows = inc.shape[1]
    chunk_rows = 2 * block * per_chunk
    targets = rows // block
    channels = inc.shape[0]
    part = jax.ShapeDtypeStruct((channels // 2, rows), BF)
    k0 = pltpu.with_memory_space_constraint(k0, pltpu.VMEM)
    table = pl.BlockSpec(memory_space=pltpu.VMEM)
    return pl.pallas_call(
        functools.partial(build_sweep_kernel, block, per_chunk, len(pieces), scale),
        grid=(patches // (block * per_chunk),),
        out_shape=(pltpu.VMEM(k0.shape, BF), jax.ShapeDtypeStruct(k0.shape, BF), part, part),
        in_specs=[pl.BlockSpec(memory_space=pltpu.SMEM), whole(own), whole(before), whole(after), whole(inc),
                  whole(ends), table] + [whole(p) for p in pieces],
        out_specs=(table, pl.BlockSpec(memory_space=pl.ANY), whole(part), whole(part)),
        scratch_shapes=[
            pltpu.VMEM((FEATURES, rows), BF),
            pltpu.VMEM((patches, FEATURES), BF),
            pltpu.VMEM((2, channels, 2 * patches), BF),
            pltpu.VMEM((2, channels, rows), F32),
            pltpu.VMEM((PAIR * block, block), F32),
            pltpu.SemaphoreType.DMA,
        ],
        compiler_params=pltpu.CompilerParams(dimension_semantics=("arbitrary",), vmem_limit_bytes=12 * 2**20),
        name="build_sweep",
    )(lists, own, before, after, inc, ends, k0, *pieces)


def sweep_kernel(groups, block, scale, first, last, *refs):
    before_ref, after_ref, inc_ref, fore_ref, back_ref, ends_ref, k0_ref, k1_ref = refs[:8]
    count = len(groups)
    piece_refs = refs[8 : 8 + count]
    refs = refs[8 + count :]
    if not first:
        base_ref, refs = refs[0], refs[1:]
    out_ref, refs = refs[0], refs[1:]
    acc_ref = refs[0] if last else out_ref
    left_ref, buf_ref, sem_ref = refs[-3:]
    targets = k0_ref.shape[0]
    rows = buf_ref.shape[2]
    copies, starts = {}, []
    for g, k in enumerate(groups):
        start = pl.multiple_of((lax.axis_index("patch") ^ k) * rows, block) if rows < k0_ref.shape[1] else 0
        starts.append(start)
        for d, k_ref in enumerate((k0_ref,)):
            copies[g, d] = pltpu.make_async_copy(
                k_ref.at[:, pl.ds(start, rows), :], buf_ref.at[g], sem_ref.at[g]
            )
            copies[g, d].start()
    for g, (k, piece_ref) in enumerate(zip(groups, piece_refs)):
        load_piece(k, piece_ref, (before_ref, after_ref), left_ref.at[g], scale, block, local=True)
    if not first:
        acc_ref[...] = base_ref[...]
    unit = 2 if targets % 2 == 0 else 1
    for d in (1, 0):
        for g in range(count):
            if d == 0:
                copies[g, d].wait()

            def body(n, carry, g=g, d=d):
                if d == 0:
                    parts = [buf_ref[g, n * unit + u] for u in range(unit)]
                else:
                    parts = [k1_ref[n * unit + u, pl.ds(starts[g], rows), :] for u in range(unit)]
                right = jnp.concatenate(parts, 1)
                lanes = pl.ds(pl.multiple_of(n * (unit * block), unit * block), unit * block)
                part = jnp.dot(left_ref[g, d], right, preferred_element_type=F32)
                acc_ref[d, :, lanes] = part if first and g == 0 else acc_ref[d, :, lanes] + part
                return carry

            lax.fori_loop(0, targets // unit, body, 0)
    if last:
        half = out_ref.shape[0] // 2

        def store(d, value):
            out_ref[d * half : (d + 1) * half] = value

        finish(acc_ref, inc_ref, by_parity(fore_ref[...], back_ref[...]), ends_ref, store)


def call_sweep(groups, block, scale, before, after, inc, fore, back, ends, k0, k1, pieces, base, last):
    channels, rows = inc.shape
    targets = k0.shape[0]
    depth = 2 * pieces[0].shape[1]
    k0 = pltpu.with_memory_space_constraint(k0, pltpu.HBM)
    k1 = pltpu.with_memory_space_constraint(k1, pltpu.VMEM)
    vmem = pl.BlockSpec(memory_space=pltpu.VMEM)
    table = pl.BlockSpec(memory_space=pl.ANY)
    extra = [] if base is None else [base]
    sums = jax.ShapeDtypeStruct((2, channels, rows), F32)
    return pl.pallas_call(
        functools.partial(sweep_kernel, groups, block, scale, base is None, last),
        out_shape=jax.ShapeDtypeStruct(inc.shape, BF) if last else sums,
        in_specs=[vmem] * 6 + [table, vmem] + [vmem] * (len(pieces) + len(extra)),
        out_specs=vmem,
        scratch_shapes=([pltpu.VMEM(sums.shape, F32)] if last else [])
        + [
            pltpu.VMEM((len(groups), 2, channels, depth), BF),
            pltpu.VMEM((len(groups), targets, depth, block), BF),
            pltpu.SemaphoreType.DMA((len(groups),)),
        ],
        cost_estimate=pl.CostEstimate(
            flops=4 * len(groups) * channels * rows * depth,
            bytes_accessed=4 * len(groups) * rows * depth,
            transcendentals=0,
        ),
        compiler_params=pltpu.CompilerParams(vmem_limit_bytes=24 * 2**20),
        name="sweep" if last else "own_sweep",
    )(before, after, inc, fore, back, ends, k0, k1, *pieces, *extra)


def join_kernel(swap_ref, cross_ref, out_ref, *geo_refs):
    half = out_ref.shape[0] // 2
    after, before = by_parity(swap_ref[...], cross_ref[...])
    out_ref[:half] = before[:half].astype(BF)
    out_ref[half:] = after[:half].astype(BF)
    for ref, value in zip(geo_refs, (before, after)):
        ref[...] = value[half:]


def join(swapped, crossed, channels):
    vmem = pl.BlockSpec(memory_space=pltpu.VMEM)
    rows, width = swapped.shape
    geo = rows - channels // 2
    extra = [jax.ShapeDtypeStruct((geo, width), F32)] * 2 if geo else []
    return pl.pallas_call(
        join_kernel,
        out_shape=[jax.ShapeDtypeStruct((channels, width), BF)] + extra,
        in_specs=[vmem] * 2,
        out_specs=[vmem] * (1 + len(extra)),
        compiler_params=pltpu.CompilerParams(vmem_limit_bytes=4 * 2**20),
        name="join",
    )(swapped, crossed)


def neighbours(first, second):
    count = lax.axis_size("seg")
    moves = []
    for start in range(2):
        pairs = [(i, i + 1) for i in range(start, count - 1, 2)]
        moves.append(pairs + [(j, i) for i, j in pairs])
    return lax.ppermute(first, "seg", moves[0]), lax.ppermute(second, "seg", moves[1])


def gather_patches(value):
    count = lax.axis_size("patch")
    if count not in (1, 2, 4):
        return [lax.all_gather(value, "patch", axis=1, tiled=True)]
    return [value] + [
        lax.ppermute(value, "patch", [(i, i ^ k) for i in range(count)]) for k in range(1, count)
    ]


def on_device(incident, wall_axial, wall_angle, wall_area, visibility, end_reflection):
    channels = incident.shape[1]
    patches = wall_axial.shape[1]
    block = patches // visibility.shape[3]
    half = channels // 2
    per_chunk = min(8, patches // block)
    scale = KAPPA / math.sqrt(patches)
    inc = incident[0]
    own, other, lists = call_prep(per_chunk, wall_axial, wall_angle, wall_area, inc, visibility)
    moved, before, after = join(*neighbours(own, other), channels)
    pieces = gather_patches(moved)
    k0 = call_build(0, block, per_chunk, half, lists, own, before, patches)
    k1, k0, first, second = call_build_sweep(
        block, per_chunk, scale, patches, lists, own, before, after, inc, end_reflection, k0, pieces
    )
    for sweep in range(1, ITERS):
        pieces = gather_patches(join(*neighbours(first, second), channels)[0])
        groups = tuple(range(len(pieces)))
        common = (block, scale, before, after, inc, first, second, end_reflection, k0, k1)
        base = None
        if len(groups) > 1:
            base = call_sweep(groups[:1], *common, pieces[:1], None, False)
            groups, pieces = groups[1:], pieces[1:]
        state = call_sweep(groups, *common, pieces, base, True)
        if sweep + 1 < ITERS:
            first, second = by_parity(state[:half], state[half:])
    return state[None]


def solution(mesh):
    return jax.shard_map(
        on_device,
        mesh=mesh,
        in_specs=(
            P("seg", None, "patch"),
            P("seg", None),
            P("seg", None),
            P("seg", None),
            P("seg", None, "patch", None),
            P(),
        ),
        out_specs=P("seg", None, "patch"),
        check_vma=False,
    )
```

```python
import functools
import math

import jax
import jax.numpy as jnp
from jax import lax
from jax.experimental import pallas as pl
from jax.experimental.pallas import tpu as pltpu
from jax.sharding import PartitionSpec as P

ITERS = 2

WAVENUMBER = 40.0
RADIUS = 0.5
SOFTENING = 0.25

KAPPA = WAVENUMBER / (2.0 * math.pi)
HALF_CHORD = 2.0 * RADIUS * RADIUS * KAPPA * KAPPA
SINE = tuple(
    value * (1.0 - 5e-7)
    for value in (4.442867903112522, -7.307443423342558, 3.5947880930735288, -0.7843740618048793)
)
SINE_HALF = (0.999999976589841, -0.16666647634617332, 0.00833289982302485, -0.00019800897745117133,
             2.5904884686762915e-06)
COSINE_HALF = (0.9999999997806504, -0.4999999935847076, 0.04166663625803946, -0.0013888361399933481,
               2.476016133696864e-05, -2.605149496508554e-07)

FEATURES = 32
ROOMY = 12 * 2**20
PAIR = 8
BF = jnp.bfloat16
F32 = jnp.float32


def leading(x):
    wide = x * 65537.0
    return wide - (wide - x)


def split3(x):
    high = leading(x)
    rest = x - high
    mid = leading(rest)
    return high, mid, rest - mid


def near_side(geo, direction):
    return (geo[0:1] if direction == 0 else 1.0 - geo[0:1]) * KAPPA


def far_side(geo, direction):
    return (1.0 - geo[0:1] if direction == 0 else geo[0:1]) * KAPPA


def pad_rows(rows):
    width = rows[0].shape[1]
    rows = rows + [jnp.zeros((FEATURES - len(rows), width), F32)]
    return jnp.concatenate(rows, 0)


def target_features(geo, direction):
    u = near_side(geo, direction)
    one = jnp.ones_like(u)
    rows = list(split3(u * u + HALF_CHORD)) + [one, one, one]
    for value in (2.0 * u, -HALF_CHORD * geo[1:2], -HALF_CHORD * geo[2:3]):
        h, m, l = split3(value)
        rows += [h, h, m, m, h, l]
    return pad_rows(rows)


def source_features(geo, direction):
    v = far_side(geo, direction)
    one = jnp.ones_like(v)
    rows = [one, one, one] + list(split3(v * v))
    for value in (v, geo[1:2], geo[2:3]):
        h, m, l = split3(value)
        rows += [h, m, h, m, l, h]
    return pad_rows(rows)


def horner(coefs, x):
    total = coefs[-1]
    for coef in coefs[-2::-1]:
        total = total * x + coef
    return total


def exact_dot(a, b):
    return jnp.dot(a.astype(BF), b.astype(BF), preferred_element_type=F32)


def make_lists(lit, per_chunk):
    targets, sources = lit.shape
    chunks = sources // per_chunk
    size = per_chunk * targets
    i0 = lax.broadcasted_iota(jnp.int32, (sources, sources), 0)
    i1 = lax.broadcasted_iota(jnp.int32, (sources, sources), 1)
    same = i0 // per_chunk == i1 // per_chunk
    above = lax.broadcasted_iota(jnp.int32, (targets, targets), 0) > lax.broadcasted_iota(
        jnp.int32, (targets, targets), 1
    )
    sums = exact_dot(lit, jnp.where(same, 1.0, 0.0))
    rank = exact_dot(lit, jnp.where(same & (i0 < i1), 1.0, 0.0)) + exact_dot(
        jnp.where(above, 1.0, 0.0), sums
    )
    src = lax.broadcasted_iota(jnp.int32, lit.shape, 1) % per_chunk
    tgt = lax.broadcasted_iota(jnp.int32, lit.shape, 0)
    order = (tgt * per_chunk + src).astype(F32)
    place = jnp.where(lit > 0.5, rank, size - 1 - (order - rank))
    code = (src * targets + tgt).astype(F32)
    slot = lax.broadcasted_iota(jnp.int32, (size, sources), 0).astype(F32)
    found = jnp.zeros((size, sources), F32)
    for t in range(targets):
        found += jnp.where(slot == place[t : t + 1], code[t : t + 1], 0.0)
    c0 = lax.broadcasted_iota(jnp.int32, (sources, chunks), 0)
    c1 = lax.broadcasted_iota(jnp.int32, (sources, chunks), 1)
    pick = jnp.where(c0 // per_chunk == c1, 1.0, 0.0)
    codes = exact_dot(found, pick)
    counts = jnp.sum(exact_dot(lit, pick), axis=0, keepdims=True)
    return codes.astype(jnp.int32), counts.astype(jnp.int32)


def by_parity(even, odd):
    is_odd = lax.rem(lax.axis_index("seg"), 2) == 1
    wide = [x.astype(F32) for x in (even, odd)]
    pair = jnp.where(is_odd, wide[1], wide[0]), jnp.where(is_odd, wide[0], wide[1])
    return tuple(x.astype(even.dtype) for x in pair)


def prep_kernel(per_chunk, axial_ref, angle_ref, area_ref, inc_ref, vis_ref, swap_ref, cross_ref, list_ref):
    rows = inc_ref.shape[1]
    channels = inc_ref.shape[0] // 2
    half = angle_ref[...] * 0.5
    square = half * half
    sine = horner(SINE_HALF, square) * half
    cosine = horner(COSINE_HALF, square)
    geo = [axial_ref[...], 1.0 - 2.0 * sine * sine, 2.0 * sine * cosine, area_ref[...]]
    for j in range(axial_ref.shape[1] // rows):
        part = jnp.concatenate([g[:, j * rows : (j + 1) * rows] for g in geo], 0)
        swap_ref[channels + 4 * j : channels + 4 * j + 4] = part
        cross_ref[channels + 4 * j : channels + 4 * j + 4] = part
    fore, back = inc_ref[:channels].astype(F32), inc_ref[channels:].astype(F32)
    swap_ref[:channels], cross_ref[:channels] = by_parity(fore, back)
    for d in range(2):
        codes, counts = make_lists(vis_ref[0, d].astype(F32), per_chunk)
        list_ref[d, : codes.shape[0]] = codes
        list_ref[d, codes.shape[0] :] = jnp.broadcast_to(counts, (8, counts.shape[1]))


def call_prep(per_chunk, axial, angle, area, inc, visibility):
    targets, sources = visibility.shape[2], visibility.shape[3]
    channels = inc.shape[0] // 2
    rows, patches = inc.shape[1], axial.shape[1]
    pack = jax.ShapeDtypeStruct((channels + 4 * (patches // rows), rows), F32)
    vmem = pl.BlockSpec(memory_space=pltpu.VMEM)
    axial, angle, area, inc, visibility = [
        pltpu.with_memory_space_constraint(x, pltpu.HBM) for x in (axial, angle, area, inc, visibility)
    ]
    return pl.pallas_call(
        functools.partial(prep_kernel, per_chunk),
        out_shape=(
            pack, pack,
            jax.ShapeDtypeStruct((2, per_chunk * targets + 8, sources // per_chunk), jnp.int32),
        ),
        in_specs=[vmem] * 5,
        out_specs=[vmem] * 3,
        compiler_params=pltpu.CompilerParams(vmem_limit_bytes=ROOMY),
        name="prep",
    )(axial, angle, area, inc, visibility)


def table_block(q):
    q = jnp.maximum(q, 1e-12)
    turns = q * lax.rsqrt(q)
    f = turns - jnp.round(turns)
    mag = lax.rsqrt(q + SOFTENING * KAPPA * KAPPA)
    s = horner(SINE, f * f) * f
    rest = 2.0 - s * s
    both = mag * rest
    real = both - mag
    imag = (s * both) * lax.rsqrt(rest)
    return real.astype(BF), imag.astype(BF)


def build_chunk(direction, chunk, block, targets, list_ref, tf_ref, sf_ref, base, k_ref, q_ref):
    size = list_ref.shape[1] - 8
    count = list_ref[direction, size, chunk]

    def block_of(n):
        code = list_ref[direction, jnp.maximum(jnp.minimum(n, count - 1), 0), chunk]
        return lax.div(code, jnp.int32(targets)), lax.rem(code, jnp.int32(targets))

    def distances(group, q_ref):
        for u in range(PAIR):
            src, tgt = block_of(group * PAIR + u)
            cols = pl.ds(pl.multiple_of(tgt * block, block), block)
            feats = sf_ref[pl.ds(pl.multiple_of(base + src * block, block), block), :]
            q_ref[u * block : (u + 1) * block] = jnp.dot(feats, tf_ref[:, cols], preferred_element_type=F32)

    def entries(group, q_ref):
        for u in range(PAIR):
            src, tgt = block_of(group * PAIR + u)
            top = pl.multiple_of(src * (2 * block), 2 * block)
            part = 32
            for h in range(0, block, part):
                real, imag = table_block(q_ref[u * block + h : u * block + h + part])
                k_ref[tgt, pl.ds(pl.multiple_of(top + h, part), part), :] = real
                k_ref[tgt, pl.ds(pl.multiple_of(top + block + h, part), part), :] = imag

    def body(step, carry):
        distances(step, q_ref)
        entries(step, q_ref)
        return carry

    lax.fori_loop(0, lax.div(count + PAIR - 1, jnp.int32(PAIR)), body, 0)

    def clear(n, carry):
        code = list_ref[direction, n, chunk]
        src, tgt = lax.div(code, jnp.int32(targets)), lax.rem(code, jnp.int32(targets))
        rows = pl.ds(pl.multiple_of(src * (2 * block), 2 * block), 2 * block)
        k_ref[tgt, rows, :] = jnp.zeros((2 * block, block), BF)
        return carry

    lax.fori_loop(count, size, clear, 0)


def quarters(pack_ref, channels):
    return [pack_ref[r : r + 4] for r in range(channels, pack_ref.shape[0], 4)]


def pick(parts, index):
    chosen = parts[0]
    for j in range(1, len(parts)):
        chosen = jnp.where(index == j, parts[j], chosen)
    return chosen


def build_features(direction, channels, own_ref, pack_ref, tf_ref, sf_ref):
    rows = own_ref.shape[1]
    own = pick(quarters(own_ref, channels), lax.axis_index("patch"))
    tf_ref[...] = target_features(own, direction).astype(BF)
    for j, geo in enumerate(quarters(pack_ref, 0)):
        sf_ref[j * rows : (j + 1) * rows] = source_features(geo, direction).T.astype(BF)


def build_kernel(direction, block, per_chunk, channels, list_ref, own_ref, pack_ref, k_ref, tf_ref, sf_ref, *q):
    chunk = pl.program_id(0)

    @pl.when(chunk == 0)
    def _():
        build_features(direction, channels, own_ref, pack_ref, tf_ref, sf_ref)

    build_chunk(
        direction, chunk, block, k_ref.shape[0], list_ref, tf_ref, sf_ref, chunk * (per_chunk * block),
        rows_of(k_ref, chunk, 2 * per_chunk * block), *q
    )


def rows_of(k_ref, chunk, rows):
    return k_ref.at[:, pl.ds(pl.multiple_of(chunk * rows, rows), rows), :]


def whole(x):
    return pl.BlockSpec(x.shape, lambda c: (0,) * x.ndim)


def table_spec(targets, chunk_rows, block):
    return pl.BlockSpec((targets, chunk_rows, block), lambda c: (0, c, 0))


def call_build(direction, block, per_chunk, channels, lists, own, pack, patches):
    rows = own.shape[1]
    targets = rows // block
    chunk_rows = 2 * block * per_chunk
    return pl.pallas_call(
        functools.partial(build_kernel, direction, block, per_chunk, channels),
        grid=(patches // (block * per_chunk),),
        out_shape=pltpu.VMEM((targets, 2 * patches, block), BF),
        in_specs=[pl.BlockSpec(memory_space=pltpu.SMEM), whole(own), whole(pack)],
        out_specs=pl.BlockSpec(memory_space=pltpu.VMEM),
        scratch_shapes=[
            pltpu.VMEM((FEATURES, rows), BF),
            pltpu.VMEM((patches, FEATURES), BF),
            pltpu.VMEM((PAIR * block, block), F32),
        ],
        compiler_params=pltpu.CompilerParams(dimension_semantics=("arbitrary",), vmem_limit_bytes=ROOMY),
        name=f"build{direction}",
    )(lists, own, pack)


def load_piece(k, piece_ref, packs, left_ref, scale, block, local=False):
    channels = piece_ref.shape[0] // 2
    half = channels // 2
    width = piece_ref.shape[1]
    gathered = width != packs[0].shape[1]
    group = lax.axis_index("patch") ^ k
    for d, pack_ref in enumerate(packs):
        areas = [pack_ref[r + 3 : r + 4] for r in range(0, pack_ref.shape[0], 4)]
        area = jnp.concatenate(areas, 1) if gathered else pick(areas, group)
        area = area * scale
        for n in range(width // block):
            cur = piece_ref[d * channels : (d + 1) * channels, n * block : (n + 1) * block].astype(F32)
            cur = cur * area[:, n * block : (n + 1) * block]
            high = leading(cur)
            low = (cur - high).astype(BF)
            high = high.astype(BF)
            a = jnp.concatenate([high, low], 0)
            b = jnp.concatenate([high[half:], -high[:half], low[half:], -low[:half]], 0)
            start = n * block if gathered or local else group * width + n * block
            top = pl.multiple_of(2 * start, 2 * block)
            left_ref[d, :, pl.ds(top, block)] = a
            left_ref[d, :, pl.ds(pl.multiple_of(top + block, block), block)] = b


def finish(acc_ref, inc_ref, prev, ends_ref, store):
    channels = inc_ref.shape[0] // 2
    half = channels // 2
    seg = lax.axis_index("seg")
    diagonal = lax.broadcasted_iota(jnp.int32, (channels, channels), 0) == lax.broadcasted_iota(
        jnp.int32, (channels, channels), 1
    )
    for d, end in enumerate((0, lax.axis_size("seg") - 1)):
        total = acc_ref[d, :channels] + acc_ref[d, channels:]
        other = prev[1 - d].astype(F32)
        flag = jnp.where(seg == end, 1.0, 0.0)
        coef = jnp.sum(jnp.where(diagonal, ends_ref[d : d + 1] * flag, 0.0), axis=1, keepdims=True)
        cre = coef[:half]
        cim = coef[half:]
        mirrored = jnp.concatenate(
            [cre * other[:half] - cim * other[half:], cre * other[half:] + cim * other[:half]], 0
        )
        rows = slice(d * channels, (d + 1) * channels)
        store(d, (inc_ref[rows].astype(F32) + total + mirrored).astype(BF))


def accumulate(acc_ref, left_ref, chunk, k_refs):
    targets, rows, block = k_refs[1].shape
    cols = pl.ds(pl.multiple_of(chunk * rows, rows), rows)
    group = 2 if targets % 2 == 0 else 1

    def body(n, carry):
        lanes = pl.ds(pl.multiple_of(n * (group * block), group * block), group * block)
        for d, k_ref in k_refs.items():
            right = jnp.concatenate([k_ref[n * group + g] for g in range(group)], 1)
            part = jnp.dot(left_ref[d, :, cols], right, preferred_element_type=F32)
            acc_ref[d, :, lanes] = jnp.where(chunk == 0, part, acc_ref[d, :, lanes] + part)
        return carry

    lax.fori_loop(0, targets // group, body, 0, unroll=True)


def build_sweep_kernel(
    block, per_chunk, pieces, scale, list_ref, own_ref, before_ref, after_ref, inc_ref, ends_ref, k0_ref, *rest
):
    piece_refs = rest[:pieces]
    k1_ref, kept_ref, fore_ref, back_ref, tf_ref, sf_ref, left_ref, acc_ref, q_ref, sem_ref = rest[pieces:]
    chunk = pl.program_id(0)
    chunks = pl.num_programs(0)
    channels = inc_ref.shape[0] // 2
    rows = 2 * per_chunk * block
    k_ref = rows_of(k1_ref, chunk, rows)
    keep = pltpu.make_async_copy(k0_ref, kept_ref, sem_ref)

    @pl.when(chunk == 0)
    def _():
        keep.start()

    @pl.when(chunk == 0)
    def _():
        build_features(1, channels, own_ref, after_ref, tf_ref, sf_ref)
        for k, piece_ref in enumerate(piece_refs):
            load_piece(k, piece_ref, (before_ref, after_ref), left_ref, scale, block)

    build_chunk(
        1, chunk, block, k1_ref.shape[0], list_ref, tf_ref, sf_ref, chunk * (per_chunk * block),
        k_ref, q_ref,
    )
    accumulate(acc_ref, left_ref, chunk, {0: rows_of(k0_ref, chunk, rows), 1: k_ref})

    @pl.when(chunk == chunks - 1)
    def _():
        state = {}
        finish(acc_ref, inc_ref, (inc_ref[:channels], inc_ref[channels:]), ends_ref, state.__setitem__)
        fore_ref[...], back_ref[...] = by_parity(state[0], state[1])
        keep.wait()


def call_build_sweep(block, per_chunk, scale, patches, lists, own, before, after, inc, ends, k0, pieces):
    rows = inc.shape[1]
    chunk_rows = 2 * block * per_chunk
    targets = rows // block
    channels = inc.shape[0]
    part = jax.ShapeDtypeStruct((channels // 2, rows), BF)
    k0 = pltpu.with_memory_space_constraint(k0, pltpu.VMEM)
    table = pl.BlockSpec(memory_space=pltpu.VMEM)
    return pl.pallas_call(
        functools.partial(build_sweep_kernel, block, per_chunk, len(pieces), scale),
        grid=(patches // (block * per_chunk),),
        out_shape=(pltpu.VMEM(k0.shape, BF), jax.ShapeDtypeStruct(k0.shape, BF), part, part),
        in_specs=[pl.BlockSpec(memory_space=pltpu.SMEM), whole(own), whole(before), whole(after), whole(inc),
                  whole(ends), table] + [whole(p) for p in pieces],
        out_specs=(table, pl.BlockSpec(memory_space=pl.ANY), whole(part), whole(part)),
        scratch_shapes=[
            pltpu.VMEM((FEATURES, rows), BF),
            pltpu.VMEM((patches, FEATURES), BF),
            pltpu.VMEM((2, channels, 2 * patches), BF),
            pltpu.VMEM((2, channels, rows), F32),
            pltpu.VMEM((PAIR * block, block), F32),
            pltpu.SemaphoreType.DMA,
        ],
        compiler_params=pltpu.CompilerParams(dimension_semantics=("arbitrary",), vmem_limit_bytes=12 * 2**20),
        name="build_sweep",
    )(lists, own, before, after, inc, ends, k0, *pieces)


def sweep_kernel(groups, block, scale, first, last, *refs):
    before_ref, after_ref, inc_ref, fore_ref, back_ref, ends_ref, k0_ref, k1_ref = refs[:8]
    count = len(groups)
    piece_refs = refs[8 : 8 + count]
    refs = refs[8 + count :]
    if not first:
        base_ref, refs = refs[0], refs[1:]
    out_ref, refs = refs[0], refs[1:]
    acc_ref = refs[0] if last else out_ref
    left_ref, buf_ref, sem_ref = refs[-3:]
    targets = k0_ref.shape[0]
    rows = buf_ref.shape[2]
    copies, starts = {}, []
    for g, k in enumerate(groups):
        start = pl.multiple_of((lax.axis_index("patch") ^ k) * rows, block) if rows < k0_ref.shape[1] else 0
        starts.append(start)
        for d, k_ref in enumerate((k0_ref,)):
            copies[g, d] = pltpu.make_async_copy(
                k_ref.at[:, pl.ds(start, rows), :], buf_ref.at[g], sem_ref.at[g]
            )
            copies[g, d].start()
    for g, (k, piece_ref) in enumerate(zip(groups, piece_refs)):
        load_piece(k, piece_ref, (before_ref, after_ref), left_ref.at[g], scale, block, local=True)
    if not first:
        acc_ref[...] = base_ref[...]
    unit = 2 if targets % 2 == 0 else 1
    for d in (1, 0):
        for g in range(count):
            if d == 0:
                copies[g, d].wait()

            def body(n, carry, g=g, d=d):
                if d == 0:
                    parts = [buf_ref[g, n * unit + u] for u in range(unit)]
                else:
                    parts = [k1_ref[n * unit + u, pl.ds(starts[g], rows), :] for u in range(unit)]
                right = jnp.concatenate(parts, 1)
                lanes = pl.ds(pl.multiple_of(n * (unit * block), unit * block), unit * block)
                part = jnp.dot(left_ref[g, d], right, preferred_element_type=F32)
                acc_ref[d, :, lanes] = part if first and g == 0 else acc_ref[d, :, lanes] + part
                return carry

            lax.fori_loop(0, targets // unit, body, 0, unroll=2)
    if last:
        half = out_ref.shape[0] // 2

        def store(d, value):
            out_ref[d * half : (d + 1) * half] = value

        finish(acc_ref, inc_ref, by_parity(fore_ref[...], back_ref[...]), ends_ref, store)


def call_sweep(groups, block, scale, before, after, inc, fore, back, ends, k0, k1, pieces, base, last):
    channels, rows = inc.shape
    targets = k0.shape[0]
    depth = 2 * pieces[0].shape[1]
    k0 = pltpu.with_memory_space_constraint(k0, pltpu.HBM)
    k1 = pltpu.with_memory_space_constraint(k1, pltpu.VMEM)
    vmem = pl.BlockSpec(memory_space=pltpu.VMEM)
    table = pl.BlockSpec(memory_space=pl.ANY)
    extra = [] if base is None else [base]
    sums = jax.ShapeDtypeStruct((2, channels, rows), F32)
    return pl.pallas_call(
        functools.partial(sweep_kernel, groups, block, scale, base is None, last),
        out_shape=jax.ShapeDtypeStruct(inc.shape, BF) if last else sums,
        in_specs=[vmem] * 6 + [table, vmem] + [vmem] * (len(pieces) + len(extra)),
        out_specs=vmem,
        scratch_shapes=([pltpu.VMEM(sums.shape, F32)] if last else [])
        + [
            pltpu.VMEM((len(groups), 2, channels, depth), BF),
            pltpu.VMEM((len(groups), targets, depth, block), BF),
            pltpu.SemaphoreType.DMA((len(groups),)),
        ],
        cost_estimate=pl.CostEstimate(
            flops=4 * len(groups) * channels * rows * depth,
            bytes_accessed=4 * len(groups) * rows * depth,
            transcendentals=0,
        ),
        compiler_params=pltpu.CompilerParams(vmem_limit_bytes=24 * 2**20),
        name="sweep" if last else "own_sweep",
    )(before, after, inc, fore, back, ends, k0, k1, *pieces, *extra)


def join_kernel(swap_ref, cross_ref, out_ref, *geo_refs):
    half = out_ref.shape[0] // 2
    after, before = by_parity(swap_ref[...], cross_ref[...])
    out_ref[:half] = before[:half].astype(BF)
    out_ref[half:] = after[:half].astype(BF)
    for ref, value in zip(geo_refs, (before, after)):
        ref[...] = value[half:]


def join(swapped, crossed, channels):
    vmem = pl.BlockSpec(memory_space=pltpu.VMEM)
    rows, width = swapped.shape
    geo = rows - channels // 2
    extra = [jax.ShapeDtypeStruct((geo, width), F32)] * 2 if geo else []
    return pl.pallas_call(
        join_kernel,
        out_shape=[jax.ShapeDtypeStruct((channels, width), BF)] + extra,
        in_specs=[vmem] * 2,
        out_specs=[vmem] * (1 + len(extra)),
        compiler_params=pltpu.CompilerParams(vmem_limit_bytes=4 * 2**20),
        name="join",
    )(swapped, crossed)


def neighbours(first, second):
    count = lax.axis_size("seg")
    moves = []
    for start in range(2):
        pairs = [(i, i + 1) for i in range(start, count - 1, 2)]
        moves.append(pairs + [(j, i) for i, j in pairs])
    return lax.ppermute(first, "seg", moves[0]), lax.ppermute(second, "seg", moves[1])


def gather_patches(value):
    count = lax.axis_size("patch")
    if count not in (1, 2, 4):
        return [lax.all_gather(value, "patch", axis=1, tiled=True)]
    return [value] + [
        lax.ppermute(value, "patch", [(i, i ^ k) for i in range(count)]) for k in range(1, count)
    ]


def on_device(incident, wall_axial, wall_angle, wall_area, visibility, end_reflection):
    channels = incident.shape[1]
    patches = wall_axial.shape[1]
    block = patches // visibility.shape[3]
    half = channels // 2
    per_chunk = min(8, patches // block)
    scale = KAPPA / math.sqrt(patches)
    inc = incident[0]
    own, other, lists = call_prep(per_chunk, wall_axial, wall_angle, wall_area, inc, visibility)
    moved, before, after = join(*neighbours(own, other), channels)
    pieces = gather_patches(moved)
    k0 = call_build(0, block, per_chunk, half, lists, own, before, patches)
    k1, k0, first, second = call_build_sweep(
        block, per_chunk, scale, patches, lists, own, before, after, inc, end_reflection, k0, pieces
    )
    for sweep in range(1, ITERS):
        pieces = gather_patches(join(*neighbours(first, second), channels)[0])
        groups = tuple(range(len(pieces)))
        common = (block, scale, before, after, inc, first, second, end_reflection, k0, k1)
        base = None
        if len(groups) > 1:
            base = call_sweep(groups[:1], *common, pieces[:1], None, False)
            groups, pieces = groups[1:], pieces[1:]
        state = call_sweep(groups, *common, pieces, base, True)
        if sweep + 1 < ITERS:
            first, second = by_parity(state[:half], state[half:])
    return state[None]


def solution(mesh):
    return jax.shard_map(
        on_device,
        mesh=mesh,
        in_specs=(
            P("seg", None, "patch"),
            P("seg", None),
            P("seg", None),
            P("seg", None),
            P("seg", None, "patch", None),
            P(),
        ),
        out_specs=P("seg", None, "patch"),
        check_vma=False,
    )
```

```python
import functools
import math

import jax
import jax.numpy as jnp
from jax import lax
from jax.experimental import pallas as pl
from jax.experimental.pallas import tpu as pltpu
from jax.sharding import PartitionSpec as P

ITERS = 2

WAVENUMBER = 40.0
RADIUS = 0.5
SOFTENING = 0.25

KAPPA = WAVENUMBER / (2.0 * math.pi)
HALF_CHORD = 2.0 * RADIUS * RADIUS * KAPPA * KAPPA
SINE = tuple(
    value * (1.0 - 5e-7)
    for value in (4.442867903112522, -7.307443423342558, 3.5947880930735288, -0.7843740618048793)
)
SINE_HALF = (0.999999976589841, -0.16666647634617332, 0.00833289982302485, -0.00019800897745117133,
             2.5904884686762915e-06)
COSINE_HALF = (0.9999999997806504, -0.4999999935847076, 0.04166663625803946, -0.0013888361399933481,
               2.476016133696864e-05, -2.605149496508554e-07)

FEATURES = 32
ROOMY = 12 * 2**20
PAIR = 8
BF = jnp.bfloat16
F32 = jnp.float32


def leading(x):
    wide = x * 65537.0
    return wide - (wide - x)


def split3(x):
    high = leading(x)
    rest = x - high
    mid = leading(rest)
    return high, mid, rest - mid


def near_side(geo, direction):
    return (geo[0:1] if direction == 0 else 1.0 - geo[0:1]) * KAPPA


def far_side(geo, direction):
    return (1.0 - geo[0:1] if direction == 0 else geo[0:1]) * KAPPA


def pad_rows(rows):
    width = rows[0].shape[1]
    rows = rows + [jnp.zeros((FEATURES - len(rows), width), F32)]
    return jnp.concatenate(rows, 0)


def target_features(geo, direction):
    u = near_side(geo, direction)
    one = jnp.ones_like(u)
    rows = list(split3(u * u + HALF_CHORD)) + [one, one, one]
    for value in (2.0 * u, -HALF_CHORD * geo[1:2], -HALF_CHORD * geo[2:3]):
        h, m, l = split3(value)
        rows += [h, h, m, m, h, l]
    return pad_rows(rows)


def source_features(geo, direction):
    v = far_side(geo, direction)
    one = jnp.ones_like(v)
    rows = [one, one, one] + list(split3(v * v))
    for value in (v, geo[1:2], geo[2:3]):
        h, m, l = split3(value)
        rows += [h, m, h, m, l, h]
    return pad_rows(rows)


def horner(coefs, x):
    total = coefs[-1]
    for coef in coefs[-2::-1]:
        total = total * x + coef
    return total


def exact_dot(a, b):
    return jnp.dot(a.astype(BF), b.astype(BF), preferred_element_type=F32)


def make_lists(lit, per_chunk):
    targets, sources = lit.shape
    chunks = sources // per_chunk
    size = per_chunk * targets
    i0 = lax.broadcasted_iota(jnp.int32, (sources, sources), 0)
    i1 = lax.broadcasted_iota(jnp.int32, (sources, sources), 1)
    same = i0 // per_chunk == i1 // per_chunk
    above = lax.broadcasted_iota(jnp.int32, (targets, targets), 0) > lax.broadcasted_iota(
        jnp.int32, (targets, targets), 1
    )
    sums = exact_dot(lit, jnp.where(same, 1.0, 0.0))
    rank = exact_dot(lit, jnp.where(same & (i0 < i1), 1.0, 0.0)) + exact_dot(
        jnp.where(above, 1.0, 0.0), sums
    )
    src = lax.broadcasted_iota(jnp.int32, lit.shape, 1) % per_chunk
    tgt = lax.broadcasted_iota(jnp.int32, lit.shape, 0)
    order = (tgt * per_chunk + src).astype(F32)
    place = jnp.where(lit > 0.5, rank, size - 1 - (order - rank))
    code = (src * targets + tgt).astype(F32)
    slot = lax.broadcasted_iota(jnp.int32, (size, sources), 0).astype(F32)
    found = jnp.zeros((size, sources), F32)
    for t in range(targets):
        found += jnp.where(slot == place[t : t + 1], code[t : t + 1], 0.0)
    c0 = lax.broadcasted_iota(jnp.int32, (sources, chunks), 0)
    c1 = lax.broadcasted_iota(jnp.int32, (sources, chunks), 1)
    pick = jnp.where(c0 // per_chunk == c1, 1.0, 0.0)
    codes = exact_dot(found, pick)
    counts = jnp.sum(exact_dot(lit, pick), axis=0, keepdims=True)
    return codes.astype(jnp.int32), counts.astype(jnp.int32)


def by_parity(even, odd):
    is_odd = lax.rem(lax.axis_index("seg"), 2) == 1
    wide = [x.astype(F32) for x in (even, odd)]
    pair = jnp.where(is_odd, wide[1], wide[0]), jnp.where(is_odd, wide[0], wide[1])
    return tuple(x.astype(even.dtype) for x in pair)


def prep_kernel(per_chunk, axial_ref, angle_ref, area_ref, inc_ref, vis_ref, swap_ref, cross_ref, list_ref):
    rows = inc_ref.shape[1]
    channels = inc_ref.shape[0] // 2
    half = angle_ref[...] * 0.5
    square = half * half
    sine = horner(SINE_HALF, square) * half
    cosine = horner(COSINE_HALF, square)
    geo = [axial_ref[...], 1.0 - 2.0 * sine * sine, 2.0 * sine * cosine, area_ref[...]]
    for j in range(axial_ref.shape[1] // rows):
        part = jnp.concatenate([g[:, j * rows : (j + 1) * rows] for g in geo], 0)
        swap_ref[channels + 4 * j : channels + 4 * j + 4] = part
        cross_ref[channels + 4 * j : channels + 4 * j + 4] = part
    fore, back = inc_ref[:channels].astype(F32), inc_ref[channels:].astype(F32)
    swap_ref[:channels], cross_ref[:channels] = by_parity(fore, back)
    for d in range(2):
        codes, counts = make_lists(vis_ref[0, d].astype(F32), per_chunk)
        list_ref[d, : codes.shape[0]] = codes
        list_ref[d, codes.shape[0] :] = jnp.broadcast_to(counts, (8, counts.shape[1]))


def call_prep(per_chunk, axial, angle, area, inc, visibility):
    targets, sources = visibility.shape[2], visibility.shape[3]
    channels = inc.shape[0] // 2
    rows, patches = inc.shape[1], axial.shape[1]
    pack = jax.ShapeDtypeStruct((channels + 4 * (patches // rows), rows), F32)
    vmem = pl.BlockSpec(memory_space=pltpu.VMEM)
    axial, angle, area, inc, visibility = [
        pltpu.with_memory_space_constraint(x, pltpu.HBM) for x in (axial, angle, area, inc, visibility)
    ]
    return pl.pallas_call(
        functools.partial(prep_kernel, per_chunk),
        out_shape=(
            pack, pack,
            jax.ShapeDtypeStruct((2, per_chunk * targets + 8, sources // per_chunk), jnp.int32),
        ),
        in_specs=[vmem] * 5,
        out_specs=[vmem] * 3,
        compiler_params=pltpu.CompilerParams(vmem_limit_bytes=ROOMY),
        name="prep",
    )(axial, angle, area, inc, visibility)


def table_block(q):
    q = jnp.maximum(q, 1e-12)
    turns = q * lax.rsqrt(q)
    f = turns - jnp.round(turns)
    mag = lax.rsqrt(q + SOFTENING * KAPPA * KAPPA)
    s = horner(SINE, f * f) * f
    rest = 2.0 - s * s
    both = mag * rest
    real = both - mag
    imag = (s * both) * lax.rsqrt(rest)
    return real.astype(BF), imag.astype(BF)


def build_chunk(direction, chunk, block, targets, list_ref, tf_ref, sf_ref, base, k_ref, q_ref):
    size = list_ref.shape[1] - 8
    count = list_ref[direction, size, chunk]

    def block_of(n):
        code = list_ref[direction, jnp.maximum(jnp.minimum(n, count - 1), 0), chunk]
        return lax.div(code, jnp.int32(targets)), lax.rem(code, jnp.int32(targets))

    def distances(group, q_ref):
        for u in range(PAIR):
            src, tgt = block_of(group * PAIR + u)
            cols = pl.ds(pl.multiple_of(tgt * block, block), block)
            feats = sf_ref[pl.ds(pl.multiple_of(base + src * block, block), block), :]
            q_ref[u * block : (u + 1) * block] = jnp.dot(feats, tf_ref[:, cols], preferred_element_type=F32)

    def entries(group, q_ref):
        for u in range(PAIR):
            src, tgt = block_of(group * PAIR + u)
            top = pl.multiple_of(src * (2 * block), 2 * block)
            part = 32
            for h in range(0, block, part):
                real, imag = table_block(q_ref[u * block + h : u * block + h + part])
                k_ref[tgt, pl.ds(pl.multiple_of(top + h, part), part), :] = real
                k_ref[tgt, pl.ds(pl.multiple_of(top + block + h, part), part), :] = imag

    def body(step, carry):
        distances(step, q_ref)
        entries(step, q_ref)
        return carry

    lax.fori_loop(0, lax.div(count + PAIR - 1, jnp.int32(PAIR)), body, 0)

    def clear(step, carry):
        for u in range(4):
            code = list_ref[direction, jnp.minimum(count + step * 4 + u, size - 1), chunk]
            src, tgt = lax.div(code, jnp.int32(targets)), lax.rem(code, jnp.int32(targets))
            rows = pl.ds(pl.multiple_of(src * (2 * block), 2 * block), 2 * block)
            k_ref[tgt, rows, :] = jnp.zeros((2 * block, block), BF)
        return carry

    lax.fori_loop(0, lax.div(size - count + 3, jnp.int32(4)), clear, 0)


def quarters(pack_ref, channels):
    return [pack_ref[r : r + 4] for r in range(channels, pack_ref.shape[0], 4)]


def pick(parts, index):
    chosen = parts[0]
    for j in range(1, len(parts)):
        chosen = jnp.where(index == j, parts[j], chosen)
    return chosen


def build_features(direction, channels, own_ref, pack_ref, tf_ref, sf_ref):
    rows = own_ref.shape[1]
    own = pick(quarters(own_ref, channels), lax.axis_index("patch"))
    tf_ref[...] = target_features(own, direction).astype(BF)
    for j, geo in enumerate(quarters(pack_ref, 0)):
        sf_ref[j * rows : (j + 1) * rows] = source_features(geo, direction).T.astype(BF)


def build_kernel(direction, block, per_chunk, channels, list_ref, own_ref, pack_ref, k_ref, tf_ref, sf_ref, *q):
    chunk = pl.program_id(0)

    @pl.when(chunk == 0)
    def _():
        build_features(direction, channels, own_ref, pack_ref, tf_ref, sf_ref)

    build_chunk(
        direction, chunk, block, k_ref.shape[0], list_ref, tf_ref, sf_ref, chunk * (per_chunk * block),
        rows_of(k_ref, chunk, 2 * per_chunk * block), *q
    )


def rows_of(k_ref, chunk, rows):
    return k_ref.at[:, pl.ds(pl.multiple_of(chunk * rows, rows), rows), :]


def whole(x):
    return pl.BlockSpec(x.shape, lambda c: (0,) * x.ndim)


def table_spec(targets, chunk_rows, block):
    return pl.BlockSpec((targets, chunk_rows, block), lambda c: (0, c, 0))


def call_build(direction, block, per_chunk, channels, lists, own, pack, patches):
    rows = own.shape[1]
    targets = rows // block
    chunk_rows = 2 * block * per_chunk
    return pl.pallas_call(
        functools.partial(build_kernel, direction, block, per_chunk, channels),
        grid=(patches // (block * per_chunk),),
        out_shape=pltpu.VMEM((targets, 2 * patches, block), BF),
        in_specs=[pl.BlockSpec(memory_space=pltpu.SMEM), whole(own), whole(pack)],
        out_specs=pl.BlockSpec(memory_space=pltpu.VMEM),
        scratch_shapes=[
            pltpu.VMEM((FEATURES, rows), BF),
            pltpu.VMEM((patches, FEATURES), BF),
            pltpu.VMEM((PAIR * block, block), F32),
        ],
        compiler_params=pltpu.CompilerParams(dimension_semantics=("arbitrary",), vmem_limit_bytes=ROOMY),
        name=f"build{direction}",
    )(lists, own, pack)


def load_piece(k, piece_ref, packs, left_ref, scale, block, local=False):
    channels = piece_ref.shape[0] // 2
    half = channels // 2
    width = piece_ref.shape[1]
    gathered = width != packs[0].shape[1]
    group = lax.axis_index("patch") ^ k
    for d, pack_ref in enumerate(packs):
        areas = [pack_ref[r + 3 : r + 4] for r in range(0, pack_ref.shape[0], 4)]
        area = jnp.concatenate(areas, 1) if gathered else pick(areas, group)
        area = area * scale
        for n in range(width // block):
            cur = piece_ref[d * channels : (d + 1) * channels, n * block : (n + 1) * block].astype(F32)
            cur = cur * area[:, n * block : (n + 1) * block]
            high = leading(cur)
            low = (cur - high).astype(BF)
            high = high.astype(BF)
            a = jnp.concatenate([high, low], 0)
            b = jnp.concatenate([high[half:], -high[:half], low[half:], -low[:half]], 0)
            start = n * block if gathered or local else group * width + n * block
            top = pl.multiple_of(2 * start, 2 * block)
            left_ref[d, :, pl.ds(top, block)] = a
            left_ref[d, :, pl.ds(pl.multiple_of(top + block, block), block)] = b


def finish(acc_ref, inc_ref, prev, ends_ref, store):
    channels = inc_ref.shape[0] // 2
    half = channels // 2
    seg = lax.axis_index("seg")
    diagonal = lax.broadcasted_iota(jnp.int32, (channels, channels), 0) == lax.broadcasted_iota(
        jnp.int32, (channels, channels), 1
    )
    for d, end in enumerate((0, lax.axis_size("seg") - 1)):
        total = acc_ref[d, :channels] + acc_ref[d, channels:]
        other = prev[1 - d].astype(F32)
        flag = jnp.where(seg == end, 1.0, 0.0)
        coef = jnp.sum(jnp.where(diagonal, ends_ref[d : d + 1] * flag, 0.0), axis=1, keepdims=True)
        cre = coef[:half]
        cim = coef[half:]
        mirrored = jnp.concatenate(
            [cre * other[:half] - cim * other[half:], cre * other[half:] + cim * other[:half]], 0
        )
        rows = slice(d * channels, (d + 1) * channels)
        store(d, (inc_ref[rows].astype(F32) + total + mirrored).astype(BF))


def accumulate(acc_ref, left_ref, chunk, k_refs):
    targets, rows, block = k_refs[1].shape
    cols = pl.ds(pl.multiple_of(chunk * rows, rows), rows)
    group = 2 if targets % 2 == 0 else 1

    def body(n, carry):
        lanes = pl.ds(pl.multiple_of(n * (group * block), group * block), group * block)
        for d, k_ref in k_refs.items():
            right = jnp.concatenate([k_ref[n * group + g] for g in range(group)], 1)
            part = jnp.dot(left_ref[d, :, cols], right, preferred_element_type=F32)
            acc_ref[d, :, lanes] = jnp.where(chunk == 0, part, acc_ref[d, :, lanes] + part)
        return carry

    lax.fori_loop(0, targets // group, body, 0, unroll=True)


def build_sweep_kernel(
    block, per_chunk, pieces, scale, list_ref, own_ref, before_ref, after_ref, inc_ref, ends_ref, k0_ref, *rest
):
    piece_refs = rest[:pieces]
    k1_ref, kept_ref, fore_ref, back_ref, tf_ref, sf_ref, left_ref, acc_ref, q_ref, sem_ref = rest[pieces:]
    chunk = pl.program_id(0)
    chunks = pl.num_programs(0)
    channels = inc_ref.shape[0] // 2
    rows = 2 * per_chunk * block
    k_ref = rows_of(k1_ref, chunk, rows)
    keep = pltpu.make_async_copy(k0_ref, kept_ref, sem_ref)

    @pl.when(chunk == 0)
    def _():
        keep.start()

    @pl.when(chunk == 0)
    def _():
        build_features(1, channels, own_ref, after_ref, tf_ref, sf_ref)
        for k, piece_ref in enumerate(piece_refs):
            load_piece(k, piece_ref, (before_ref, after_ref), left_ref, scale, block)

    build_chunk(
        1, chunk, block, k1_ref.shape[0], list_ref, tf_ref, sf_ref, chunk * (per_chunk * block),
        k_ref, q_ref,
    )
    accumulate(acc_ref, left_ref, chunk, {0: rows_of(k0_ref, chunk, rows), 1: k_ref})

    @pl.when(chunk == chunks - 1)
    def _():
        state = {}
        finish(acc_ref, inc_ref, (inc_ref[:channels], inc_ref[channels:]), ends_ref, state.__setitem__)
        fore_ref[...], back_ref[...] = by_parity(state[0], state[1])
        keep.wait()


def call_build_sweep(block, per_chunk, scale, patches, lists, own, before, after, inc, ends, k0, pieces):
    rows = inc.shape[1]
    chunk_rows = 2 * block * per_chunk
    targets = rows // block
    channels = inc.shape[0]
    part = jax.ShapeDtypeStruct((channels // 2, rows), BF)
    k0 = pltpu.with_memory_space_constraint(k0, pltpu.VMEM)
    table = pl.BlockSpec(memory_space=pltpu.VMEM)
    return pl.pallas_call(
        functools.partial(build_sweep_kernel, block, per_chunk, len(pieces), scale),
        grid=(patches // (block * per_chunk),),
        out_shape=(pltpu.VMEM(k0.shape, BF), jax.ShapeDtypeStruct(k0.shape, BF), part, part),
        in_specs=[pl.BlockSpec(memory_space=pltpu.SMEM), whole(own), whole(before), whole(after), whole(inc),
                  whole(ends), table] + [whole(p) for p in pieces],
        out_specs=(table, pl.BlockSpec(memory_space=pl.ANY), whole(part), whole(part)),
        scratch_shapes=[
            pltpu.VMEM((FEATURES, rows), BF),
            pltpu.VMEM((patches, FEATURES), BF),
            pltpu.VMEM((2, channels, 2 * patches), BF),
            pltpu.VMEM((2, channels, rows), F32),
            pltpu.VMEM((PAIR * block, block), F32),
            pltpu.SemaphoreType.DMA,
        ],
        compiler_params=pltpu.CompilerParams(dimension_semantics=("arbitrary",), vmem_limit_bytes=12 * 2**20),
        name="build_sweep",
    )(lists, own, before, after, inc, ends, k0, *pieces)


def sweep_kernel(groups, block, scale, first, last, *refs):
    before_ref, after_ref, inc_ref, fore_ref, back_ref, ends_ref, k0_ref, k1_ref = refs[:8]
    count = len(groups)
    piece_refs = refs[8 : 8 + count]
    refs = refs[8 + count :]
    if not first:
        base_ref, refs = refs[0], refs[1:]
    out_ref, refs = refs[0], refs[1:]
    acc_ref = refs[0] if last else out_ref
    left_ref, buf_ref, sem_ref = refs[-3:]
    targets = k0_ref.shape[0]
    rows = buf_ref.shape[2]
    copies, starts = {}, []
    for g, k in enumerate(groups):
        start = pl.multiple_of((lax.axis_index("patch") ^ k) * rows, block) if rows < k0_ref.shape[1] else 0
        starts.append(start)
        for d, k_ref in enumerate((k0_ref,)):
            copies[g, d] = pltpu.make_async_copy(
                k_ref.at[:, pl.ds(start, rows), :], buf_ref.at[g], sem_ref.at[g]
            )
            copies[g, d].start()
    for g, (k, piece_ref) in enumerate(zip(groups, piece_refs)):
        load_piece(k, piece_ref, (before_ref, after_ref), left_ref.at[g], scale, block, local=True)
    if not first:
        acc_ref[...] = base_ref[...]
    unit = 2 if targets % 2 == 0 else 1
    for d in (1, 0):
        for g in range(count):
            if d == 0:
                copies[g, d].wait()

            def body(n, carry, g=g, d=d):
                if d == 0:
                    parts = [buf_ref[g, n * unit + u] for u in range(unit)]
                else:
                    parts = [k1_ref[n * unit + u, pl.ds(starts[g], rows), :] for u in range(unit)]
                right = jnp.concatenate(parts, 1)
                lanes = pl.ds(pl.multiple_of(n * (unit * block), unit * block), unit * block)
                part = jnp.dot(left_ref[g, d], right, preferred_element_type=F32)
                acc_ref[d, :, lanes] = part if first and g == 0 else acc_ref[d, :, lanes] + part
                return carry

            lax.fori_loop(0, targets // unit, body, 0, unroll=2)
    if last:
        half = out_ref.shape[0] // 2

        def store(d, value):
            out_ref[d * half : (d + 1) * half] = value

        finish(acc_ref, inc_ref, by_parity(fore_ref[...], back_ref[...]), ends_ref, store)


def call_sweep(groups, block, scale, before, after, inc, fore, back, ends, k0, k1, pieces, base, last):
    channels, rows = inc.shape
    targets = k0.shape[0]
    depth = 2 * pieces[0].shape[1]
    k0 = pltpu.with_memory_space_constraint(k0, pltpu.HBM)
    k1 = pltpu.with_memory_space_constraint(k1, pltpu.VMEM)
    vmem = pl.BlockSpec(memory_space=pltpu.VMEM)
    table = pl.BlockSpec(memory_space=pl.ANY)
    extra = [] if base is None else [base]
    sums = jax.ShapeDtypeStruct((2, channels, rows), F32)
    return pl.pallas_call(
        functools.partial(sweep_kernel, groups, block, scale, base is None, last),
        out_shape=jax.ShapeDtypeStruct(inc.shape, BF) if last else sums,
        in_specs=[vmem] * 6 + [table, vmem] + [vmem] * (len(pieces) + len(extra)),
        out_specs=vmem,
        scratch_shapes=([pltpu.VMEM(sums.shape, F32)] if last else [])
        + [
            pltpu.VMEM((len(groups), 2, channels, depth), BF),
            pltpu.VMEM((len(groups), targets, depth, block), BF),
            pltpu.SemaphoreType.DMA((len(groups),)),
        ],
        cost_estimate=pl.CostEstimate(
            flops=4 * len(groups) * channels * rows * depth,
            bytes_accessed=4 * len(groups) * rows * depth,
            transcendentals=0,
        ),
        compiler_params=pltpu.CompilerParams(vmem_limit_bytes=24 * 2**20),
        name="sweep" if last else "own_sweep",
    )(before, after, inc, fore, back, ends, k0, k1, *pieces, *extra)


def join_kernel(swap_ref, cross_ref, out_ref, *geo_refs):
    half = out_ref.shape[0] // 2
    after, before = by_parity(swap_ref[...], cross_ref[...])
    out_ref[:half] = before[:half].astype(BF)
    out_ref[half:] = after[:half].astype(BF)
    for ref, value in zip(geo_refs, (before, after)):
        ref[...] = value[half:]


def join(swapped, crossed, channels):
    vmem = pl.BlockSpec(memory_space=pltpu.VMEM)
    rows, width = swapped.shape
    geo = rows - channels // 2
    extra = [jax.ShapeDtypeStruct((geo, width), F32)] * 2 if geo else []
    return pl.pallas_call(
        join_kernel,
        out_shape=[jax.ShapeDtypeStruct((channels, width), BF)] + extra,
        in_specs=[vmem] * 2,
        out_specs=[vmem] * (1 + len(extra)),
        compiler_params=pltpu.CompilerParams(vmem_limit_bytes=4 * 2**20),
        name="join",
    )(swapped, crossed)


def neighbours(first, second):
    count = lax.axis_size("seg")
    moves = []
    for start in range(2):
        pairs = [(i, i + 1) for i in range(start, count - 1, 2)]
        moves.append(pairs + [(j, i) for i, j in pairs])
    return lax.ppermute(first, "seg", moves[0]), lax.ppermute(second, "seg", moves[1])


def gather_patches(value):
    count = lax.axis_size("patch")
    if count not in (1, 2, 4):
        return [lax.all_gather(value, "patch", axis=1, tiled=True)]
    return [value] + [
        lax.ppermute(value, "patch", [(i, i ^ k) for i in range(count)]) for k in range(1, count)
    ]


def on_device(incident, wall_axial, wall_angle, wall_area, visibility, end_reflection):
    channels = incident.shape[1]
    patches = wall_axial.shape[1]
    block = patches // visibility.shape[3]
    half = channels // 2
    per_chunk = min(8, patches // block)
    scale = KAPPA / math.sqrt(patches)
    inc = incident[0]
    own, other, lists = call_prep(per_chunk, wall_axial, wall_angle, wall_area, inc, visibility)
    moved, before, after = join(*neighbours(own, other), channels)
    pieces = gather_patches(moved)
    k0 = call_build(0, block, per_chunk, half, lists, own, before, patches)
    k1, k0, first, second = call_build_sweep(
        block, per_chunk, scale, patches, lists, own, before, after, inc, end_reflection, k0, pieces
    )
    for sweep in range(1, ITERS):
        pieces = gather_patches(join(*neighbours(first, second), channels)[0])
        groups = tuple(range(len(pieces)))
        common = (block, scale, before, after, inc, first, second, end_reflection, k0, k1)
        base = None
        if len(groups) > 1:
            base = call_sweep(groups[:1], *common, pieces[:1], None, False)
            groups, pieces = groups[1:], pieces[1:]
        state = call_sweep(groups, *common, pieces, base, True)
        if sweep + 1 < ITERS:
            first, second = by_parity(state[:half], state[half:])
    return state[None]


def solution(mesh):
    return jax.shard_map(
        on_device,
        mesh=mesh,
        in_specs=(
            P("seg", None, "patch"),
            P("seg", None),
            P("seg", None),
            P("seg", None),
            P("seg", None, "patch", None),
            P(),
        ),
        out_specs=P("seg", None, "patch"),
        check_vma=False,
    )
```
